32 devices in a mesh: groups: 2 (over y), rows: 4 (over z), disp: 2 (over x), cols: 2 (over core).
Axes of the slice: x: 2, y: 2, z: 4, core: 2. Of those that a mesh axis runs over, the one named last changes fastest.
Arguments:
- cost_volume_section: bfloat16 [32, 32, 8192], P(('groups', 'rows'), 'cols', 'disp'), parts along dimension 0, may hold values from -6 to 6
- picture_convolution_taps_grid: bfloat16 [3, 3, 3, 64, 64], replicated, may hold values from -0.25 to 0.25
- picture_convolution_offset_terms: float32 [3, 64], replicated, may hold values from -3 to 3
- shiftaxis_convolution_taps: bfloat16 [2, 17, 64, 64], replicated, may hold values from -0.1875 to 0.1875
- shiftaxis_convolution_biases: float32 [2, 64], replicated, may hold values from -3 to 3
- prior_norm_scale: float32 [64], replicated, may hold values from 0.1 to 1.9
- qkv_side_projections: bfloat16 [64, 192], replicated, may hold values from -0.75 to 0.75
- attn_exit_projection: bfloat16 [64, 64], replicated, may hold values from -0.75 to 0.75
- each_mixer_scale: float32 [4], replicated, may hold values from 0.25 to 25, as said below
- gating_projection: bfloat16 [64, 64], replicated, may hold values from -0.75 to 0.75
- gating_offset_terms: float32 [64], replicated, may hold values from -3 to 3
Outputs:
- filtered: bfloat16 [32, 32, 8192], P(('groups', 'rows'), 'cols', 'disp'), parts along dimension 0
The draws below stay inside these ranges and needn't reach their ends.
There are 2 independent parts, one for each index of `groups`. The reference program is written for one: setup_inputs(seed, part) draws one part's arguments, and reference() takes and returns one part's arrays. A program takes and returns all parts, laid end to end along the dimension named above; an argument that names none is the same for every part. Nothing has to cross between parts.
Inputs may be any that keep to these rules, and one draw needn't show every extreme that they name: `each_mixer_scale`: positive score scales, one for each head.
All inputs are finite; a program needn't handle non-finite values.
Results may differ from the reference program's by a relative error of at most 0.0095.
Values may be sent and summed in bfloat16 or wider, within the bound.
No kernel may reach another device: no remote copies, remote signals or barrier semaphores. Data moves between devices by JAX's collectives and lax.ppermute only.
A program may use at most 64 MiB of HBM per device.

```python
import math
import jax
import jax.numpy as jnp
from jax import lax

FEATURE_DEPTH = 64
DSP = 128
HEADS = 4
TAPS = 17
FLAT_LAYER_COUNT = 3
H = 16
W = 32


def draw_each_mixer_scale(key, part):
    upper = math.log(8.0)
    uniform_part = jax.random.uniform(key, (HEADS,), jnp.float32)
    return jnp.exp(uniform_part * upper).astype(jnp.float32)


def block_scale(stream_key, dims, pieces, low, top_value):
    def one(axis_at, shards_of):
        steps = jax.random.uniform(jax.random.fold_in(jax.random.fold_in(stream_key, 6), axis_at), (shards_of,), jnp.float32, low / len(pieces), top_value / len(pieces))
        return jnp.repeat(jnp.exp(steps), dims[axis_at] // shards_of).reshape((-1,) + (1,) * (len(dims) - axis_at - 1))

    loudness = one(*pieces[0])
    for cut in pieces[1:]:
        loudness = loudness * one(*cut)
    return loudness


def noise(rng, shape, deviation, most, pieces=(), held_as=jnp.bfloat16):
    result = jax.random.normal(rng, shape, jnp.float32) * deviation
    if len(pieces) > 0:
        result = block_scale(rng, shape, pieces, -0.22, 0.18) * result
    return jnp.clip(result, min=-most, max=most).astype(held_as)


def setup_inputs(seed: int = 0, part: int = 0) -> dict:
    keys = jax.random.split(jax.random.key(seed), 12)
    part_keys = jax.random.split(jax.random.fold_in(keys[11], part), 12)
    return {
        "cost_volume_section": noise(part_keys[0], (H, W, DSP * FEATURE_DEPTH), 1.0, 6.0, ((0, 4), (1, 2), (2, 2))),
        "picture_convolution_taps_grid": noise(keys[1], (FLAT_LAYER_COUNT, 3, 3, FEATURE_DEPTH, FEATURE_DEPTH), (9 * FEATURE_DEPTH) ** -0.5, 0.25),
        "picture_convolution_offset_terms": noise(keys[2], (FLAT_LAYER_COUNT, FEATURE_DEPTH), 0.5, 3.0, (), jnp.float32),
        "shiftaxis_convolution_taps": noise(keys[3], (2, TAPS, FEATURE_DEPTH, FEATURE_DEPTH), (TAPS * FEATURE_DEPTH) ** -0.5, 0.1875),
        "shiftaxis_convolution_biases": noise(keys[4], (2, FEATURE_DEPTH), 0.5, 3.0, (), jnp.float32),
        "prior_norm_scale": jnp.clip(1.0 + 0.18 * jax.random.normal(keys[5], (FEATURE_DEPTH,), jnp.float32), 0.1, 1.9),
        "qkv_side_projections": noise(keys[6], (FEATURE_DEPTH, 3 * FEATURE_DEPTH), FEATURE_DEPTH ** -0.5, 0.75),
        "attn_exit_projection": noise(keys[7], (FEATURE_DEPTH, FEATURE_DEPTH), FEATURE_DEPTH ** -0.5, 0.75),
        "each_mixer_scale": draw_each_mixer_scale(jax.random.fold_in(keys[11], 71), part),
        "gating_projection": noise(keys[9], (FEATURE_DEPTH, FEATURE_DEPTH), FEATURE_DEPTH ** -0.5, 0.75),
        "gating_offset_terms": noise(keys[10], (FEATURE_DEPTH,), 0.5, 3.0, (), jnp.float32),
    }


def image_plane_step(slices_list, kernel, bias_terms):
    border_extended = jnp.pad(slices_list, ((1, 1), (1, 1), (0, 0), (0, 0)))
    row_count = slices_list.shape[0]
    column_count = slices_list.shape[1]
    summed = jnp.zeros(slices_list.shape, jnp.float32)
    for row_tap in range(3):
        for col_tap in range(3):
            window = border_extended[row_tap:row_tap + row_count, col_tap:col_tap + column_count].astype(jnp.float32)
            summed = summed + jnp.einsum('rwdc,co->rwdo', window, kernel[row_tap, col_tap].astype(jnp.float32))
    return jax.nn.silu(summed + bias_terms).astype(jnp.bfloat16)

def parallax_step(image_lines, kernel, bias_terms):
    tap_count = kernel.shape[0]
    half_span = tap_count // 2
    candidate_levels = image_lines.shape[1]
    border_extended = jnp.pad(image_lines, ((0, 0), (half_span, half_span), (0, 0))).astype(jnp.float32)
    summed = jnp.zeros(image_lines.shape, jnp.float32)
    for tap_index in range(tap_count):
        window = border_extended[:, tap_index:tap_index + candidate_levels]
        summed = summed + jnp.einsum('pdc,co->pdo', window, kernel[tap_index].astype(jnp.float32))
    return summed + bias_terms

def project(latter_result, prior_norm_scale, qkv_side_projections):
    wide_copy = latter_result.astype(jnp.float32)
    normed = (wide_copy * lax.rsqrt(lax.optimization_barrier(jnp.mean(wide_copy * wide_copy, axis=-1, keepdims=True)) + 1e-05) * prior_norm_scale).astype(jnp.bfloat16)
    joined = jnp.einsum('pdc,ce->pde', normed.astype(jnp.float32), qkv_side_projections.astype(jnp.float32)).astype(jnp.bfloat16)
    feat_width = latter_result.shape[-1]
    return (joined[..., :feat_width], joined[..., feat_width:2 * feat_width], joined[..., 2 * feat_width:])

def displacement_self_mixing(probe_items, address_items, payload_items, each_mixer_scale):
    pixel_count, candidate_levels, feat_width = probe_items.shape
    arm_index = each_mixer_scale.shape[0]
    lanes_each = feat_width // arm_index
    query_heads = probe_items.astype(jnp.float32).reshape(pixel_count, candidate_levels, arm_index, lanes_each)
    key_heads = address_items.astype(jnp.float32).reshape(pixel_count, -1, arm_index, lanes_each)
    value_heads = payload_items.astype(jnp.float32).reshape(pixel_count, -1, arm_index, lanes_each)
    softmax_scale_amount = each_mixer_scale / math.sqrt(lanes_each)
    scores = jnp.einsum('pqhc,pkhc->phqk', query_heads, key_heads) * softmax_scale_amount[None, :, None, None]
    soft_weights = jax.nn.softmax(scores, axis=-1).astype(jnp.bfloat16)
    reunited_arms = jnp.einsum('phqk,pkhc->pqhc', soft_weights.astype(jnp.float32), value_heads)
    return reunited_arms.reshape(pixel_count, candidate_levels, feat_width).astype(jnp.bfloat16)

def finish(latter_result, reunited_arms, attn_exit_projection):
    moved = jnp.einsum('pdc,ce->pde', reunited_arms.astype(jnp.float32), attn_exit_projection.astype(jnp.float32))
    return (latter_result.astype(jnp.float32) + moved).astype(jnp.bfloat16)

def reference(cost_volume_section, picture_convolution_taps_grid, picture_convolution_offset_terms, shiftaxis_convolution_taps, shiftaxis_convolution_biases, prior_norm_scale, qkv_side_projections, attn_exit_projection, each_mixer_scale, gating_projection, gating_offset_terms):
    height = cost_volume_section.shape[0]
    column_count = cost_volume_section.shape[1]
    slices_list = cost_volume_section.reshape(height, column_count, DSP, FEATURE_DEPTH)
    for level_ordinal in range(FLAT_LAYER_COUNT):
        slices_list = image_plane_step(slices_list, picture_convolution_taps_grid[level_ordinal], picture_convolution_offset_terms[level_ordinal])

    def one_row(row_pair):
        horizontal_line, volume_row = row_pair
        initial_result = jax.nn.silu(parallax_step(horizontal_line, shiftaxis_convolution_taps[0], shiftaxis_convolution_biases[0])).astype(jnp.bfloat16)
        latter_result = parallax_step(initial_result, shiftaxis_convolution_taps[1], shiftaxis_convolution_biases[1]).astype(jnp.bfloat16)
        probe_items, address_items, payload_items = project(latter_result, prior_norm_scale, qkv_side_projections)
        reunited_arms = displacement_self_mixing(probe_items, address_items, payload_items, each_mixer_scale)
        attended = finish(latter_result, reunited_arms, attn_exit_projection)
        gate_value = jax.nn.sigmoid(jnp.einsum('pdc,ce->pde', attended.astype(jnp.float32), gating_projection.astype(jnp.float32)) + gating_offset_terms)
        gated = volume_row.reshape(column_count, DSP, FEATURE_DEPTH).astype(jnp.float32) * gate_value
        return gated.astype(jnp.bfloat16).reshape(column_count, DSP * FEATURE_DEPTH)
    return lax.map(one_row, (slices_list, cost_volume_section))
```

```python
import functools
import math

import jax
import jax.numpy as jnp
from jax import lax
from jax.experimental import pallas as pl
from jax.experimental.pallas import tpu as pltpu
from jax.sharding import PartitionSpec as P

F32 = jnp.float32
BF16 = jnp.bfloat16
PACK = 4
WIDE = 256


def vmem():
    return pl.BlockSpec(memory_space=pltpu.VMEM)


def smem():
    return pl.BlockSpec(memory_space=pltpu.SMEM)


def silu(v):
    half = 0.5 * v
    return half + half * jnp.tanh(half)


def sigmoid(v):
    return 0.5 + 0.5 * jnp.tanh(0.5 * v)


def dot(a, b):
    return jnp.dot(a, b, preferred_element_type=F32)


def dot_nt(a, b):
    return lax.dot_general(a, b, (((1,), (1,)), ((), ())), preferred_element_type=F32)


def widen_kernel(plane_lo, plane_hi, pairs, plane_out, band_out):
    ch = plane_lo.shape[1]
    count = plane_lo.shape[0]
    plane_out[...] = jnp.zeros_like(plane_out)

    def one(i, carry):
        for u in range(PACK):
            src = plane_hi if u % 2 else plane_lo
            col = (u // 2) * 2 * ch
            plane_out[i, u * ch : (u + 1) * ch, col : col + 2 * ch] = src[i]
        return carry

    lax.fori_loop(0, count, one, 0)
    taps = pairs.shape[1] - 1
    half = taps // 2
    spans = band_out.shape[1]
    for s in range(2):
        for j in range(spans):
            for u in range(PACK):
                for b in range(PACK // 2):
                    t = PACK * (j - spans // 2) + u - 2 * b + half
                    rows = slice(u * ch, (u + 1) * ch)
                    cols = slice(2 * b * ch, 2 * (b + 1) * ch)
                    if 0 <= t <= taps:
                        band_out[s, j, rows, cols] = pairs[s, t]
                    else:
                        band_out[s, j, rows, cols] = jnp.zeros((ch, 2 * ch), BF16)


def widen(planar_taps, shift_taps):
    layers, ch = planar_taps.shape[0], planar_taps.shape[-1]
    taps = shift_taps.shape[1]
    flat = planar_taps.reshape(layers * 9, ch, ch)
    zero = jnp.zeros_like(flat)
    lo = jnp.concatenate([flat, zero], axis=-1)
    hi = jnp.concatenate([zero, flat], axis=-1)
    gap = jnp.zeros((2, 1, ch, ch), shift_taps.dtype)
    pairs = jnp.concatenate(
        [
            jnp.concatenate([shift_taps, gap], axis=1),
            jnp.concatenate([gap, shift_taps], axis=1),
        ],
        axis=-1,
    )
    spans = 2 * (-(-(taps // 2) // PACK)) + 1
    size = PACK * ch
    return pl.pallas_call(
        widen_kernel,
        out_shape=(
            jax.ShapeDtypeStruct((layers * 9, size, size), BF16),
            jax.ShapeDtypeStruct((2, spans, size, size), BF16),
        ),
        in_specs=[vmem()] * 3,
        out_specs=(vmem(), vmem()),
        compiler_params=pltpu.CompilerParams(vmem_limit_bytes=20 << 20),
        cost_estimate=pl.CostEstimate(
            flops=0, bytes_accessed=12 << 20, transcendentals=0
        ),
        name="widen",
    )(lo, hi, pairs)


def planar_kernel(nd, nc, spot, mine, halo_a, halo_b, taps, bias, *rest):
    outs = rest[: nd * nc]
    bufs = rest[nd * nc :]
    rows, cols, lanes = mine.shape
    layers = bias.shape[0]
    halo = halo_a.shape[0]
    wide = taps.shape[1]
    groups = lanes // wide
    first_edge, last_edge, even, has_up, has_down, xi = [spot[i] for i in range(6)]
    col = lax.broadcasted_iota(jnp.int32, (cols, wide), 0)
    drop_left = col == first_edge
    drop_right = col == last_edge
    total = rows + 2 * halo

    def put(buf, g, r, value):
        buf[1, r] = value.astype(BF16)
        left = pltpu.roll(value, 1, 0)
        right = pltpu.roll(value, cols - 1, 0)
        buf[0, r] = jnp.where(drop_left, 0.0, left).astype(BF16)
        buf[2, r] = jnp.where(drop_right, 0.0, right).astype(BF16)

    at_a = jnp.where(even == 1, halo + rows, 0)
    at_b = jnp.where(even == 1, 0, halo + rows)

    def group(g, carry):
        lane = pl.ds(pl.multiple_of(g * wide, wide), wide)
        for r in range(rows):
            put(bufs[0], g, halo + r, mine[r, :, lane].astype(F32))
        for r in range(halo):
            put(bufs[0], g, at_a + r, halo_a[r, :, lane].astype(F32))
            put(bufs[0], g, at_b + r, halo_b[r, :, lane].astype(F32))
        for layer in range(layers):
            height = total - 2 * (layer + 1)
            src = bufs[layer]
            acc = None
            for i in range(3):
                for j in range(3):
                    lhs = src[j, i : i + height].reshape(height * cols, wide)
                    part = dot(lhs, taps[layer * 9 + i * 3 + j])
                    acc = part if acc is None else acc + part
            y = silu(acc + bias[layer])
            if layer < layers - 1:
                beyond = layers - 1 - layer
                for r in range(height):
                    slab = y[r * cols : (r + 1) * cols]
                    if r < beyond:
                        slab = jnp.where(has_up == 1, slab, 0.0)
                    if r >= height - beyond:
                        slab = jnp.where(has_down == 1, slab, 0.0)
                    put(bufs[layer + 1], g, r, slab)
            else:
                bufs[layers][...] = y.reshape(height, cols, wide)
        part_rows = rows // nd
        own = cols // nc
        for a in range(nd):
            top = lax.rem(xi + a, nd) * part_rows
            for r in range(part_rows):
                slab = bufs[layers][top + r]
                for k in range(nc):
                    outs[a * nc + k][r * own : (r + 1) * own, lane] = slab[
                        k * own : (k + 1) * own
                    ].astype(BF16)
        return carry

    lax.fori_loop(0, groups, group, 0)


def planar(nd, nc, spot, mine, halo_a, halo_b, taps, bias):
    rows, cols, lanes = mine.shape
    layers = bias.shape[0]
    halo = halo_a.shape[0]
    wide = taps.shape[1]
    total = rows + 2 * halo
    pixels = rows * cols // (nd * nc)
    scratch = [
        pltpu.VMEM((3, total - 2 * k, cols, wide), BF16) for k in range(layers)
    ] + [pltpu.VMEM((rows, cols, wide), F32)]
    return pl.pallas_call(
        functools.partial(planar_kernel, nd, nc),
        out_shape=[jax.ShapeDtypeStruct((pixels, lanes), BF16)] * (nd * nc),
        in_specs=[smem()] + [vmem()] * 5,
        out_specs=[vmem()] * (nd * nc),
        scratch_shapes=scratch,
        compiler_params=pltpu.CompilerParams(vmem_limit_bytes=24 << 20),
        name="planar",
    )(spot, mine, halo_a, halo_b, taps, bias)


def disparity_kernel(
    nd,
    nc,
    heads,
    spot,
    *refs,
):
    pieces = refs[: nd * nc]
    (
        band,
        bias,
        gain,
        w_qe,
        w_qo,
        w_k,
        w_v,
        q_scale,
        w_out,
        w_gate,
        gate_off,
        mean_mat,
    ) = refs[nd * nc : nd * nc + 12]
    outs = refs[nd * nc + 12 : nd * nc + 12 + nd]
    xs, ys, sf, nrm, qe, qo, kk, vv, mix, sec = refs[nd * nc + 12 + nd :]
    pixels, lanes = pieces[0].shape
    wide = band.shape[2]
    per_piece = lanes // wide
    groups = per_piece * nd * nc
    spans = band.shape[1]
    pad = spans // 2
    ch = wide // PACK
    per_head = ch // heads
    pairs = pixels // 2
    xi, ci = spot[0], spot[1]

    for side in range(pad):
        xs[side] = jnp.zeros((pixels, wide), BF16)
        xs[pad + groups + side] = jnp.zeros((pixels, wide), BF16)
        ys[side] = jnp.zeros((pixels, wide), BF16)
        ys[pad + groups + side] = jnp.zeros((pixels, wide), BF16)
    for a in range(nd):
        for k in range(nc):
            src_x = lax.rem(xi - a + nd, nd)
            src_c = lax.rem(ci - k + nc, nc)
            at = pad + (src_x * nc + src_c) * per_piece
            piece = pieces[a * nc + k]
            for g in range(per_piece):
                xs[at + g] = piece[:, g * wide : (g + 1) * wide]

    step = math.gcd(groups, 16)

    def conv(src, s, g0):
        acc = None
        for j in range(spans):
            lhs = src[pl.ds(g0 + j, step)].reshape(step * pixels, wide)
            part = dot(lhs, band[s, j])
            acc = part if acc is None else acc + part
        return acc + bias[s]

    def first(i, carry):
        g0 = i * step
        y = silu(conv(xs, 0, g0)).astype(BF16)
        ys[pl.ds(pad + g0, step)] = y.reshape(step, pixels, wide)
        return carry

    lax.fori_loop(0, groups // step, first, 0)

    def second(i, carry):
        g0 = i * step
        y = conv(ys, 1, g0).astype(BF16).astype(F32)
        for b in range(wide // 128):
            sf[b, pl.ds(pl.multiple_of(g0 * pixels, 8), step * pixels), :] = y[
                :, b * 128 : (b + 1) * 128
            ]
        return carry

    lax.fori_loop(0, groups // step, second, 0)

    def gather(p, carry):
        at = pl.ds(pl.multiple_of(p * groups, groups), groups)
        for q in range(2):
            for b in range(wide // 128):
                piece = sf[b, pl.ds(2 * p + q, groups, stride=pixels), :]
                sec[q, at, b * 128 : (b + 1) * 128] = piece
        return carry

    lax.fori_loop(0, pairs, gather, 0)

    for q in range(2):
        s = sec[q]
        sq = s * s
        hi = sq.astype(BF16)
        lo = (sq - hi.astype(F32)).astype(BF16)
        mean = dot(hi, mean_mat[...]) + dot(lo, mean_mat[...])
        nrm[q] = (s * lax.rsqrt(mean + 1e-05) * gain[...]).astype(BF16)
    qe[...] = (dot(nrm[0], w_qe[...]) * q_scale[...]).astype(BF16)
    qo[...] = (dot(nrm[1], w_qo[...]) * q_scale[...]).astype(BF16)
    kk[...] = (dot(nrm[0], w_k[0]) + dot(nrm[1], w_k[1])).astype(BF16)
    vv[...] = (dot(nrm[0], w_v[0]) + dot(nrm[1], w_v[1])).astype(BF16)

    keys = PACK * groups
    lane = lax.broadcasted_iota(jnp.int32, (keys, 2 * ch), 1)
    head_of = lax.rem(lane, ch) // per_head
    ones_row = lax.broadcasted_iota(jnp.int32, (16, keys * heads), 0)
    ones_col = lax.broadcasted_iota(jnp.int32, (16, keys * heads), 1)
    ones = jnp.where(ones_row == ones_col // keys, 1.0, 0.0).astype(BF16)

    def attend(p, carry):
        at = pl.ds(pl.multiple_of(p * groups, groups), groups)

        def stack(ref):
            return jnp.concatenate(
                [ref[at, u * 2 * ch : (u + 1) * 2 * ch] for u in range(PACK)], axis=0
            )

        queries = jnp.concatenate([stack(qe), stack(qo)], axis=0)
        key = stack(kk)
        zero = jnp.zeros_like(key)
        key_heads = jnp.concatenate(
            [jnp.where(head_of == h, key, zero) for h in range(heads)], axis=0
        )
        scores = dot_nt(key_heads, queries)
        weights = []
        for h in range(heads):
            part = scores[h * keys : (h + 1) * keys]
            top = jnp.max(part, axis=0, keepdims=True)
            weights.append(jnp.exp2(part - top).astype(BF16))
        weights = jnp.concatenate(weights, axis=0)
        value_t = stack(vv).astype(F32).T.astype(BF16)
        blank = jnp.zeros((per_head, keys), BF16)
        rows = []
        for q in range(2):
            for h in range(heads):
                base = q * ch + h * per_head
                rows.append(
                    jnp.concatenate(
                        [
                            value_t[base : base + per_head] if m == h else blank
                            for m in range(heads)
                        ],
                        axis=1,
                    )
                )
        rows.append(ones)
        summed = dot(jnp.concatenate(rows, axis=0), weights)
        inv = 1.0 / summed[2 * ch : 2 * ch + heads]
        blocks = []
        for q in range(2):
            cols = slice(q * keys, (q + 1) * keys)
            for h in range(heads):
                base = q * ch + h * per_head
                blocks.append(
                    summed[base : base + per_head, cols] * inv[h : h + 1, cols]
                )
        mixed = jnp.concatenate(blocks, axis=0).T
        for u in range(PACK):
            mix[at, u * 2 * ch : (u + 1) * 2 * ch] = mixed[
                u * groups : (u + 1) * groups
            ].astype(BF16)
        return carry

    lax.fori_loop(0, pairs, attend, 0)

    for q in range(2):
        attended = sec[q] + dot(mix[...], w_out[q])
        logits = dot(attended.astype(BF16), w_gate[...]) + gate_off[...]
        sec[q] = sigmoid(logits)

    def scatter(p, carry):
        at = pl.ds(pl.multiple_of(p * groups, groups), groups)
        for q in range(2):
            for b in range(wide // 128):
                sf[b, pl.ds(2 * p + q, groups, stride=pixels), :] = sec[
                    q, at, b * 128 : (b + 1) * 128
                ]
        return carry

    lax.fori_loop(0, pairs, scatter, 0)
    slab = groups // nd
    for a in range(nd):
        g0 = lax.rem(xi + a, nd) * slab
        for g in range(slab):
            row = pl.ds(pl.multiple_of((g0 + g) * pixels, pixels), pixels)
            for b in range(wide // 128):
                at = g * wide + b * 128
                outs[a][:, at : at + 128] = sf[b, row, :].astype(BF16)


def disparity(nd, nc, heads, spot, pieces, weights):
    pixels, lanes = pieces[0].shape
    band = weights[0]
    wide = band.shape[2]
    groups = lanes * nd * nc // wide
    pad = band.shape[1] // 2
    pairs = pixels // 2
    scratch = [
        pltpu.VMEM((groups + 2 * pad, pixels, wide), BF16),
        pltpu.VMEM((groups + 2 * pad, pixels, wide), BF16),
        pltpu.VMEM((wide // 128, groups * pixels, 128), F32),
        pltpu.VMEM((2, pairs * groups, wide), BF16),
        pltpu.VMEM((pairs * groups, 2 * wide), BF16),
        pltpu.VMEM((pairs * groups, 2 * wide), BF16),
        pltpu.VMEM((pairs * groups, 2 * wide), BF16),
        pltpu.VMEM((pairs * groups, 2 * wide), BF16),
        pltpu.VMEM((pairs * groups, 2 * wide), BF16),
        pltpu.VMEM((2, pairs * groups, wide), F32),
    ]
    return pl.pallas_call(
        functools.partial(disparity_kernel, nd, nc, heads),
        out_shape=[jax.ShapeDtypeStruct((pixels, groups * wide // nd), BF16)] * nd,
        in_specs=[smem()] + [vmem()] * (nd * nc + 12),
        out_specs=[vmem()] * nd,
        scratch_shapes=scratch,
        compiler_params=pltpu.CompilerParams(vmem_limit_bytes=32 << 20),
        name="disparity",
    )(spot, *pieces, *weights)


def gate_kernel(nd, spot, volume, *refs):
    gates, out = refs[:nd], refs[nd]
    rows, cols, lanes = volume.shape
    part = rows // nd
    for a in range(nd):
        top = lax.rem(spot[0] - a + nd, nd) * part
        for r in range(part):
            g = gates[a][r * cols : (r + 1) * cols]
            v = volume[top + r].astype(F32) * g.astype(F32)
            out[top + r] = v.astype(BF16)


def gate(nd, spot, volume, gates):
    return pl.pallas_call(
        functools.partial(gate_kernel, nd),
        out_shape=jax.ShapeDtypeStruct(volume.shape, volume.dtype),
        in_specs=[smem()] + [vmem()] * (1 + nd),
        out_specs=vmem(),
        compiler_params=pltpu.CompilerParams(vmem_limit_bytes=8 << 20),
        name="gate",
    )(spot, volume, *gates)


def shift_pairs(sizes, moves):
    out = []
    count = math.prod(sizes)
    for flat in range(count):
        rest, place = flat, []
        for size in reversed(sizes):
            place.append(rest % size)
            rest //= size
        place = place[::-1]
        target = 0
        for at, move, size in zip(place, moves, sizes):
            target = target * size + (at + move) % size
        out.append((flat, target))
    return out


def per_device(
    volume,
    planar_taps,
    planar_bias,
    shift_taps,
    shift_bias,
    norm_gain,
    qkv,
    exit_proj,
    head_scale,
    gate_proj,
    gate_bias,
):
    rows, cols, flat = volume.shape
    layers, ch = planar_bias.shape
    heads = head_scale.shape[0]
    nz, nd, nc = [lax.axis_size(a) for a in ("rows", "disp", "cols")]
    zi, xi, ci = [lax.axis_index(a) for a in ("rows", "disp", "cols")]
    part = flat // nc

    shares = []
    for k in range(nc):
        start = lax.rem(ci + k, nc) * part
        share = lax.dynamic_slice_in_dim(volume, start, part, 2)
        if k:
            share = lax.ppermute(share, "cols", shift_pairs((nc,), (k,)))
        shares.append(share)
    order = [shares[0]] + shares[:0:-1]
    mine = jnp.concatenate(order, axis=1)

    even = lax.rem(zi + 1, 2)
    far = rows - layers
    pairs_a = [(z, z + 1) for z in range(0, nz - 1, 2)]
    pairs_b = [(z, z + 1) for z in range(1, nz - 1, 2)]
    both = lambda ps: ps + [(j, i) for i, j in ps]
    send_a = lax.dynamic_slice_in_dim(mine, even * far, layers, 0)
    send_b = lax.dynamic_slice_in_dim(mine, (1 - even) * far, layers, 0)
    halo_a = lax.ppermute(send_a, "rows", both(pairs_a))
    halo_b = lax.ppermute(send_b, "rows", both(pairs_b))

    wide_taps, band = widen(planar_taps, shift_taps)
    tile = lambda v: jnp.tile(v, (1,) * (v.ndim - 1) + (PACK,))
    eye = jnp.eye(PACK, dtype=BF16)

    def spread(w, lead, width):
        w = jnp.pad(w, ((0, 0), (lead, width - lead - w.shape[1])))
        return jnp.einsum("uv,cw->ucvw", eye, w).reshape(PACK * ch, PACK * width)

    w_q, w_key, w_val = [qkv[:, i * ch : (i + 1) * ch] for i in range(3)]
    w_qe, w_qo = spread(w_q, 0, 2 * ch), spread(w_q, ch, 2 * ch)
    w_k = jnp.stack([spread(w_key, 0, 2 * ch), spread(w_key, ch, 2 * ch)])
    w_v = jnp.stack([spread(w_val, 0, 2 * ch), spread(w_val, ch, 2 * ch)])
    scale = head_scale * (math.log2(math.e) / math.sqrt(ch // heads))
    q_scale = tile(jnp.repeat(scale, ch // heads)[None])
    q_scale = jnp.concatenate([q_scale, q_scale], axis=1)
    w_out = jnp.stack(
        [
            jnp.einsum(
                "uv,cw->ucvw", eye, jnp.pad(exit_proj, ((q * ch, ch - q * ch), (0, 0)))
            ).reshape(PACK * 2 * ch, PACK * ch)
            for q in range(2)
        ]
    )
    w_gate = spread(gate_proj, 0, ch)
    mean_mat = spread(jnp.full((ch, ch), 1.0 / ch, BF16), 0, ch)

    first_edge = lax.rem(nc - ci, nc) * cols
    last_edge = lax.rem(first_edge + nc * cols - 1, nc * cols)
    as_int = lambda v: jnp.asarray(v, jnp.int32)
    spot = jnp.stack(
        [
            as_int(v)
            for v in (first_edge, last_edge, even, zi > 0, zi < nz - 1, xi, ci)
        ]
    )
    pieces = planar(nd, nc, spot, mine, halo_a, halo_b, wide_taps, tile(planar_bias))
    got = []
    for a in range(nd):
        for k in range(nc):
            piece = pieces[a * nc + k]
            if a or k:
                piece = lax.ppermute(
                    piece, ("disp", "cols"), shift_pairs((nd, nc), (a, k))
                )
            got.append(piece)
    place = jnp.stack([as_int(xi), as_int(ci)])
    gates = disparity(
        nd,
        nc,
        heads,
        place,
        got,
        [
            band,
            tile(shift_bias),
            tile(norm_gain[None]),
            w_qe,
            w_qo,
            w_k,
            w_v,
            q_scale,
            w_out,
            w_gate,
            tile(gate_bias[None]),
            mean_mat,
        ],
    )
    gates = [
        lax.ppermute(g, "disp", shift_pairs((nd,), (a,))) if a else g
        for a, g in enumerate(gates)
    ]
    return gate(nd, place, volume, gates)


def solution(mesh):
    spec = P(("groups", "rows"), "cols", "disp")
    return jax.shard_map(
        per_device,
        mesh=mesh,
        in_specs=(spec,) + (P(),) * 10,
        out_specs=spec,
        check_vma=False,
    )
```

```python
import functools
import math

import jax
import jax.numpy as jnp
from jax import lax
from jax.experimental import pallas as pl
from jax.experimental.pallas import tpu as pltpu
from jax.sharding import PartitionSpec as P

F32 = jnp.float32
BF16 = jnp.bfloat16
PACK = 4
WIDE = 256


def vmem():
    return pl.BlockSpec(memory_space=pltpu.VMEM)


def smem():
    return pl.BlockSpec(memory_space=pltpu.SMEM)


def silu(v):
    half = 0.5 * v
    return half + half * jnp.tanh(half)


def sigmoid(v):
    return 0.5 + 0.5 * jnp.tanh(0.5 * v)


def dot(a, b):
    return jnp.dot(a, b, preferred_element_type=F32)


def dot_nt(a, b):
    return lax.dot_general(a, b, (((1,), (1,)), ((), ())), preferred_element_type=F32)


def prepare_kernel(heads, taps3, taps17, qkv, exit_proj, gate_proj, vecs, scale, *rest):
    outs, (t3, t17, wq, we, wg, vec, sems) = rest[:12], rest[12:]
    copies = [
        pltpu.make_async_copy(src, dst, sems.at[i])
        for i, (src, dst) in enumerate(
            [(taps3, t3), (taps17, t17), (qkv, wq), (exit_proj, we), (gate_proj, wg)]
        )
    ]
    for i, v in enumerate(vecs):
        copies.append(pltpu.make_async_copy(v, vec[i], sems.at[5 + i]))
    for c in copies:
        c.start()
    rows_w, band, w_qe, w_qo, w_k, w_v, w_out, w_gate, mean_mat, plane_b, shift_b, ends = outs
    layers = rows_w.shape[0]
    ch = we.shape[0]
    spans = band.shape[1]
    taps = t17.shape[1]
    zero = jnp.zeros((ch, ch), BF16)
    none = jnp.zeros((ch, 2 * ch), BF16)
    for ref in (w_qe, w_qo, w_k, w_v, w_out, w_gate):
        ref[...] = jnp.zeros_like(ref)
    r = lax.broadcasted_iota(jnp.int32, mean_mat.shape, 0) // ch
    c = lax.broadcasted_iota(jnp.int32, mean_mat.shape, 1) // ch
    mean_mat[...] = jnp.where(r == c, 1.0 / ch, 0.0).astype(BF16)
    for c in copies:
        c.wait()

    def pair(x, y):
        return jnp.concatenate([x, y], axis=1)

    def planar_block(layer, carry):
        for j in range(3):
            tap = [t3[layer * 9 + i * 3 + j] for i in range(3)] + [zero]
            for rr in range(6):
                top = (j * 6 + rr) * ch
                for b in range(2):
                    t = rr - 2 * b
                    block = none
                    if 0 <= t <= 3:
                        block = pair(tap[t], tap[t - 1] if t else zero)
                    rows_w[layer, top : top + ch, b * 2 * ch : (b + 1) * 2 * ch] = block
        return carry

    lax.fori_loop(0, layers, planar_block, 0)

    def band_block(s, carry):
        table = []
        for t in range(taps + 1):
            table.append(
                pair(t17[s, t] if t < taps else zero, t17[s, t - 1] if t else zero)
            )
        for j in range(spans):
            for u in range(PACK):
                for b in range(PACK // 2):
                    t = PACK * (j - spans // 2) + u - 2 * b + taps // 2
                    block = table[t] if 0 <= t <= taps else none
                    band[s, j, u * ch : (u + 1) * ch, 2 * b * ch : 2 * (b + 1) * ch] = block
        return carry

    lax.fori_loop(0, 2, band_block, 0)
    w = wq[...]
    parts = [w[:, i * ch : (i + 1) * ch] for i in range(3)]
    lo = [pair(p, zero) for p in parts]
    hi = [pair(zero, p) for p in parts]
    out_lo, out_hi = pair(we[...], zero), pair(zero, we[...])
    gate_lo, gate_hi = pair(wg[...], zero), pair(zero, wg[...])
    for u in range(PACK):
        rows = slice(u * ch, (u + 1) * ch)
        lanes = slice(u * 2 * ch, (u + 1) * 2 * ch)
        w_qe[rows, lanes] = lo[0]
        w_qo[rows, lanes] = hi[0]
        w_k[0, rows, lanes] = lo[1]
        w_k[1, rows, lanes] = hi[1]
        w_v[0, rows, lanes] = lo[2]
        w_v[1, rows, lanes] = hi[2]
        tile = slice((u // 2) * 2 * ch, (u // 2 + 1) * 2 * ch)
        for q in range(2):
            at = u * 2 * ch + q * ch
            w_out[q, at : at + ch, tile] = out_hi if u % 2 else out_lo
        w_gate[rows, tile] = gate_hi if u % 2 else gate_lo

    def tiled(v):
        return jnp.concatenate([v] * PACK, axis=1)

    plane_b[...] = tiled(vec[0][...])
    shift_b[...] = tiled(vec[1][...])
    ends[0:1] = tiled(vec[2][...])
    ends[1:2] = tiled(vec[3][...])
    head = lax.rem(lax.broadcasted_iota(jnp.int32, (1, PACK * ch), 1), ch) // (ch // heads)
    row = jnp.zeros((1, PACK * ch), F32)
    for h in range(heads):
        row = jnp.where(head == h, scale[0, h], row)
    ends[2:3] = row * (math.log2(math.e) / math.sqrt(ch // heads))


def prepare(planar_taps, planar_bias, shift_taps, shift_bias, gain, qkv, exit_proj, head_scale, gate_proj, gate_bias):
    layers, ch = planar_bias.shape
    taps = shift_taps.shape[1]
    heads = head_scale.shape[0]
    spans = 2 * (-(-(taps // 2) // PACK)) + 1
    size = PACK * ch
    sds = jax.ShapeDtypeStruct
    outs = [
        sds((layers, 18 * ch, size), BF16),
        sds((2, spans, size, size), BF16),
        sds((size, 2 * size), BF16),
        sds((size, 2 * size), BF16),
        sds((2, size, 2 * size), BF16),
        sds((2, size, 2 * size), BF16),
        sds((2, 2 * size, size), BF16),
        sds((size, size), BF16),
        sds((size, size), BF16),
        sds((layers, size), F32),
        sds((2, size), F32),
        sds((3, size), F32),
    ]
    anywhere = pl.BlockSpec(memory_space=pl.ANY)
    vecs = [planar_bias, shift_bias, gain[None], gate_bias[None]]
    big = [planar_taps.reshape(layers * 9, ch, ch), shift_taps, qkv, exit_proj, gate_proj]

    def body(*refs):
        prepare_kernel(heads, *refs[:5], refs[5:9], refs[9], *refs[10:22], *refs[22:27], refs[27:31], refs[31])

    return pl.pallas_call(
        body,
        out_shape=outs,
        in_specs=[anywhere] * 9 + [smem()],
        out_specs=[vmem()] * 12,
        scratch_shapes=[pltpu.VMEM(v.shape, v.dtype) for v in big + vecs]
        + [pltpu.SemaphoreType.DMA((9,))],
        compiler_params=pltpu.CompilerParams(vmem_limit_bytes=10 << 20),
        cost_estimate=pl.CostEstimate(flops=0, bytes_accessed=8 << 20, transcendentals=0),
        name="prepare",
    )(*big, *vecs, head_scale[None])


def cut_kernel(nc, axis, volume, *rest):
    outs, sems = rest[:nc], rest[nc]
    lanes = outs[0].shape[2]
    ci = lax.axis_index(axis)
    copies = []
    for k in range(nc):
        start = pl.multiple_of(lax.rem(ci + k, nc) * lanes, lanes)
        copies.append(
            pltpu.make_async_copy(volume.at[:, :, pl.ds(start, lanes)], outs[k], sems.at[k])
        )
    for c in copies:
        c.start()
    for c in copies:
        c.wait()


def cut(nc, volume):
    rows, cols, lanes = volume.shape
    return pl.pallas_call(
        functools.partial(cut_kernel, nc, "cols"),
        out_shape=[jax.ShapeDtypeStruct((rows, cols, lanes // nc), BF16)] * nc,
        in_specs=[pl.BlockSpec(memory_space=pl.ANY)],
        out_specs=[vmem()] * nc,
        scratch_shapes=[pltpu.SemaphoreType.DMA((nc,))],
        compiler_params=pltpu.CompilerParams(vmem_limit_bytes=2 << 20),
        name="cut",
    )(volume)


def pack_kernel(nc, halo, *refs):
    pieces, outs = refs[:nc], refs[nc:]
    rows = pieces[0].shape[0]
    even = lax.rem(lax.axis_index("rows") + 1, 2)
    for i, far in enumerate((even, 1 - even)):
        top = far * (rows - halo)
        for r in range(halo):
            for k in range(nc):
                outs[i][r, k] = pieces[k][top + r]


def pack(nc, halo, pieces):
    rows, cols, lanes = pieces[0].shape
    return pl.pallas_call(
        functools.partial(pack_kernel, nc, halo),
        out_shape=[jax.ShapeDtypeStruct((halo, nc, cols, lanes), BF16)] * 2,
        in_specs=[vmem()] * nc,
        out_specs=[vmem()] * 2,
        compiler_params=pltpu.CompilerParams(vmem_limit_bytes=3 << 20),
        name="pack",
    )(*pieces)


def planar_kernel(nd, nc, *refs):
    pieces = refs[:nc]
    halo_a, halo_b, weights, bias = refs[nc : nc + 4]
    outs = refs[nc + 4 : nc + 4 + nd * nc]
    flat, x1, *xs, last, back = refs[nc + 4 + nd * nc :]
    rows, own, lanes = pieces[0].shape
    halo = halo_a.shape[0]
    layers = bias.shape[0]
    cols = own * nc
    tiles = lanes // 128
    ch = 64
    total = rows + 2 * halo
    xi, ci, zi = [lax.axis_index(n) for n in ("disp", "cols", "rows")]
    nz = lax.axis_size("rows")
    even = lax.rem(zi + 1, 2)
    at_a = even * (halo + rows)
    at_b = (1 - even) * (halo + rows)
    bases = [lax.rem(ci + m, nc) * own for m in range(nc)]

    def put(r, m, value):
        for t in range(tiles):
            at = pl.ds(pl.multiple_of(t * cols + bases[m], own), own)
            flat[r, at, :] = value[:, t * 128 : (t + 1) * 128].astype(F32)

    def put_own(r, carry):
        for m in range(nc):
            put(halo + r, m, pieces[m][r])
        return carry

    def put_halo(r, carry):
        for m in range(nc):
            put(at_a + r, m, halo_a[r, m])
            put(at_b + r, m, halo_b[r, m])
        return carry

    lax.fori_loop(0, rows, put_own, 0)
    lax.fori_loop(0, halo, put_halo, 0)
    low = lax.broadcasted_iota(jnp.int32, (tiles, 128), 1) < ch
    stages = [x1] + xs
    for x in stages:
        x[0] = jnp.zeros(x.shape[1:], BF16)
        x[cols + 1] = jnp.zeros(x.shape[1:], BF16)

    def turn(c, carry):
        at = pl.ds(c, tiles, stride=cols)
        for p in range(total // 2):
            a, b = flat[2 * p, at, :], flat[2 * p + 1, at, :]
            e = jnp.where(low, a, pltpu.roll(b, ch, 1))
            o = jnp.where(low, pltpu.roll(a, ch, 1), b)
            x1[c + 1, :, p * 128 : (p + 1) * 128] = jnp.concatenate([e, o], axis=0).astype(BF16)
        return carry

    lax.fori_loop(0, cols, turn, 0, unroll=4)
    block = max(1, 512 // (2 * tiles))
    while cols % block:
        block -= 1
    size = block * 2 * tiles
    row_of = lax.broadcasted_iota(jnp.int32, (1, 256), 1) // ch
    for layer in range(layers):
        height = total - 2 * (layer + 1)
        beyond = layers - 1 - layer
        src = stages[layer]
        for q in range(0, height // 2, 2):
            single = q + 1 == height // 2
            span = 128 * (2 if single else 3)
            width = 128 if single else 256
            row = row_of[:, :width] + 2 * q
            keep = jnp.ones((1, width), F32)
            keep = jnp.where((row < beyond) & (zi == 0), 0.0, keep)
            keep = jnp.where((row >= height - beyond) & (zi == nz - 1), 0.0, keep)

            def run(i, carry):
                c0 = i * block
                lhs = jnp.concatenate(
                    [
                        src[pl.ds(c0 + j, block), :, q * 128 : q * 128 + span].reshape(size, span)
                        for j in range(3)
                    ],
                    axis=1,
                )
                if single:
                    rhs = jnp.concatenate(
                        [weights[layer, j * 384 : j * 384 + span, :width] for j in range(3)], axis=0
                    )
                else:
                    rhs = weights[layer]
                y = silu(dot(lhs, rhs) + bias[layer : layer + 1, :width])
                if layer < layers - 1:
                    y = (y * keep).astype(BF16).reshape(block, 2 * tiles, width)
                    stages[layer + 1][pl.ds(c0 + 1, block), :, q * 128 : q * 128 + width] = y
                else:
                    y = y.reshape(block, 2 * tiles, width)
                    last[pl.ds(c0, block), :, q * 128 : q * 128 + width] = y
                return carry

            lax.fori_loop(0, cols // block, run, 0)

    def turn_back(c, carry):
        at = pl.ds(c, tiles, stride=cols)
        for p in range(rows // 2):
            e = last[c, :tiles, p * 128 : (p + 1) * 128]
            o = last[c, tiles:, p * 128 : (p + 1) * 128]
            back[2 * p, at, :] = jnp.where(low, e, pltpu.roll(o, ch, 1))
            back[2 * p + 1, at, :] = jnp.where(low, pltpu.roll(e, ch, 1), o)
        return carry

    lax.fori_loop(0, cols, turn_back, 0, unroll=4)
    part = rows // nd
    for a in range(nd):
        top = lax.rem(xi + a, nd) * part
        for r in range(part):
            for m in range(nc):
                for t in range(tiles):
                    at = pl.ds(pl.multiple_of(t * cols + bases[m], own), own)
                    outs[a * nc + m][r * own : (r + 1) * own, t * 128 : (t + 1) * 128] = back[
                        top + r, at, :
                    ].astype(BF16)


def planar(nd, nc, pieces, halo_a, halo_b, weights, bias):
    rows, own, lanes = pieces[0].shape
    layers = bias.shape[0]
    halo = halo_a.shape[0]
    cols = own * nc
    tiles = lanes // 128
    total = rows + 2 * halo
    pixels = rows * cols // (nd * nc)
    scratch = [pltpu.VMEM((total, tiles * cols, 128), F32)]
    scratch += [
        pltpu.VMEM((cols + 2, 2 * tiles, (total // 2 - k) * 128), BF16) for k in range(layers)
    ]
    scratch += [
        pltpu.VMEM((cols, 2 * tiles, rows * 64), F32),
        pltpu.VMEM((rows, tiles * cols, 128), F32),
    ]
    return pl.pallas_call(
        functools.partial(planar_kernel, nd, nc),
        out_shape=[jax.ShapeDtypeStruct((pixels, lanes), BF16)] * (nd * nc),
        in_specs=[vmem()] * (nc + 4),
        out_specs=[vmem()] * (nd * nc),
        scratch_shapes=scratch,
        compiler_params=pltpu.CompilerParams(vmem_limit_bytes=18 << 20),
        name="planar",
    )(*pieces, halo_a, halo_b, weights, bias)


def disparity_kernel(
    nd,
    nc,
    heads,
    *refs,
):
    pieces = refs[: nd * nc]
    band, bias, ends, w_qe, w_qo, w_k, w_v, w_out, w_gate, mean_mat = refs[nd * nc : nd * nc + 10]
    outs = refs[nd * nc + 10 : nd * nc + 10 + nd]
    xs, ys, sf, nrm, qe, qo, kk, vv, mix, sec = refs[nd * nc + 10 + nd :]
    gain, gate_off = ends[0:1], ends[1:2]
    q_scale = jnp.concatenate([ends[2:3]] * 2, axis=1)
    pixels, lanes = pieces[0].shape
    wide = band.shape[2]
    per_piece = lanes // wide
    groups = per_piece * nd * nc
    spans = band.shape[1]
    pad = spans // 2
    ch = wide // PACK
    per_head = ch // heads
    pairs = pixels // 2
    xi, ci = lax.axis_index("disp"), lax.axis_index("cols")

    for side in range(pad):
        xs[side] = jnp.zeros((pixels, wide), BF16)
        xs[pad + groups + side] = jnp.zeros((pixels, wide), BF16)
        ys[side] = jnp.zeros((pixels, wide), BF16)
        ys[pad + groups + side] = jnp.zeros((pixels, wide), BF16)
    for a in range(nd):
        for k in range(nc):
            src_x = lax.rem(xi - a + nd, nd)
            src_c = lax.rem(ci - k + nc, nc)
            at = pad + (src_x * nc + src_c) * per_piece
            piece = pieces[a * nc + k]
            for g in range(per_piece):
                xs[at + g] = piece[:, g * wide : (g + 1) * wide]

    step = math.gcd(groups, 16)

    def conv(src, s, g0):
        acc = None
        for j in range(spans):
            lhs = src[pl.ds(g0 + j, step)].reshape(step * pixels, wide)
            part = dot(lhs, band[s, j])
            acc = part if acc is None else acc + part
        return acc + bias[s : s + 1]

    def first(i, carry):
        g0 = i * step
        y = silu(conv(xs, 0, g0)).astype(BF16)
        ys[pl.ds(pad + g0, step)] = y.reshape(step, pixels, wide)
        return carry

    lax.fori_loop(0, groups // step, first, 0)

    def second(i, carry):
        g0 = i * step
        y = conv(ys, 1, g0).astype(BF16).astype(F32)
        for b in range(wide // 128):
            sf[b, pl.ds(pl.multiple_of(g0 * pixels, 8), step * pixels), :] = y[
                :, b * 128 : (b + 1) * 128
            ]
        return carry

    lax.fori_loop(0, groups // step, second, 0)

    def gather(p, carry):
        at = pl.ds(pl.multiple_of(p * groups, groups), groups)
        for q in range(2):
            for b in range(wide // 128):
                piece = sf[b, pl.ds(2 * p + q, groups, stride=pixels), :]
                sec[q, at, b * 128 : (b + 1) * 128] = piece
        return carry

    lax.fori_loop(0, pairs, gather, 0)

    for q in range(2):
        s = sec[q]
        sq = s * s
        hi = sq.astype(BF16)
        lo = (sq - hi.astype(F32)).astype(BF16)
        mean = dot(hi, mean_mat[...]) + dot(lo, mean_mat[...])
        nrm[q] = (s * lax.rsqrt(mean + 1e-05) * gain).astype(BF16)
    qe[...] = (dot(nrm[0], w_qe[...]) * q_scale).astype(BF16)
    qo[...] = (dot(nrm[1], w_qo[...]) * q_scale).astype(BF16)
    kk[...] = (dot(nrm[0], w_k[0]) + dot(nrm[1], w_k[1])).astype(BF16)
    vv[...] = (dot(nrm[0], w_v[0]) + dot(nrm[1], w_v[1])).astype(BF16)

    keys = PACK * groups
    lane = lax.broadcasted_iota(jnp.int32, (keys, 2 * ch), 1)
    head_of = lax.rem(lane, ch) // per_head
    ones_row = lax.broadcasted_iota(jnp.int32, (16, keys * heads), 0)
    ones_col = lax.broadcasted_iota(jnp.int32, (16, keys * heads), 1)
    ones = jnp.where(ones_row == ones_col // keys, 1.0, 0.0).astype(BF16)

    def attend(p, carry):
        at = pl.ds(pl.multiple_of(p * groups, groups), groups)

        def stack(ref):
            return jnp.concatenate(
                [ref[at, u * 2 * ch : (u + 1) * 2 * ch] for u in range(PACK)], axis=0
            )

        queries = jnp.concatenate([stack(qe), stack(qo)], axis=0)
        key = stack(kk)
        zero = jnp.zeros_like(key)
        key_heads = jnp.concatenate(
            [jnp.where(head_of == h, key, zero) for h in range(heads)], axis=0
        )
        scores = dot_nt(key_heads, queries)
        weights = []
        for h in range(heads):
            part = scores[h * keys : (h + 1) * keys]
            top = jnp.max(part, axis=0, keepdims=True)
            weights.append(jnp.exp2(part - top).astype(BF16))
        weights = jnp.concatenate(weights, axis=0)
        value_t = stack(vv).astype(F32).T.astype(BF16)
        blank = jnp.zeros((per_head, keys), BF16)
        rows = []
        for q in range(2):
            for h in range(heads):
                base = q * ch + h * per_head
                rows.append(
                    jnp.concatenate(
                        [
                            value_t[base : base + per_head] if m == h else blank
                            for m in range(heads)
                        ],
                        axis=1,
                    )
                )
        rows.append(ones)
        summed = dot(jnp.concatenate(rows, axis=0), weights)
        inv = 1.0 / summed[2 * ch : 2 * ch + heads]
        blocks = []
        for q in range(2):
            cols = slice(q * keys, (q + 1) * keys)
            for h in range(heads):
                base = q * ch + h * per_head
                blocks.append(
                    summed[base : base + per_head, cols] * inv[h : h + 1, cols]
                )
        mixed = jnp.concatenate(blocks, axis=0).T
        for u in range(PACK):
            mix[at, u * 2 * ch : (u + 1) * 2 * ch] = mixed[
                u * groups : (u + 1) * groups
            ].astype(BF16)
        return carry

    lax.fori_loop(0, pairs, attend, 0, unroll=2)

    for q in range(2):
        attended = sec[q] + dot(mix[...], w_out[q])
        logits = dot(attended.astype(BF16), w_gate[...]) + gate_off
        sec[q] = sigmoid(logits)

    def scatter(p, carry):
        at = pl.ds(pl.multiple_of(p * groups, groups), groups)
        for q in range(2):
            for b in range(wide // 128):
                sf[b, pl.ds(2 * p + q, groups, stride=pixels), :] = sec[
                    q, at, b * 128 : (b + 1) * 128
                ]
        return carry

    lax.fori_loop(0, pairs, scatter, 0)
    slab = groups // nd
    for a in range(nd):
        g0 = lax.rem(xi + a, nd) * slab
        for g in range(slab):
            row = pl.ds(pl.multiple_of((g0 + g) * pixels, pixels), pixels)
            for b in range(wide // 128):
                at = g * wide + b * 128
                outs[a][:, at : at + 128] = sf[b, row, :].astype(BF16)


def disparity(nd, nc, heads, pieces, weights):
    pixels, lanes = pieces[0].shape
    band = weights[0]
    wide = band.shape[2]
    groups = lanes * nd * nc // wide
    pad = band.shape[1] // 2
    pairs = pixels // 2
    scratch = [
        pltpu.VMEM((groups + 2 * pad, pixels, wide), BF16),
        pltpu.VMEM((groups + 2 * pad, pixels, wide), BF16),
        pltpu.VMEM((wide // 128, groups * pixels, 128), F32),
        pltpu.VMEM((2, pairs * groups, wide), BF16),
        pltpu.VMEM((pairs * groups, 2 * wide), BF16),
        pltpu.VMEM((pairs * groups, 2 * wide), BF16),
        pltpu.VMEM((pairs * groups, 2 * wide), BF16),
        pltpu.VMEM((pairs * groups, 2 * wide), BF16),
        pltpu.VMEM((pairs * groups, 2 * wide), BF16),
        pltpu.VMEM((2, pairs * groups, wide), F32),
    ]
    return pl.pallas_call(
        functools.partial(disparity_kernel, nd, nc, heads),
        out_shape=[jax.ShapeDtypeStruct((pixels, groups * wide // nd), BF16)] * nd,
        in_specs=[vmem()] * (nd * nc + 10),
        out_specs=[vmem()] * nd,
        scratch_shapes=scratch,
        compiler_params=pltpu.CompilerParams(vmem_limit_bytes=20 << 20),
        name="disparity",
    )(*pieces, *weights)


def gate_kernel(nd, volume, *refs):
    gates, out = refs[:nd], refs[nd]
    rows, cols, lanes = volume.shape
    part = rows // nd
    for a in range(nd):
        top = lax.rem(lax.axis_index("disp") - a + nd, nd) * part
        for r in range(part):
            g = gates[a][r * cols : (r + 1) * cols]
            v = volume[top + r].astype(F32) * g.astype(F32)
            out[top + r] = v.astype(BF16)


def gate(nd, volume, gates):
    return pl.pallas_call(
        functools.partial(gate_kernel, nd),
        out_shape=jax.ShapeDtypeStruct(volume.shape, volume.dtype),
        in_specs=[vmem()] * (1 + nd),
        out_specs=vmem(),
        compiler_params=pltpu.CompilerParams(vmem_limit_bytes=3 << 20),
        name="gate",
    )(volume, *gates)


def shift_pairs(sizes, moves):
    out = []
    count = math.prod(sizes)
    for flat in range(count):
        rest, place = flat, []
        for size in reversed(sizes):
            place.append(rest % size)
            rest //= size
        place = place[::-1]
        target = 0
        for at, move, size in zip(place, moves, sizes):
            target = target * size + (at + move) % size
        out.append((flat, target))
    return out


def per_device(
    volume,
    planar_taps,
    planar_bias,
    shift_taps,
    shift_bias,
    norm_gain,
    qkv,
    exit_proj,
    head_scale,
    gate_proj,
    gate_bias,
):
    layers = planar_bias.shape[0]
    heads = head_scale.shape[0]
    nz, nd, nc = [lax.axis_size(a) for a in ("rows", "disp", "cols")]

    shares = [
        lax.ppermute(v, "cols", shift_pairs((nc,), (k,))) if k else v
        for k, v in enumerate(cut(nc, volume))
    ]
    mine = [shares[0]] + shares[:0:-1]
    send_a, send_b = pack(nc, layers, mine)
    pairs_a = [(z, z + 1) for z in range(0, nz - 1, 2)]
    pairs_b = [(z, z + 1) for z in range(1, nz - 1, 2)]
    halo_a = lax.ppermute(send_a, "rows", pairs_a + [(j, i) for i, j in pairs_a])
    halo_b = lax.ppermute(send_b, "rows", pairs_b + [(j, i) for i, j in pairs_b])

    rows_w, band, w_qe, w_qo, w_k, w_v, w_out, w_gate, mean_mat, plane_b, shift_b, ends = prepare(
        planar_taps,
        planar_bias,
        shift_taps,
        shift_bias,
        norm_gain,
        qkv,
        exit_proj,
        head_scale,
        gate_proj,
        gate_bias,
    )
    pieces = planar(nd, nc, mine, halo_a, halo_b, rows_w, plane_b)
    got = []
    for a in range(nd):
        for k in range(nc):
            piece = pieces[a * nc + k]
            if a or k:
                piece = lax.ppermute(piece, ("disp", "cols"), shift_pairs((nd, nc), (a, k)))
            got.append(piece)
    gates = disparity(
        nd, nc, heads, got, [band, shift_b, ends, w_qe, w_qo, w_k, w_v, w_out, w_gate, mean_mat]
    )
    gates = [
        lax.ppermute(g, "disp", shift_pairs((nd,), (a,))) if a else g for a, g in enumerate(gates)
    ]
    return gate(nd, volume, gates)


def solution(mesh):
    spec = P(("groups", "rows"), "cols", "disp")
    return jax.shard_map(
        per_device,
        mesh=mesh,
        in_specs=(spec,) + (P(),) * 10,
        out_specs=spec,
        check_vma=False,
    )
```

```python
import functools
import math

import jax
import jax.numpy as jnp
from jax import lax
from jax.experimental import pallas as pl
from jax.experimental.pallas import tpu as pltpu
from jax.sharding import PartitionSpec as P


F32 = jnp.float32
BF16 = jnp.bfloat16
PACK = 4
WIDE = 256


def vmem():
    return pl.BlockSpec(memory_space=pltpu.VMEM)


def silu(v):
    half = 0.5 * v
    return half + half * jnp.tanh(half)


def sigmoid(v):
    return 0.5 + 0.5 * jnp.tanh(0.5 * v)


def dot(a, b):
    return jnp.dot(a, b, preferred_element_type=F32)


def dot_nt(a, b):
    return lax.dot_general(a, b, (((1,), (1,)), ((), ())), preferred_element_type=F32)


def prepare_kernel(heads, taps3, taps17, qkv, exit_proj, gate_proj, vecs, *rest):
    outs, (t3, t17, wq, we, wg, vec, sems) = rest[:12], rest[12:]
    copies = [
        pltpu.make_async_copy(src, dst, sems.at[i])
        for i, (src, dst) in enumerate(
            [(taps3, t3), (taps17, t17), (qkv, wq), (exit_proj, we), (gate_proj, wg)]
        )
    ]
    for i, v in enumerate(vecs):
        copies.append(pltpu.make_async_copy(v, vec[i], sems.at[5 + i]))
    for c in copies:
        c.start()
    rows_w, band, w_qe, w_qo, w_k, w_v, w_out, w_gate, mean_mat, plane_b, shift_b, ends = outs
    layers = rows_w.shape[0]
    ch = we.shape[0]
    spans = band.shape[1]
    taps = t17.shape[1]
    zero = jnp.zeros((ch, ch), BF16)
    none = jnp.zeros((ch, 2 * ch), BF16)
    for ref in (w_qe, w_qo, w_k, w_v, w_out, w_gate):
        ref[...] = jnp.zeros_like(ref)
    r = lax.broadcasted_iota(jnp.int32, mean_mat.shape, 0) // ch
    c = lax.broadcasted_iota(jnp.int32, mean_mat.shape, 1) // ch
    mean_mat[...] = jnp.where(r == c, 1.0 / ch, 0.0).astype(BF16)
    for c in copies:
        c.wait()

    def pair(x, y):
        return jnp.concatenate([x, y], axis=1)

    def planar_block(layer, carry):
        for j in range(3):
            tap = [t3[layer * 9 + i * 3 + j] for i in range(3)] + [zero]
            for rr in range(6):
                top = (j * 6 + rr) * ch
                for b in range(2):
                    t = rr - 2 * b
                    block = none
                    if 0 <= t <= 3:
                        block = pair(tap[t], tap[t - 1] if t else zero)
                    rows_w[layer, top : top + ch, b * 2 * ch : (b + 1) * 2 * ch] = block
        return carry

    lax.fori_loop(0, layers, planar_block, 0)

    def band_block(s, carry):
        table = []
        for t in range(taps + 1):
            table.append(
                pair(t17[s, t] if t < taps else zero, t17[s, t - 1] if t else zero)
            )
        for j in range(spans):
            for u in range(PACK):
                for b in range(PACK // 2):
                    t = PACK * (j - spans // 2) + u - 2 * b + taps // 2
                    block = table[t] if 0 <= t <= taps else none
                    band[s, j, u * ch : (u + 1) * ch, 2 * b * ch : 2 * (b + 1) * ch] = block
        return carry

    lax.fori_loop(0, 2, band_block, 0)
    w = wq[...]
    parts = [w[:, i * ch : (i + 1) * ch] for i in range(3)]
    lo = [pair(p, zero) for p in parts]
    hi = [pair(zero, p) for p in parts]
    out_lo, out_hi = pair(we[...], zero), pair(zero, we[...])
    gate_lo, gate_hi = pair(wg[...], zero), pair(zero, wg[...])
    for u in range(PACK):
        rows = slice(u * ch, (u + 1) * ch)
        lanes = slice(u * 2 * ch, (u + 1) * 2 * ch)
        w_qe[rows, lanes] = lo[0]
        w_qo[rows, lanes] = hi[0]
        w_k[0, rows, lanes] = lo[1]
        w_k[1, rows, lanes] = hi[1]
        w_v[0, rows, lanes] = lo[2]
        w_v[1, rows, lanes] = hi[2]
        tile = slice((u // 2) * 2 * ch, (u // 2 + 1) * 2 * ch)
        for q in range(2):
            at = u * 2 * ch + q * ch
            w_out[q, at : at + ch, tile] = out_hi if u % 2 else out_lo
        w_gate[rows, tile] = gate_hi if u % 2 else gate_lo

    def tiled(v):
        return jnp.concatenate([v] * PACK, axis=1)

    plane_b[...] = tiled(vec[0][...])
    shift_b[...] = tiled(vec[1][...])
    ends[0:1] = tiled(vec[2][...])
    ends[1:2] = tiled(vec[3][...])
    head = lax.rem(lax.broadcasted_iota(jnp.int32, (1, PACK * ch), 1), ch) // (ch // heads)
    row = jnp.zeros((1, PACK * ch), F32)
    for h in range(heads):
        row = jnp.where(head == h, vec[4][:, h : h + 1], row)
    ends[2:3] = row * (math.log2(math.e) / math.sqrt(ch // heads))


def prepare(planar_taps, planar_bias, shift_taps, shift_bias, gain, qkv, exit_proj, head_scale, gate_proj, gate_bias):
    layers, ch = planar_bias.shape
    taps = shift_taps.shape[1]
    heads = head_scale.shape[0]
    spans = 2 * (-(-(taps // 2) // PACK)) + 1
    size = PACK * ch
    sds = jax.ShapeDtypeStruct
    outs = [
        sds((layers, 18 * ch, size), BF16),
        sds((2, spans, size, size), BF16),
        sds((size, 2 * size), BF16),
        sds((size, 2 * size), BF16),
        sds((2, size, 2 * size), BF16),
        sds((2, size, 2 * size), BF16),
        sds((2, 2 * size, size), BF16),
        sds((size, size), BF16),
        sds((size, size), BF16),
        sds((layers, size), F32),
        sds((2, size), F32),
        sds((3, size), F32),
    ]
    anywhere = pl.BlockSpec(memory_space=pltpu.HBM)
    vecs = [planar_bias, shift_bias, gain[None], gate_bias[None], head_scale[None]]
    big = [planar_taps.reshape(layers * 9, ch, ch), shift_taps, qkv, exit_proj, gate_proj]

    def body(*refs):
        prepare_kernel(heads, *refs[:5], refs[5:10], *refs[10:22], *refs[22:27], refs[27:32], refs[32])

    return pl.pallas_call(
        body,
        out_shape=outs,
        in_specs=[anywhere] * 10,
        out_specs=[vmem()] * 12,
        scratch_shapes=[pltpu.VMEM(v.shape, v.dtype) for v in big + vecs]
        + [pltpu.SemaphoreType.DMA((10,))],
        compiler_params=pltpu.CompilerParams(vmem_limit_bytes=10 << 20),
        cost_estimate=pl.CostEstimate(flops=0, bytes_accessed=8 << 20, transcendentals=0),
        name="prepare",
    )(*[pltpu.with_memory_space_constraint(v, pltpu.HBM) for v in big + vecs])


def cut_kernel(nc, axis, volume, *rest):
    outs, sems = rest[:nc], rest[nc]
    lanes = outs[0].shape[2]
    ci = lax.axis_index(axis)
    copies = []
    for k in range(nc):
        start = pl.multiple_of(lax.rem(ci + k, nc) * lanes, lanes)
        copies.append(
            pltpu.make_async_copy(volume.at[:, :, pl.ds(start, lanes)], outs[k], sems.at[k])
        )
    for c in copies:
        c.start()
    for c in copies:
        c.wait()


def cut(nc, volume):
    rows, cols, lanes = volume.shape
    return pl.pallas_call(
        functools.partial(cut_kernel, nc, "cols"),
        out_shape=[jax.ShapeDtypeStruct((rows, cols, lanes // nc), BF16)] * nc,
        in_specs=[pl.BlockSpec(memory_space=pltpu.HBM)],
        out_specs=[vmem()] * nc,
        scratch_shapes=[pltpu.SemaphoreType.DMA((nc,))],
        compiler_params=pltpu.CompilerParams(vmem_limit_bytes=2 << 20),
        name="cut",
    )(pltpu.with_memory_space_constraint(volume, pltpu.HBM))


def pack_kernel(nc, halo, chunks, *refs):
    pieces, outs = refs[:nc], refs[nc:]
    rows = pieces[0].shape[0]
    lanes = pieces[0].shape[2] // chunks
    even = lax.rem(lax.axis_index("rows") + 1, 2)
    for n in range(chunks):
        for i, far in enumerate((even, 1 - even)):
            top = far * (rows - halo)
            for r in range(halo):
                for k in range(nc):
                    outs[2 * n + i][r, k] = pieces[k][top + r, :, n * lanes : (n + 1) * lanes]


def pack(nc, halo, chunks, pieces):
    _, cols, lanes = pieces[0].shape
    return pl.pallas_call(
        functools.partial(pack_kernel, nc, halo, chunks),
        out_shape=[jax.ShapeDtypeStruct((halo, nc, cols, lanes // chunks), BF16)] * (2 * chunks),
        in_specs=[vmem()] * nc,
        out_specs=[vmem()] * (2 * chunks),
        compiler_params=pltpu.CompilerParams(vmem_limit_bytes=3 << 20),
        name="pack",
    )(*pieces)


def planar_kernel(nd, nc, chunk, *refs):
    pieces = refs[:nc]
    halo_a, halo_b, weights, bias = refs[nc : nc + 4]
    outs = refs[nc + 4 : nc + 4 + nd * nc]
    flat, x1, *xs, last, back = refs[nc + 4 + nd * nc :]
    rows, own = pieces[0].shape[:2]
    halo, lanes = halo_a.shape[0], halo_a.shape[3]
    layers = bias.shape[0]
    cols = own * nc
    tiles = lanes // 128
    pitch = cols + 8
    ch = 64
    total = rows + 2 * halo
    xi, ci, zi = [lax.axis_index(n) for n in ("disp", "cols", "rows")]
    nz = lax.axis_size("rows")
    even = lax.rem(zi + 1, 2)
    at_a = even * (halo + rows)
    at_b = (1 - even) * (halo + rows)
    bases = [lax.rem(ci + m, nc) * own for m in range(nc)]

    def put(r, m, value):
        for t in range(tiles):
            at = pl.ds(pl.multiple_of(t * pitch + bases[m], 8), own)
            flat[r, at, :] = value[:, t * 128 : (t + 1) * 128].astype(F32)

    def put_own(r, carry):
        for m in range(nc):
            put(halo + r, m, pieces[m][r, :, chunk * lanes : (chunk + 1) * lanes])
        return carry

    def put_halo(r, carry):
        for m in range(nc):
            put(at_a + r, m, halo_a[r, m])
            put(at_b + r, m, halo_b[r, m])
        return carry

    lax.fori_loop(0, rows, put_own, 0)
    lax.fori_loop(0, halo, put_halo, 0)
    low = lax.broadcasted_iota(jnp.int32, (tiles, 128), 1) < ch
    stages = [x1] + xs
    for x in stages:
        x[0] = jnp.zeros(x.shape[1:], BF16)
        x[cols + 1] = jnp.zeros(x.shape[1:], BF16)

    def turn(c, carry):
        at = pl.ds(c, tiles, stride=pitch)
        for p in range(total // 2):
            a, b = flat[2 * p, at, :], flat[2 * p + 1, at, :]
            e = jnp.where(low, a, pltpu.roll(b, ch, 1))
            o = jnp.where(low, pltpu.roll(a, ch, 1), b)
            x1[c + 1, :, p * 128 : (p + 1) * 128] = jnp.concatenate([e, o], axis=0).astype(BF16)
        return carry

    lax.fori_loop(0, cols, turn, 0, unroll=8)
    block = max(1, 512 // (2 * tiles))
    while cols % block:
        block -= 1
    size = block * 2 * tiles
    row_of = lax.broadcasted_iota(jnp.int32, (1, 256), 1) // ch
    for layer in range(layers):
        height = total - 2 * (layer + 1)
        beyond = layers - 1 - layer
        src = stages[layer]
        for q in range(0, height // 2, 2):
            single = q + 1 == height // 2
            span = 128 * (2 if single else 3)
            width = 128 if single else 256
            row = row_of[:, :width] + 2 * q
            keep = jnp.ones((1, width), F32)
            keep = jnp.where((row < beyond) & (zi == 0), 0.0, keep)
            keep = jnp.where((row >= height - beyond) & (zi == nz - 1), 0.0, keep)

            def run(i, carry):
                c0 = i * block
                lhs = jnp.concatenate(
                    [
                        src[pl.ds(c0 + j, block), :, q * 128 : q * 128 + span].reshape(size, span)
                        for j in range(3)
                    ],
                    axis=1,
                )
                if single:
                    rhs = jnp.concatenate(
                        [weights[layer, j * 384 : j * 384 + span, :width] for j in range(3)], axis=0
                    )
                else:
                    rhs = weights[layer]
                y = silu(dot(lhs, rhs) + bias[layer : layer + 1, :width])
                if layer < layers - 1:
                    y = (y * keep).astype(BF16).reshape(block, 2 * tiles, width)
                    stages[layer + 1][pl.ds(c0 + 1, block), :, q * 128 : q * 128 + width] = y
                else:
                    y = y.reshape(block, 2 * tiles, width)
                    last[pl.ds(c0, block), :, q * 128 : q * 128 + width] = y
                return carry

            lax.fori_loop(0, cols // block, run, 0)

    def turn_back(c, carry):
        at = pl.ds(c, tiles, stride=pitch)
        for p in range(rows // 2):
            e = last[c, :tiles, p * 128 : (p + 1) * 128]
            o = last[c, tiles:, p * 128 : (p + 1) * 128]
            back[2 * p, at, :] = jnp.where(low, e, pltpu.roll(o, ch, 1))
            back[2 * p + 1, at, :] = jnp.where(low, pltpu.roll(e, ch, 1), o)
        return carry

    lax.fori_loop(0, cols, turn_back, 0, unroll=8)
    part = rows // nd
    for a in range(nd):
        top = lax.rem(xi + a, nd) * part
        for r in range(part):
            for m in range(nc):
                for t in range(tiles):
                    at = pl.ds(pl.multiple_of(t * pitch + bases[m], 8), own)
                    outs[a * nc + m][r * own : (r + 1) * own, t * 128 : (t + 1) * 128] = back[
                        top + r, at, :
                    ].astype(BF16)


def planar(nd, nc, chunk, pieces, halo_a, halo_b, weights, bias):
    rows, own = pieces[0].shape[:2]
    lanes = halo_a.shape[3]
    layers = bias.shape[0]
    halo = halo_a.shape[0]
    cols = own * nc
    tiles = lanes // 128
    pitch = cols + 8
    total = rows + 2 * halo
    pixels = rows * cols // (nd * nc)
    scratch = [pltpu.VMEM((total, tiles * pitch, 128), F32)]
    scratch += [
        pltpu.VMEM((cols + 2, 2 * tiles, (total // 2 - k) * 128), BF16) for k in range(layers)
    ]
    scratch += [
        pltpu.VMEM((cols, 2 * tiles, rows * 64), F32),
        pltpu.VMEM((rows, tiles * pitch, 128), F32),
    ]
    return pl.pallas_call(
        functools.partial(planar_kernel, nd, nc, chunk),
        out_shape=[jax.ShapeDtypeStruct((pixels, lanes), BF16)] * (nd * nc),
        in_specs=[vmem()] * (nc + 4),
        out_specs=[vmem()] * (nd * nc),
        scratch_shapes=scratch,
        compiler_params=pltpu.CompilerParams(vmem_limit_bytes=16 << 20),
        cost_estimate=pl.CostEstimate(
            flops=36 * lanes * cols * total * 256, bytes_accessed=4 << 20, transcendentals=0
        ),
        name="planar",
    )(*pieces, halo_a, halo_b, weights, bias)


def disparity_kernel(
    nd,
    nc,
    heads,
    chunks,
    half,
    *refs,
):
    count = chunks * nd * nc
    pieces = refs[:count]
    band, bias, ends, w_qe, w_qo, w_k, w_v, w_out, w_gate, mean_mat = refs[count : count + 10]
    outs = refs[count + 10 : count + 10 + nd]
    xs, ys, sf, nrm, qe, qo, kk, vv, mix, sec, soft = refs[count + 10 + nd :]
    gain, gate_off = ends[0:1], ends[1:2]
    q_scale = jnp.concatenate([ends[2:3]] * 2, axis=1)
    pixels, lanes = outs[0].shape[0], pieces[0].shape[1]
    wide = band.shape[2]
    per_piece = lanes // wide
    groups = per_piece * count
    spans = band.shape[1]
    pad = spans // 2
    ch = wide // PACK
    per_head = ch // heads
    pairs = pixels // 2
    pitch = pixels + 8
    xi, ci = lax.axis_index("disp"), lax.axis_index("cols")

    for side in range(pad):
        xs[side] = jnp.zeros((pixels, wide), BF16)
        xs[pad + groups + side] = jnp.zeros((pixels, wide), BF16)
        ys[side] = jnp.zeros((pixels, wide), BF16)
        ys[pad + groups + side] = jnp.zeros((pixels, wide), BF16)
    for a in range(nd):
        for k in range(nc):
            src_x = lax.rem(xi - a + nd, nd)
            src_c = lax.rem(ci - k + nc, nc)
            for n in range(chunks):
                at = pad + ((src_x * nc + src_c) * chunks + n) * per_piece
                piece = pieces[(n * nd + a) * nc + k]
                for g in range(per_piece):
                    xs[at + g] = piece[
                        half * pixels : (half + 1) * pixels, g * wide : (g + 1) * wide
                    ]

    step = math.gcd(groups, 512 // pixels)

    def conv(src, s, g0):
        acc = None
        for j in range(spans):
            lhs = src[pl.ds(g0 + j, step)].reshape(step * pixels, wide)
            part = dot(lhs, band[s, j])
            acc = part if acc is None else acc + part
        return acc + bias[s : s + 1]

    def first(i, carry):
        g0 = i * step
        y = silu(conv(xs, 0, g0)).astype(BF16)
        ys[pl.ds(pad + g0, step)] = y.reshape(step, pixels, wide)
        return carry

    lax.fori_loop(0, groups // step, first, 0)

    def second(i, carry):
        g0 = i * step
        y = conv(ys, 1, g0).astype(BF16).astype(F32)
        for i in range(step):
            at = pl.ds(pl.multiple_of((g0 + i) * pitch, 8), pixels)
            for b in range(wide // 128):
                sf[b, at, :] = y[i * pixels : (i + 1) * pixels, b * 128 : (b + 1) * 128]
        return carry

    lax.fori_loop(0, groups // step, second, 0)

    def gather(p, carry):
        at = pl.ds(pl.multiple_of(p * groups, groups), groups)
        for q in range(2):
            for b in range(wide // 128):
                piece = sf[b, pl.ds(2 * p + q, groups, stride=pitch), :]
                sec[q, at, b * 128 : (b + 1) * 128] = piece
        return carry

    lax.fori_loop(0, pairs, gather, 0)

    for q in range(2):
        s = sec[q]
        sq = s * s
        hi = sq.astype(BF16)
        lo = (sq - hi.astype(F32)).astype(BF16)
        mean = dot(hi, mean_mat[...]) + dot(lo, mean_mat[...])
        nrm[q] = (s * lax.rsqrt(mean + 1e-05) * gain).astype(BF16)
    qe[...] = (dot(nrm[0], w_qe[...]) * q_scale).astype(BF16)
    qo[...] = (dot(nrm[1], w_qo[...]) * q_scale).astype(BF16)
    kk[...] = (dot(nrm[0], w_k[0]) + dot(nrm[1], w_k[1])).astype(BF16)
    vv[...] = (dot(nrm[0], w_v[0]) + dot(nrm[1], w_v[1])).astype(BF16)

    keys = PACK * groups
    lane = lax.broadcasted_iota(jnp.int32, (keys, 2 * ch), 1)
    head_of = lax.rem(lane, ch) // per_head
    ones_row = lax.broadcasted_iota(jnp.int32, (16, keys * heads), 0)
    ones_col = lax.broadcasted_iota(jnp.int32, (16, keys * heads), 1)
    ones = jnp.where(ones_row == ones_col // keys, 1.0, 0.0).astype(BF16)

    def stack(ref, at):
        return jnp.concatenate(
            [ref[at, u * 2 * ch : (u + 1) * 2 * ch] for u in range(PACK)], axis=0
        )

    def score(p, carry):
        at = pl.ds(pl.multiple_of(p * groups, groups), groups)
        queries = jnp.concatenate([stack(qe, at), stack(qo, at)], axis=0)
        key = stack(kk, at)
        zero = jnp.zeros_like(key)
        for h in range(heads):
            part = dot_nt(jnp.where(head_of == h, key, zero), queries)
            top = jnp.max(part, axis=0, keepdims=True)
            soft[p, h * keys : (h + 1) * keys] = jnp.exp2(part - top).astype(BF16)
        return carry

    blank = jnp.zeros((per_head, keys), BF16)

    def mixing(p, carry):
        at = pl.ds(pl.multiple_of(p * groups, groups), groups)
        value_t = stack(vv, at).astype(F32).T.astype(BF16)
        rows = []
        for q in range(2):
            for h in range(heads):
                base = q * ch + h * per_head
                rows.append(
                    jnp.concatenate(
                        [
                            value_t[base : base + per_head] if m == h else blank
                            for m in range(heads)
                        ],
                        axis=1,
                    )
                )
        rows.append(ones)
        summed = dot(jnp.concatenate(rows, axis=0), soft[p])
        inv = 1.0 / summed[2 * ch : 2 * ch + heads]
        blocks = []
        for q in range(2):
            cols = slice(q * keys, (q + 1) * keys)
            for h in range(heads):
                base = q * ch + h * per_head
                blocks.append(
                    summed[base : base + per_head, cols] * inv[h : h + 1, cols]
                )
        mixed = jnp.concatenate(blocks, axis=0).T
        for u in range(PACK):
            mix[at, u * 2 * ch : (u + 1) * 2 * ch] = mixed[
                u * groups : (u + 1) * groups
            ].astype(BF16)
        return carry

    lax.fori_loop(0, pairs, score, 0, unroll=min(pairs, 8))
    lax.fori_loop(0, pairs, mixing, 0, unroll=min(pairs, 8))

    for q in range(2):
        attended = sec[q] + dot(mix[...], w_out[q])
        logits = dot(attended.astype(BF16), w_gate[...]) + gate_off
        sec[q] = sigmoid(logits)

    def scatter(p, carry):
        at = pl.ds(pl.multiple_of(p * groups, groups), groups)
        for q in range(2):
            for b in range(wide // 128):
                sf[b, pl.ds(2 * p + q, groups, stride=pitch), :] = sec[
                    q, at, b * 128 : (b + 1) * 128
                ]
        return carry

    lax.fori_loop(0, pairs, scatter, 0)
    slab = groups // nd
    for a in range(nd):
        g0 = lax.rem(xi + a, nd) * slab
        for g in range(slab):
            row = pl.ds(pl.multiple_of((g0 + g) * pitch, 8), pixels)
            for b in range(wide // 128):
                at = g * wide + b * 128
                outs[a][:, at : at + 128] = sf[b, row, :].astype(BF16)


def disparity(nd, nc, heads, chunks, half, halves, pieces, weights):
    pixels, lanes = pieces[0].shape
    pixels //= halves
    band = weights[0]
    wide = band.shape[2]
    groups = lanes * nd * nc * chunks // wide
    pad = band.shape[1] // 2
    pairs = pixels // 2
    scratch = [
        pltpu.VMEM((groups + 2 * pad, pixels, wide), BF16),
        pltpu.VMEM((groups + 2 * pad, pixels, wide), BF16),
        pltpu.VMEM((wide // 128, groups * (pixels + 8), 128), F32),
        pltpu.VMEM((2, pairs * groups, wide), BF16),
        pltpu.VMEM((pairs * groups, 2 * wide), BF16),
        pltpu.VMEM((pairs * groups, 2 * wide), BF16),
        pltpu.VMEM((pairs * groups, 2 * wide), BF16),
        pltpu.VMEM((pairs * groups, 2 * wide), BF16),
        pltpu.VMEM((pairs * groups, 2 * wide), BF16),
        pltpu.VMEM((2, pairs * groups, wide), F32),
        pltpu.VMEM((pairs, heads * PACK * groups, 2 * PACK * groups), BF16),
    ]
    return pl.pallas_call(
        functools.partial(disparity_kernel, nd, nc, heads, chunks, half),
        out_shape=[jax.ShapeDtypeStruct((pixels, groups * wide // nd), BF16)] * nd,
        in_specs=[vmem()] * (len(pieces) + 10),
        out_specs=[vmem()] * nd,
        scratch_shapes=scratch,
        compiler_params=pltpu.CompilerParams(vmem_limit_bytes=18 << 20),
        cost_estimate=pl.CostEstimate(
            flops=pixels * 340_000_000, bytes_accessed=4 << 20, transcendentals=0
        ),
        name="disparity",
    )(*pieces, *weights)


def gate_kernel(nd, halves, volume, *refs):
    gates, out = refs[: nd * halves], refs[nd * halves]
    rows, cols, _ = volume.shape
    part = rows // nd
    own = part // halves
    for h in range(halves):
        for a in range(nd):
            top = lax.rem(lax.axis_index("disp") - a + nd, nd) * part + h * own
            for r in range(own):
                g = gates[h * nd + a][r * cols : (r + 1) * cols]
                v = volume[top + r].astype(F32) * g.astype(F32)
                out[top + r] = v.astype(BF16)


def gate(nd, halves, volume, gates):
    return pl.pallas_call(
        functools.partial(gate_kernel, nd, halves),
        out_shape=jax.ShapeDtypeStruct(volume.shape, volume.dtype),
        in_specs=[vmem()] * (1 + nd * halves),
        out_specs=vmem(),
        compiler_params=pltpu.CompilerParams(vmem_limit_bytes=3 << 20),
        name="gate",
    )(volume, *gates)


def shift_pairs(sizes, moves):
    out = []
    count = math.prod(sizes)
    for flat in range(count):
        rest, place = flat, []
        for size in reversed(sizes):
            place.append(rest % size)
            rest //= size
        place = place[::-1]
        target = 0
        for at, move, size in zip(place, moves, sizes):
            target = target * size + (at + move) % size
        out.append((flat, target))
    return out


def per_device(
    volume,
    planar_taps,
    planar_bias,
    shift_taps,
    shift_bias,
    norm_gain,
    qkv,
    exit_proj,
    head_scale,
    gate_proj,
    gate_bias,
):
    layers = planar_bias.shape[0]
    heads = head_scale.shape[0]
    nz, nd, nc = [lax.axis_size(a) for a in ("rows", "disp", "cols")]

    shares = [
        lax.ppermute(v, "cols", shift_pairs((nc,), (k,))) if k else v
        for k, v in enumerate(cut(nc, volume))
    ]
    mine = [shares[0]] + shares[:0:-1]
    lanes = mine[0].shape[2]
    chunks = 2 if lanes % (2 * WIDE) == 0 else 1
    sends = pack(nc, layers, chunks, mine)
    pairs_a = [(z, z + 1) for z in range(0, nz - 1, 2)]
    pairs_b = [(z, z + 1) for z in range(1, nz - 1, 2)]
    both = [ps + [(j, i) for i, j in ps] for ps in (pairs_a, pairs_b)]
    halos = []
    for i, v in enumerate(sends):
        halos.append(lax.ppermute(v, "rows", both[i % 2]))

    made = prepare(
        planar_taps,
        planar_bias,
        shift_taps,
        shift_bias,
        norm_gain,
        qkv,
        exit_proj,
        head_scale,
        gate_proj,
        gate_bias,
    )
    rows_w, band, w_qe, w_qo, w_k, w_v, w_out, w_gate, mean_mat, plane_b, shift_b, ends = made
    got = []
    for n in range(chunks):
        pieces = planar(nd, nc, n, mine, halos[2 * n], halos[2 * n + 1], rows_w, plane_b)
        for a in range(nd):
            for k in range(nc):
                piece = pieces[a * nc + k]
                if a or k:
                    piece = lax.ppermute(piece, ("disp", "cols"), shift_pairs((nd, nc), (a, k)))
                got.append(piece)
    pixels = got[0].shape[0]
    halves = 2 if pixels % 32 == 0 else 1
    weights = [band, shift_b, ends, w_qe, w_qo, w_k, w_v, w_out, w_gate, mean_mat]
    gates = []
    for h in range(halves):
        parts = disparity(nd, nc, heads, chunks, h, halves, got, weights)
        for a, g in enumerate(parts):
            if a:
                g = lax.ppermute(g, "disp", shift_pairs((nd,), (a,)))
            gates.append(g)
    return gate(nd, halves, volume, gates)


def solution(mesh):
    spec = P(("groups", "rows"), "cols", "disp")

    return jax.shard_map(
        per_device, mesh=mesh, in_specs=(spec,) + (P(),) * 10, out_specs=spec, check_vma=False
    )
```

```python
import functools
import math

import jax
import jax.numpy as jnp
from jax import lax
from jax.experimental import pallas as pl
from jax.experimental.pallas import tpu as pltpu
from jax.sharding import PartitionSpec as P


F32 = jnp.float32
BF16 = jnp.bfloat16
SPLIT = 2
PACK = 4
WIDE = 256


def vmem():
    return pl.BlockSpec(memory_space=pltpu.VMEM)


def silu(v):
    half = 0.5 * v
    return half + half * jnp.tanh(half)


def sigmoid(v):
    return 0.5 + 0.5 * jnp.tanh(0.5 * v)


def dot(a, b):
    return jnp.dot(a, b, preferred_element_type=F32)


def dot_nt(a, b):
    return lax.dot_general(a, b, (((1,), (1,)), ((), ())), preferred_element_type=F32)


def prepare_kernel(heads, taps3, taps17, qkv, exit_proj, gate_proj, vecs, *rest):
    outs, (t3, t17, wq, we, wg, vec, sems) = rest[:12], rest[12:]
    copies = [
        pltpu.make_async_copy(src, dst, sems.at[i])
        for i, (src, dst) in enumerate(
            [(taps3, t3), (taps17, t17), (qkv, wq), (exit_proj, we), (gate_proj, wg)]
        )
    ]
    for i, v in enumerate(vecs):
        copies.append(pltpu.make_async_copy(v, vec[i], sems.at[5 + i]))
    for c in copies:
        c.start()
    rows_w, band, w_qe, w_qo, w_k, w_v, w_out, w_gate, mean_mat, plane_b, shift_b, ends = outs
    layers = rows_w.shape[0]
    ch = we.shape[0]
    spans = band.shape[1]
    taps = t17.shape[1]
    zero = jnp.zeros((ch, ch), BF16)
    none = jnp.zeros((ch, 2 * ch), BF16)
    for ref in (w_qe, w_qo, w_k, w_v, w_out, w_gate):
        ref[...] = jnp.zeros_like(ref)
    r = lax.broadcasted_iota(jnp.int32, mean_mat.shape, 0) // ch
    c = lax.broadcasted_iota(jnp.int32, mean_mat.shape, 1) // ch
    mean_mat[...] = jnp.where(r == c, 1.0 / ch, 0.0).astype(BF16)
    for c in copies:
        c.wait()

    def pair(x, y):
        return jnp.concatenate([x, y], axis=1)

    def planar_block(layer, carry):
        for j in range(3):
            tap = [t3[layer * 9 + i * 3 + j] for i in range(3)] + [zero]
            for rr in range(6):
                top = (j * 6 + rr) * ch
                for b in range(2):
                    t = rr - 2 * b
                    block = none
                    if 0 <= t <= 3:
                        block = pair(tap[t], tap[t - 1] if t else zero)
                    rows_w[layer, top : top + ch, b * 2 * ch : (b + 1) * 2 * ch] = block
        return carry

    lax.fori_loop(0, layers, planar_block, 0)

    def band_block(s, carry):
        table = []
        for t in range(taps + 1):
            table.append(
                pair(t17[s, t] if t < taps else zero, t17[s, t - 1] if t else zero)
            )
        for j in range(spans):
            for u in range(PACK):
                for b in range(PACK // 2):
                    t = PACK * (j - spans // 2) + u - 2 * b + taps // 2
                    block = table[t] if 0 <= t <= taps else none
                    band[s, j, u * ch : (u + 1) * ch, 2 * b * ch : 2 * (b + 1) * ch] = block
        return carry

    lax.fori_loop(0, 2, band_block, 0)
    w = wq[...]
    parts = [w[:, i * ch : (i + 1) * ch] for i in range(3)]
    lo = [pair(p, zero) for p in parts]
    hi = [pair(zero, p) for p in parts]
    out_lo, out_hi = pair(we[...], zero), pair(zero, we[...])
    gate_lo, gate_hi = pair(wg[...], zero), pair(zero, wg[...])
    for u in range(PACK):
        rows = slice(u * ch, (u + 1) * ch)
        lanes = slice(u * 2 * ch, (u + 1) * 2 * ch)
        w_qe[rows, lanes] = lo[0]
        w_qo[rows, lanes] = hi[0]
        w_k[0, rows, lanes] = lo[1]
        w_k[1, rows, lanes] = hi[1]
        w_v[0, rows, lanes] = lo[2]
        w_v[1, rows, lanes] = hi[2]
        tile = slice((u // 2) * 2 * ch, (u // 2 + 1) * 2 * ch)
        for q in range(2):
            at = u * 2 * ch + q * ch
            w_out[q, at : at + ch, tile] = out_hi if u % 2 else out_lo
        w_gate[rows, tile] = gate_hi if u % 2 else gate_lo

    def tiled(v):
        return jnp.concatenate([v] * PACK, axis=1)

    plane_b[...] = tiled(vec[0][...])
    shift_b[...] = tiled(vec[1][...])
    ends[0:1] = tiled(vec[2][...])
    ends[1:2] = tiled(vec[3][...])
    head = lax.rem(lax.broadcasted_iota(jnp.int32, (1, PACK * ch), 1), ch) // (ch // heads)
    row = jnp.zeros((1, PACK * ch), F32)
    for h in range(heads):
        row = jnp.where(head == h, vec[4][:, h : h + 1], row)
    ends[2:3] = row * (math.log2(math.e) / math.sqrt(ch // heads))


def prepare(planar_taps, planar_bias, shift_taps, shift_bias, gain, qkv, exit_proj, head_scale, gate_proj, gate_bias):
    layers, ch = planar_bias.shape
    taps = shift_taps.shape[1]
    heads = head_scale.shape[0]
    spans = 2 * (-(-(taps // 2) // PACK)) + 1
    size = PACK * ch
    sds = jax.ShapeDtypeStruct
    outs = [
        sds((layers, 18 * ch, size), BF16),
        sds((2, spans, size, size), BF16),
        sds((size, 2 * size), BF16),
        sds((size, 2 * size), BF16),
        sds((2, size, 2 * size), BF16),
        sds((2, size, 2 * size), BF16),
        sds((2, 2 * size, size), BF16),
        sds((size, size), BF16),
        sds((size, size), BF16),
        sds((layers, size), F32),
        sds((2, size), F32),
        sds((3, size), F32),
    ]
    anywhere = pl.BlockSpec(memory_space=pltpu.HBM)
    vecs = [planar_bias, shift_bias, gain[None], gate_bias[None], head_scale[None]]
    big = [planar_taps.reshape(layers * 9, ch, ch), shift_taps, qkv, exit_proj, gate_proj]

    def body(*refs):
        prepare_kernel(heads, *refs[:5], refs[5:10], *refs[10:22], *refs[22:27], refs[27:32], refs[32])

    return pl.pallas_call(
        body,
        out_shape=outs,
        in_specs=[anywhere] * 10,
        out_specs=[vmem()] * 12,
        scratch_shapes=[pltpu.VMEM(v.shape, v.dtype) for v in big + vecs]
        + [pltpu.SemaphoreType.DMA((10,))],
        compiler_params=pltpu.CompilerParams(vmem_limit_bytes=10 << 20),
        cost_estimate=pl.CostEstimate(flops=0, bytes_accessed=8 << 20, transcendentals=0),
        name="prepare",
    )(*[pltpu.with_memory_space_constraint(v, pltpu.HBM) for v in big + vecs])


def cut_kernel(halo, chunk, volume, *rest):
    outs, sems = rest[:-1], rest[-1]
    rows = volume.shape[0]
    lanes = outs[0].shape[2]
    even = lax.rem(lax.axis_index("rows") + 1, 2)
    copies = []
    for i, far in enumerate((even, 1 - even)):
        at = slice(chunk * lanes, (chunk + 1) * lanes)
        part = volume.at[pl.ds(far * (rows - halo), halo), :, at]
        copies.append(pltpu.make_async_copy(part, outs[i], sems.at[i]))
    if len(outs) > 2:
        copies.append(pltpu.make_async_copy(volume, outs[2], sems.at[2]))
    for c in copies:
        c.start()
    for c in copies:
        c.wait()


def cut(halo, chunks, chunk, volume):
    _, cols, lanes = volume.shape
    outs = [jax.ShapeDtypeStruct((halo, cols, lanes // chunks), BF16)] * 2
    if chunk == chunks - 1:
        outs.append(jax.ShapeDtypeStruct(volume.shape, BF16))
    return pl.pallas_call(
        functools.partial(cut_kernel, halo, chunk),
        out_shape=outs,
        in_specs=[pl.BlockSpec(memory_space=pltpu.HBM)],
        out_specs=[vmem()] * len(outs),
        scratch_shapes=[pltpu.SemaphoreType.DMA((len(outs),))],
        compiler_params=pltpu.CompilerParams(vmem_limit_bytes=3 << 20),
        name="cut",
    )(pltpu.with_memory_space_constraint(volume, pltpu.HBM))


def edge_kernel(chunk, mine, halo_a, halo_b, out):
    rows = mine.shape[0]
    halo, lanes = halo_a.shape[0], halo_a.shape[2]
    width = out.shape[1]
    even = lax.rem(lax.axis_index("rows") + 1, 2)
    first = lax.axis_index("cols") == 0
    at_a = even * (halo + rows)
    at_b = (1 - even) * (halo + rows)
    last = mine.shape[1] - width

    def take(v):
        v = v.astype(F32)
        return jnp.where(first, v[last:], v[:width]).astype(BF16)

    for r in range(rows):
        out[halo + r] = take(mine[r, :, chunk * lanes : (chunk + 1) * lanes])
    for r in range(halo):
        out[at_a + r] = take(halo_a[r])
        out[at_b + r] = take(halo_b[r])


def edge(chunk, mine, halo_a, halo_b):
    halo, cols, lanes = halo_a.shape
    total = mine.shape[0] + 2 * halo
    return pl.pallas_call(
        functools.partial(edge_kernel, chunk),
        out_shape=jax.ShapeDtypeStruct((total, min(8, cols), lanes), BF16),
        in_specs=[vmem()] * 3,
        out_specs=vmem(),
        compiler_params=pltpu.CompilerParams(vmem_limit_bytes=3 << 20),
        name="edge",
    )(mine, halo_a, halo_b)


def planar_kernel(nd, nc, chunk, *refs):
    mine, halo_a, halo_b, side, weights, bias = refs[:6]
    outs = refs[6 : 6 + nd]
    flat, x1, *xs, last, back = refs[6 + nd :]
    rows, own = mine.shape[:2]
    halo, lanes = halo_a.shape[0], halo_a.shape[2]
    layers = bias.shape[0]
    width = side.shape[1]
    tiles = lanes // 128
    pitch = own + 8
    ch = 64
    total = rows + 2 * halo
    xi, zi = [lax.axis_index(n) for n in ("disp", "rows")]
    ci = lax.axis_index("cols") if nc > 1 else 0
    more = layers if nc > 1 else 0
    nz = lax.axis_size("rows")
    even = lax.rem(zi + 1, 2)
    at_a = even * (halo + rows)
    at_b = (1 - even) * (halo + rows)

    def put(r, base, value):
        for t in range(tiles):
            at = t * pitch + base
            flat[r, at : at + value.shape[0], :] = value[:, t * 128 : (t + 1) * 128].astype(F32)

    def put_own(r, carry):
        put(halo + r, 0, mine[r, :, chunk * lanes : (chunk + 1) * lanes])
        return carry

    def put_halo(r, carry):
        put(at_a + r, 0, halo_a[r])
        put(at_b + r, 0, halo_b[r])
        return carry

    def put_side(r, carry):
        put(r, own, side[r])
        return carry

    lax.fori_loop(0, rows, put_own, 0)
    lax.fori_loop(0, halo, put_halo, 0)
    if more:
        lax.fori_loop(0, total, put_side, 0)
    low = lax.broadcasted_iota(jnp.int32, (tiles, 128), 1) < ch
    stages = [x1] + xs
    for x in stages:
        x[0] = jnp.zeros(x.shape[1:], BF16)
        x[x.shape[0] - 1] = jnp.zeros(x.shape[1:], BF16)

    def turn(source, target):
        at = pl.ds(source, tiles, stride=pitch)
        for p in range(total // 2):
            a, b = flat[2 * p, at, :], flat[2 * p + 1, at, :]
            e = jnp.where(low, a, pltpu.roll(b, ch, 1))
            o = jnp.where(low, pltpu.roll(a, ch, 1), b)
            x1[target + 1, :, p * 128 : (p + 1) * 128] = jnp.concatenate([e, o], axis=0).astype(BF16)

    def turn_own(c, carry):
        turn(c, more * ci + c)
        return carry

    lax.fori_loop(0, own, turn_own, 0, unroll=16)
    for c in range(more):
        turn(own + c + (width - more) * ci, own * (1 - ci) + c)
    row_of = lax.broadcasted_iota(jnp.int32, (1, 256), 1) // ch
    for layer in range(layers):
        height = total - 2 * (layer + 1)
        beyond = layers - 1 - layer
        src = stages[layer]
        count = own + max(more - 1 - layer, 0)
        block = -(-count // SPLIT)
        shift = ci if more else 0
        for q in range(0, height // 2, 2):
            single = q + 1 == height // 2
            span = 128 * (2 if single else 3)
            wide = 128 if single else 256
            row = row_of[:, :wide] + 2 * q
            keep = jnp.ones((1, wide), F32)
            keep = jnp.where((row < beyond) & (zi == 0), 0.0, keep)
            keep = jnp.where((row >= height - beyond) & (zi == nz - 1), 0.0, keep)

            for c0 in [min(i, count - block) for i in range(0, count, block)]:
                lhs = jnp.concatenate(
                    [
                        src[pl.ds(c0 + shift + j, block), :, q * 128 : q * 128 + span].reshape(
                            block * 2 * tiles, span
                        )
                        for j in range(3)
                    ],
                    axis=1,
                )
                if single:
                    rhs = jnp.concatenate(
                        [weights[layer, j * 384 : j * 384 + span, :wide] for j in range(3)], axis=0
                    )
                else:
                    rhs = weights[layer]
                y = silu(dot(lhs, rhs) + bias[layer : layer + 1, :wide])
                if layer < layers - 1:
                    y = (y * keep).astype(BF16).reshape(block, 2 * tiles, wide)
                    stages[layer + 1][c0 + 1 : c0 + 1 + block, :, q * 128 : q * 128 + wide] = y
                else:
                    y = y.reshape(block, 2 * tiles, wide)
                    last[c0 : c0 + block, :, q * 128 : q * 128 + wide] = y

    def turn_back(c, carry):
        at = pl.ds(c, tiles, stride=pitch)
        for p in range(rows // 2):
            e = last[c, :tiles, p * 128 : (p + 1) * 128]
            o = last[c, tiles:, p * 128 : (p + 1) * 128]
            back[2 * p, at, :] = jnp.where(low, e, pltpu.roll(o, ch, 1))
            back[2 * p + 1, at, :] = jnp.where(low, pltpu.roll(e, ch, 1), o)
        return carry

    lax.fori_loop(0, own, turn_back, 0, unroll=16)
    part = rows // nd
    for a in range(nd):
        top = lax.rem(xi + a, nd) * part
        for r in range(part):
            for t in range(tiles):
                outs[a][r * own : (r + 1) * own, t * 128 : (t + 1) * 128] = back[
                    top + r, t * pitch : t * pitch + own, :
                ].astype(BF16)


def planar(nd, nc, chunk, mine, halo_a, halo_b, side, weights, bias):
    rows, own = mine.shape[:2]
    halo, lanes = halo_a.shape[0], halo_a.shape[2]
    layers = bias.shape[0]
    tiles = lanes // 128
    total = rows + 2 * halo
    more = layers if nc > 1 else 0
    scratch = [pltpu.VMEM((total, tiles * (own + 8), 128), F32)]
    scratch += [
        pltpu.VMEM((own + max(more - k, 0) + 2, 2 * tiles, (total // 2 - k) * 128), BF16)
        for k in range(layers)
    ]
    scratch += [
        pltpu.VMEM((own, 2 * tiles, rows * 64), F32),
        pltpu.VMEM((rows, tiles * (own + 8), 128), F32),
    ]
    return pl.pallas_call(
        functools.partial(planar_kernel, nd, nc, chunk),
        out_shape=[jax.ShapeDtypeStruct((rows * own // nd, lanes), BF16)] * nd,
        in_specs=[vmem()] * 6,
        out_specs=[vmem()] * nd,
        scratch_shapes=scratch,
        compiler_params=pltpu.CompilerParams(vmem_limit_bytes=18 << 20),
        cost_estimate=pl.CostEstimate(
            flops=36 * lanes * 2 * own * total * 256, bytes_accessed=4 << 20, transcendentals=0
        ),
        name="planar",
    )(mine, halo_a, halo_b, side, weights, bias)


def disparity_kernel(
    nd,
    nc,
    heads,
    chunks,
    half,
    *refs,
):
    count = chunks * nd * nc
    pieces = refs[:count]
    band, bias, ends, w_qe, w_qo, w_k, w_v, w_out, w_gate, mean_mat = refs[count : count + 10]
    outs = refs[count + 10 : count + 10 + nd]
    xs, ys, sf, nrm, qe, qo, kk, vv, mix, sec, soft = refs[count + 10 + nd :]
    gain, gate_off = ends[0:1], ends[1:2]
    q_scale = jnp.concatenate([ends[2:3]] * 2, axis=1)
    pixels, lanes = outs[0].shape[0], pieces[0].shape[1]
    wide = band.shape[2]
    per_piece = lanes // wide
    groups = per_piece * count
    spans = band.shape[1]
    pad = spans // 2
    ch = wide // PACK
    per_head = ch // heads
    pairs = pixels // 2
    pitch = pixels + 8
    xi, ci = lax.axis_index("disp"), 0

    for side in range(pad):
        xs[side] = jnp.zeros((pixels, wide), BF16)
        xs[pad + groups + side] = jnp.zeros((pixels, wide), BF16)
        ys[side] = jnp.zeros((pixels, wide), BF16)
        ys[pad + groups + side] = jnp.zeros((pixels, wide), BF16)
    for a in range(nd):
        for k in range(nc):
            src_x = lax.rem(xi - a + nd, nd)
            src_c = lax.rem(ci - k + nc, nc)
            for n in range(chunks):
                at = pad + ((src_x * nc + src_c) * chunks + n) * per_piece
                piece = pieces[(n * nd + a) * nc + k]
                for g in range(per_piece):
                    xs[at + g] = piece[
                        half * pixels : (half + 1) * pixels, g * wide : (g + 1) * wide
                    ]

    step = math.gcd(groups, 256 // pixels)

    def conv(src, s, g0):
        acc = None
        for j in range(spans):
            lhs = src[pl.ds(g0 + j, step)].reshape(step * pixels, wide)
            part = dot(lhs, band[s, j])
            acc = part if acc is None else acc + part
        return acc + bias[s : s + 1]

    def first(i, carry):
        g0 = i * step
        y = silu(conv(xs, 0, g0)).astype(BF16)
        ys[pl.ds(pad + g0, step)] = y.reshape(step, pixels, wide)
        return carry

    lax.fori_loop(0, groups // step, first, 0, unroll=True)

    def second(i, carry):
        g0 = i * step
        y = conv(ys, 1, g0).astype(BF16).astype(F32)
        for i in range(step):
            at = pl.ds(pl.multiple_of((g0 + i) * pitch, 8), pixels)
            for b in range(wide // 128):
                sf[b, at, :] = y[i * pixels : (i + 1) * pixels, b * 128 : (b + 1) * 128]
        return carry

    lax.fori_loop(0, groups // step, second, 0, unroll=True)

    def gather(p, carry):
        at = pl.ds(pl.multiple_of(p * groups, groups), groups)
        for q in range(2):
            for b in range(wide // 128):
                piece = sf[b, pl.ds(2 * p + q, groups, stride=pitch), :]
                sec[q, at, b * 128 : (b + 1) * 128] = piece
        return carry

    lax.fori_loop(0, pairs, gather, 0, unroll=True)

    for q in range(2):
        s = sec[q]
        hi = (s * s).astype(BF16)
        mean = dot(hi, mean_mat[...])
        nrm[q] = (s * lax.rsqrt(mean + 1e-05) * gain).astype(BF16)
    qe[...] = (dot(nrm[0], w_qe[...]) * q_scale).astype(BF16)
    qo[...] = (dot(nrm[1], w_qo[...]) * q_scale).astype(BF16)
    kk[...] = (dot(nrm[0], w_k[0]) + dot(nrm[1], w_k[1])).astype(BF16)
    vv[...] = (dot(nrm[0], w_v[0]) + dot(nrm[1], w_v[1])).astype(BF16)

    keys = PACK * groups
    lane = lax.broadcasted_iota(jnp.int32, (keys, 2 * ch), 1)
    head_of = lax.rem(lane, ch) // per_head
    ones_row = lax.broadcasted_iota(jnp.int32, (16, keys * heads), 0)
    ones_col = lax.broadcasted_iota(jnp.int32, (16, keys * heads), 1)
    ones = jnp.where(ones_row == ones_col // keys, 1.0, 0.0).astype(BF16)

    def stack(ref, at):
        return jnp.concatenate(
            [ref[at, u * 2 * ch : (u + 1) * 2 * ch] for u in range(PACK)], axis=0
        )

    def score(p, carry):
        at = pl.ds(pl.multiple_of(p * groups, groups), groups)
        queries = jnp.concatenate([stack(qe, at), stack(qo, at)], axis=0)
        key = stack(kk, at)
        zero = jnp.zeros_like(key)
        for h in range(heads):
            part = dot_nt(jnp.where(head_of == h, key, zero), queries)
            top = jnp.max(part, axis=0, keepdims=True)
            soft[p, h * keys : (h + 1) * keys] = jnp.exp2(part - top).astype(BF16)
        return carry

    blank = jnp.zeros((per_head, keys), BF16)

    def mixing(p, carry):
        at = pl.ds(pl.multiple_of(p * groups, groups), groups)
        value_t = stack(vv, at).astype(F32).T.astype(BF16)
        rows = []
        for q in range(2):
            for h in range(heads):
                base = q * ch + h * per_head
                rows.append(
                    jnp.concatenate(
                        [
                            value_t[base : base + per_head] if m == h else blank
                            for m in range(heads)
                        ],
                        axis=1,
                    )
                )
        rows.append(ones)
        summed = dot(jnp.concatenate(rows, axis=0), soft[p])
        inv = 1.0 / summed[2 * ch : 2 * ch + heads]
        blocks = []
        for q in range(2):
            cols = slice(q * keys, (q + 1) * keys)
            for h in range(heads):
                base = q * ch + h * per_head
                blocks.append(
                    summed[base : base + per_head, cols] * inv[h : h + 1, cols]
                )
        mixed = jnp.concatenate(blocks, axis=0).T
        for u in range(PACK):
            mix[at, u * 2 * ch : (u + 1) * 2 * ch] = mixed[
                u * groups : (u + 1) * groups
            ].astype(BF16)
        return carry

    lax.fori_loop(0, pairs, score, 0, unroll=min(pairs, 8))
    lax.fori_loop(0, pairs, mixing, 0, unroll=min(pairs, 8))

    for q in range(2):
        attended = sec[q] + dot(mix[...], w_out[q])
        logits = dot(attended.astype(BF16), w_gate[...]) + gate_off
        sec[q] = sigmoid(logits)

    def scatter(p, carry):
        at = pl.ds(pl.multiple_of(p * groups, groups), groups)
        for q in range(2):
            for b in range(wide // 128):
                sf[b, pl.ds(2 * p + q, groups, stride=pitch), :] = sec[
                    q, at, b * 128 : (b + 1) * 128
                ]
        return carry

    lax.fori_loop(0, pairs, scatter, 0, unroll=True)
    slab = groups // nd
    for a in range(nd):
        g0 = lax.rem(xi + a, nd) * slab
        for g in range(slab):
            row = pl.ds(pl.multiple_of((g0 + g) * pitch, 8), pixels)
            for b in range(wide // 128):
                at = g * wide + b * 128
                outs[a][:, at : at + 128] = sf[b, row, :].astype(BF16)


def disparity(nd, nc, heads, chunks, half, halves, pieces, weights):
    pixels, lanes = pieces[0].shape
    pixels //= halves
    band = weights[0]
    wide = band.shape[2]
    groups = lanes * nd * nc * chunks // wide
    pad = band.shape[1] // 2
    pairs = pixels // 2
    scratch = [
        pltpu.VMEM((groups + 2 * pad, pixels, wide), BF16),
        pltpu.VMEM((groups + 2 * pad, pixels, wide), BF16),
        pltpu.VMEM((wide // 128, groups * (pixels + 8), 128), F32),
        pltpu.VMEM((2, pairs * groups, wide), BF16),
        pltpu.VMEM((pairs * groups, 2 * wide), BF16),
        pltpu.VMEM((pairs * groups, 2 * wide), BF16),
        pltpu.VMEM((pairs * groups, 2 * wide), BF16),
        pltpu.VMEM((pairs * groups, 2 * wide), BF16),
        pltpu.VMEM((pairs * groups, 2 * wide), BF16),
        pltpu.VMEM((2, pairs * groups, wide), F32),
        pltpu.VMEM((pairs, heads * PACK * groups, 2 * PACK * groups), BF16),
    ]
    return pl.pallas_call(
        functools.partial(disparity_kernel, nd, nc, heads, chunks, half),
        out_shape=[jax.ShapeDtypeStruct((pixels, groups * wide // nd), BF16)] * nd,
        in_specs=[vmem()] * (len(pieces) + 10),
        out_specs=[vmem()] * nd,
        scratch_shapes=scratch,
        compiler_params=pltpu.CompilerParams(vmem_limit_bytes=18 << 20),
        cost_estimate=pl.CostEstimate(
            flops=pixels * 340_000_000, bytes_accessed=4 << 20, transcendentals=0
        ),
        name="disparity",
    )(*pieces, *weights)


def gate_kernel(nd, halves, volume, *refs):
    gates, out = refs[: nd * halves], refs[nd * halves]
    rows, cols, _ = volume.shape
    part = rows // nd
    own = part // halves
    for h in range(halves):
        for a in range(nd):
            top = lax.rem(lax.axis_index("disp") - a + nd, nd) * part + h * own
            for r in range(own):
                g = gates[h * nd + a][r * cols : (r + 1) * cols]
                v = volume[top + r].astype(F32) * g.astype(F32)
                out[top + r] = v.astype(BF16)


def gate(nd, halves, volume, gates):
    return pl.pallas_call(
        functools.partial(gate_kernel, nd, halves),
        out_shape=jax.ShapeDtypeStruct(volume.shape, volume.dtype),
        in_specs=[vmem()] * (1 + nd * halves),
        out_specs=vmem(),
        compiler_params=pltpu.CompilerParams(vmem_limit_bytes=3 << 20),
        name="gate",
    )(volume, *gates)


def shift_pairs(sizes, moves):
    out = []
    count = math.prod(sizes)
    for flat in range(count):
        rest, place = flat, []
        for size in reversed(sizes):
            place.append(rest % size)
            rest //= size
        place = place[::-1]
        target = 0
        for at, move, size in zip(place, moves, sizes):
            target = target * size + (at + move) % size
        out.append((flat, target))
    return out


def per_device(
    volume,
    planar_taps,
    planar_bias,
    shift_taps,
    shift_bias,
    norm_gain,
    qkv,
    exit_proj,
    head_scale,
    gate_proj,
    gate_bias,
):
    layers = planar_bias.shape[0]
    heads = head_scale.shape[0]
    nz, nd, nc = [lax.axis_size(a) for a in ("rows", "disp", "cols")]

    if nc > 2:
        raise ValueError("cols: 1 or 2")
    lanes = volume.shape[2]
    chunks = 2 if lanes % (2 * WIDE) == 0 else 1
    sends = []
    for n in range(chunks):
        send_a, send_b, *whole = cut(layers, chunks, n, volume)
        sends += [send_a, send_b]
    mine = whole[0]
    pairs_a = [(z, z + 1) for z in range(0, nz - 1, 2)]
    pairs_b = [(z, z + 1) for z in range(1, nz - 1, 2)]
    both = [ps + [(j, i) for i, j in ps] for ps in (pairs_a, pairs_b)]
    halos = []
    for i, v in enumerate(sends):
        halos.append(lax.ppermute(v, "rows", both[i % 2]))

    made = prepare(
        planar_taps,
        planar_bias,
        shift_taps,
        shift_bias,
        norm_gain,
        qkv,
        exit_proj,
        head_scale,
        gate_proj,
        gate_bias,
    )
    rows_w, band, w_qe, w_qo, w_k, w_v, w_out, w_gate, mean_mat, plane_b, shift_b, ends = made
    got = []
    for n in range(chunks):
        halo_a, halo_b = halos[2 * n : 2 * n + 2]
        side = edge(n, mine, halo_a, halo_b)
        if nc > 1:
            side = lax.ppermute(side, "cols", [(0, 1), (1, 0)])
        pieces = planar(nd, nc, n, mine, halo_a, halo_b, side, rows_w, plane_b)
        for a, piece in enumerate(pieces):
            if a:
                piece = lax.ppermute(piece, "disp", shift_pairs((nd,), (a,)))
            got.append(piece)
    pixels = got[0].shape[0]
    halves = 2 if pixels % 32 == 0 else 1
    weights = [band, shift_b, ends, w_qe, w_qo, w_k, w_v, w_out, w_gate, mean_mat]
    gates = []
    for h in range(halves):
        parts = disparity(nd, 1, heads, chunks, h, halves, got, weights)
        for a, g in enumerate(parts):
            if a:
                g = lax.ppermute(g, "disp", shift_pairs((nd,), (a,)))
            gates.append(g)
    return gate(nd, halves, volume, gates)


def solution(mesh):
    spec = P(("groups", "rows"), "cols", "disp")

    return jax.shard_map(
        per_device, mesh=mesh, in_specs=(spec,) + (P(),) * 10, out_specs=spec, check_vma=False
    )
```

```python
import functools
import math

import jax
import jax.numpy as jnp
from jax import lax
from jax.experimental import pallas as pl
from jax.experimental.pallas import tpu as pltpu
from jax.sharding import PartitionSpec as P


F32 = jnp.float32
BF16 = jnp.bfloat16
SPLIT = 2
PACK = 4
WIDE = 256


def vmem():
    return pl.BlockSpec(memory_space=pltpu.VMEM)


def silu(v):
    half = 0.5 * v
    return half + half * jnp.tanh(half)


def sigmoid(v):
    return 0.5 + 0.5 * jnp.tanh(0.5 * v)


def dot(a, b):
    return jnp.dot(a, b, preferred_element_type=F32)


def dot_nt(a, b):
    return lax.dot_general(a, b, (((1,), (1,)), ((), ())), preferred_element_type=F32)


def prepare_kernel(heads, taps3, taps17, qkv, exit_proj, gate_proj, vecs, *rest):
    outs, (t3, t17, wq, we, wg, vec, sems) = rest[:9], rest[9:]
    copies = [
        pltpu.make_async_copy(src, dst, sems.at[i])
        for i, (src, dst) in enumerate(
            [(taps3, t3), (taps17, t17), (qkv, wq), (exit_proj, we), (gate_proj, wg)]
        )
    ]
    for i, v in enumerate(vecs):
        copies.append(pltpu.make_async_copy(v, vec[i], sems.at[5 + i]))
    for c in copies:
        c.start()
    rows_w, band, w_qkv, w_out, w_gate, mean_mat, plane_b, shift_b, ends = outs
    layers = rows_w.shape[0]
    ch = we.shape[0]
    spans = band.shape[1]
    taps = t17.shape[1]
    zero = jnp.zeros((ch, ch), BF16)
    none = jnp.zeros((ch, 2 * ch), BF16)
    for ref in (w_qkv, w_out, w_gate):
        ref[...] = jnp.zeros_like(ref)
    r = lax.broadcasted_iota(jnp.int32, mean_mat.shape, 0) // ch
    c = lax.broadcasted_iota(jnp.int32, mean_mat.shape, 1) // ch
    mean_mat[...] = jnp.where(r == c, 1.0 / ch, 0.0).astype(BF16)
    for c in copies:
        c.wait()

    def pair(x, y):
        return jnp.concatenate([x, y], axis=1)

    def planar_block(layer, carry):
        for j in range(3):
            tap = [t3[layer * 9 + i * 3 + j] for i in range(3)] + [zero]
            for rr in range(6):
                top = (j * 6 + rr) * ch
                for b in range(2):
                    t = rr - 2 * b
                    block = none
                    if 0 <= t <= 3:
                        block = pair(tap[t], tap[t - 1] if t else zero)
                    rows_w[layer, top : top + ch, b * 2 * ch : (b + 1) * 2 * ch] = block
        return carry

    lax.fori_loop(0, layers, planar_block, 0)

    def band_block(s, carry):
        table = []
        for t in range(taps + 1):
            table.append(
                pair(t17[s, t] if t < taps else zero, t17[s, t - 1] if t else zero)
            )
        for j in range(spans):
            for u in range(PACK):
                for b in range(PACK // 2):
                    t = PACK * (j - spans // 2) + u - 2 * b + taps // 2
                    block = table[t] if 0 <= t <= taps else none
                    band[s, j, u * ch : (u + 1) * ch, 2 * b * ch : 2 * (b + 1) * ch] = block
        return carry

    lax.fori_loop(0, 2, band_block, 0)
    w = wq[...]
    parts = [w[:, i * ch : (i + 1) * ch] for i in range(3)]
    lo = [pair(p, zero) for p in parts]
    hi = [pair(zero, p) for p in parts]
    out_lo, out_hi = pair(we[...], zero), pair(zero, we[...])
    gate_lo, gate_hi = pair(wg[...], zero), pair(zero, wg[...])
    for u in range(PACK):
        rows = slice(u * ch, (u + 1) * ch)
        tile = slice((u // 2) * 2 * ch, (u // 2 + 1) * 2 * ch)
        for i in range(3):
            w_qkv[i, rows, tile] = hi[i] if u % 2 else lo[i]
        for q in range(2):
            at = u * 2 * ch + q * ch
            w_out[q, at : at + ch, tile] = out_hi if u % 2 else out_lo
        w_gate[rows, tile] = gate_hi if u % 2 else gate_lo

    def tiled(v):
        return jnp.concatenate([v] * PACK, axis=1)

    plane_b[...] = tiled(vec[0][...])
    shift_b[...] = tiled(vec[1][...])
    ends[0:1] = tiled(vec[2][...])
    ends[1:2] = tiled(vec[3][...])
    head = lax.rem(lax.broadcasted_iota(jnp.int32, (1, PACK * ch), 1), ch) // (ch // heads)
    row = jnp.zeros((1, PACK * ch), F32)
    for h in range(heads):
        row = jnp.where(head == h, vec[4][:, h : h + 1], row)
    ends[2:3] = row * (math.log2(math.e) / math.sqrt(ch // heads))


def prepare(planar_taps, planar_bias, shift_taps, shift_bias, gain, qkv, exit_proj, head_scale, gate_proj, gate_bias):
    layers, ch = planar_bias.shape
    taps = shift_taps.shape[1]
    heads = head_scale.shape[0]
    spans = 2 * (-(-(taps // 2) // PACK)) + 1
    size = PACK * ch
    sds = jax.ShapeDtypeStruct
    outs = [
        sds((layers, 18 * ch, size), BF16),
        sds((2, spans, size, size), BF16),
        sds((3, size, size), BF16),
        sds((2, 2 * size, size), BF16),
        sds((size, size), BF16),
        sds((size, size), BF16),
        sds((layers, size), F32),
        sds((2, size), F32),
        sds((3, size), F32),
    ]
    anywhere = pl.BlockSpec(memory_space=pltpu.HBM)
    vecs = [planar_bias, shift_bias, gain[None], gate_bias[None], head_scale[None]]
    big = [planar_taps.reshape(layers * 9, ch, ch), shift_taps, qkv, exit_proj, gate_proj]

    def body(*refs):
        prepare_kernel(heads, *refs[:5], refs[5:10], *refs[10:19], *refs[19:24], refs[24:29], refs[29])

    return pl.pallas_call(
        body,
        out_shape=outs,
        in_specs=[anywhere] * 10,
        out_specs=[vmem()] * 9,
        scratch_shapes=[pltpu.VMEM(v.shape, v.dtype) for v in big + vecs]
        + [pltpu.SemaphoreType.DMA((10,))],
        compiler_params=pltpu.CompilerParams(vmem_limit_bytes=10 << 20),
        cost_estimate=pl.CostEstimate(flops=0, bytes_accessed=8 << 20, transcendentals=0),
        name="prepare",
    )(*[pltpu.with_memory_space_constraint(v, pltpu.HBM) for v in big + vecs])


def cut_kernel(halo, chunk, volume, *rest):
    outs, sems = rest[:-1], rest[-1]
    rows = volume.shape[0]
    lanes = outs[0].shape[2]
    even = lax.rem(lax.axis_index("rows") + 1, 2)
    copies = []
    for i, far in enumerate((even, 1 - even)):
        at = slice(chunk * lanes, (chunk + 1) * lanes)
        part = volume.at[pl.ds(far * (rows - halo), halo), :, at]
        copies.append(pltpu.make_async_copy(part, outs[i], sems.at[i]))
    if len(outs) > 2:
        copies.append(pltpu.make_async_copy(volume, outs[2], sems.at[2]))
    for c in copies:
        c.start()
    for c in copies:
        c.wait()


def cut(halo, chunks, chunk, volume):
    _, cols, lanes = volume.shape
    outs = [jax.ShapeDtypeStruct((halo, cols, lanes // chunks), BF16)] * 2
    if chunk == chunks - 1:
        outs.append(jax.ShapeDtypeStruct(volume.shape, BF16))
    return pl.pallas_call(
        functools.partial(cut_kernel, halo, chunk),
        out_shape=outs,
        in_specs=[pl.BlockSpec(memory_space=pltpu.HBM)],
        out_specs=[vmem()] * len(outs),
        scratch_shapes=[pltpu.SemaphoreType.DMA((len(outs),))],
        compiler_params=pltpu.CompilerParams(vmem_limit_bytes=3 << 20),
        name="cut",
    )(pltpu.with_memory_space_constraint(volume, pltpu.HBM))


def edge_kernel(chunk, mine, halo_a, halo_b, out):
    rows = mine.shape[0]
    halo, lanes = halo_a.shape[0], halo_a.shape[2]
    width = out.shape[1]
    even = lax.rem(lax.axis_index("rows") + 1, 2)
    first = lax.axis_index("cols") == 0
    at_a = even * (halo + rows)
    at_b = (1 - even) * (halo + rows)
    last = mine.shape[1] - width

    def take(v):
        v = v.astype(F32)
        return jnp.where(first, v[last:], v[:width]).astype(BF16)

    for r in range(rows):
        out[halo + r] = take(mine[r, :, chunk * lanes : (chunk + 1) * lanes])
    for r in range(halo):
        out[at_a + r] = take(halo_a[r])
        out[at_b + r] = take(halo_b[r])


def edge(chunk, mine, halo_a, halo_b):
    halo, cols, lanes = halo_a.shape
    total = mine.shape[0] + 2 * halo
    return pl.pallas_call(
        functools.partial(edge_kernel, chunk),
        out_shape=jax.ShapeDtypeStruct((total, min(8, cols), lanes), BF16),
        in_specs=[vmem()] * 3,
        out_specs=vmem(),
        compiler_params=pltpu.CompilerParams(vmem_limit_bytes=3 << 20),
        name="edge",
    )(mine, halo_a, halo_b)


def planar_kernel(nd, nc, chunk, *refs):
    mine, halo_a, halo_b, side, weights, bias = refs[:6]
    outs = refs[6 : 6 + nd]
    flat, x1, *xs, last, back = refs[6 + nd :]
    rows, own = mine.shape[:2]
    halo, lanes = halo_a.shape[0], halo_a.shape[2]
    layers = bias.shape[0]
    width = side.shape[1]
    tiles = lanes // 128
    pitch = own + 8
    ch = 64
    total = rows + 2 * halo
    xi, zi = [lax.axis_index(n) for n in ("disp", "rows")]
    ci = lax.axis_index("cols") if nc > 1 else 0
    more = layers if nc > 1 else 0
    nz = lax.axis_size("rows")
    even = lax.rem(zi + 1, 2)
    at_a = even * (halo + rows)
    at_b = (1 - even) * (halo + rows)

    def put(r, base, value):
        for t in range(tiles):
            at = t * pitch + base
            flat[r, at : at + value.shape[0], :] = value[:, t * 128 : (t + 1) * 128].astype(F32)

    def put_own(r, carry):
        put(halo + r, 0, mine[r, :, chunk * lanes : (chunk + 1) * lanes])
        return carry

    def put_halo(r, carry):
        put(at_a + r, 0, halo_a[r])
        put(at_b + r, 0, halo_b[r])
        return carry

    def put_side(r, carry):
        put(r, own, side[r])
        return carry

    lax.fori_loop(0, rows, put_own, 0)
    lax.fori_loop(0, halo, put_halo, 0)
    if more:
        lax.fori_loop(0, total, put_side, 0)
    low = lax.broadcasted_iota(jnp.int32, (tiles, 128), 1) < ch
    stages = [x1] + xs
    for x in stages:
        x[0] = jnp.zeros(x.shape[1:], BF16)
        x[x.shape[0] - 1] = jnp.zeros(x.shape[1:], BF16)

    def turn(source, target):
        at = pl.ds(source, tiles, stride=pitch)
        for p in range(total // 2):
            a, b = flat[2 * p, at, :], flat[2 * p + 1, at, :]
            e = jnp.where(low, a, pltpu.roll(b, ch, 1))
            o = jnp.where(low, pltpu.roll(a, ch, 1), b)
            x1[target + 1, :, p * 128 : (p + 1) * 128] = jnp.concatenate([e, o], axis=0).astype(BF16)

    def turn_own(c, carry):
        turn(c, more * ci + c)
        return carry

    lax.fori_loop(0, own, turn_own, 0, unroll=16)
    for c in range(more):
        turn(own + c + (width - more) * ci, own * (1 - ci) + c)
    row_of = lax.broadcasted_iota(jnp.int32, (1, 256), 1) // ch
    for layer in range(layers):
        height = total - 2 * (layer + 1)
        beyond = layers - 1 - layer
        src = stages[layer]
        count = own + max(more - 1 - layer, 0)
        block = -(-count // SPLIT)
        shift = ci if more else 0
        for q in range(0, height // 2, 2):
            single = q + 1 == height // 2
            span = 128 * (2 if single else 3)
            wide = 128 if single else 256
            row = row_of[:, :wide] + 2 * q
            keep = jnp.ones((1, wide), F32)
            keep = jnp.where((row < beyond) & (zi == 0), 0.0, keep)
            keep = jnp.where((row >= height - beyond) & (zi == nz - 1), 0.0, keep)

            for c0 in [min(i, count - block) for i in range(0, count, block)]:
                lhs = jnp.concatenate(
                    [
                        src[pl.ds(c0 + shift + j, block), :, q * 128 : q * 128 + span].reshape(
                            block * 2 * tiles, span
                        )
                        for j in range(3)
                    ],
                    axis=1,
                )
                if single:
                    rhs = jnp.concatenate(
                        [weights[layer, j * 384 : j * 384 + span, :wide] for j in range(3)], axis=0
                    )
                else:
                    rhs = weights[layer]
                y = silu(dot(lhs, rhs) + bias[layer : layer + 1, :wide])
                if layer < layers - 1:
                    y = (y * keep).astype(BF16).reshape(block, 2 * tiles, wide)
                    stages[layer + 1][c0 + 1 : c0 + 1 + block, :, q * 128 : q * 128 + wide] = y
                else:
                    y = y.reshape(block, 2 * tiles, wide)
                    last[c0 : c0 + block, :, q * 128 : q * 128 + wide] = y

    def turn_back(c, carry):
        at = pl.ds(c, tiles, stride=pitch)
        for p in range(rows // 2):
            e = last[c, :tiles, p * 128 : (p + 1) * 128]
            o = last[c, tiles:, p * 128 : (p + 1) * 128]
            back[2 * p, at, :] = jnp.where(low, e, pltpu.roll(o, ch, 1))
            back[2 * p + 1, at, :] = jnp.where(low, pltpu.roll(e, ch, 1), o)
        return carry

    lax.fori_loop(0, own, turn_back, 0, unroll=16)
    part = rows // nd
    for a in range(nd):
        top = lax.rem(xi + a, nd) * part
        for r in range(part):
            for t in range(tiles):
                outs[a][r * own : (r + 1) * own, t * 128 : (t + 1) * 128] = back[
                    top + r, t * pitch : t * pitch + own, :
                ].astype(BF16)


def planar(nd, nc, chunk, mine, halo_a, halo_b, side, weights, bias):
    rows, own = mine.shape[:2]
    halo, lanes = halo_a.shape[0], halo_a.shape[2]
    layers = bias.shape[0]
    tiles = lanes // 128
    total = rows + 2 * halo
    more = layers if nc > 1 else 0
    scratch = [pltpu.VMEM((total, tiles * (own + 8), 128), F32)]
    scratch += [
        pltpu.VMEM((own + max(more - k, 0) + 2, 2 * tiles, (total // 2 - k) * 128), BF16)
        for k in range(layers)
    ]
    scratch += [
        pltpu.VMEM((own, 2 * tiles, rows * 64), F32),
        pltpu.VMEM((rows, tiles * (own + 8), 128), F32),
    ]
    return pl.pallas_call(
        functools.partial(planar_kernel, nd, nc, chunk),
        out_shape=[jax.ShapeDtypeStruct((rows * own // nd, lanes), BF16)] * nd,
        in_specs=[vmem()] * 6,
        out_specs=[vmem()] * nd,
        scratch_shapes=scratch,
        compiler_params=pltpu.CompilerParams(vmem_limit_bytes=18 << 20),
        cost_estimate=pl.CostEstimate(
            flops=36 * lanes * 2 * own * total * 256, bytes_accessed=4 << 20, transcendentals=0
        ),
        name="planar",
    )(mine, halo_a, halo_b, side, weights, bias)


def early_kernel(chunks, *refs):
    pieces, band, bias, out, xs = refs[:chunks], *refs[chunks:]
    pixels, lanes = pieces[0].shape
    wide = band.shape[2]
    spans = band.shape[1]
    per_piece = lanes // wide
    for n in range(chunks):
        for g in range(per_piece):
            xs[n * per_piece + g] = pieces[n][:, g * wide : (g + 1) * wide]
    inner = out.shape[0]
    step = max(d for d in range(1, inner + 1) if inner % d == 0 and d * pixels <= 256)
    for g0 in range(0, inner, step):
        acc = None
        for j in range(spans):
            lhs = xs[g0 + j : g0 + j + step].reshape(step * pixels, wide)
            part = dot(lhs, band[0, j])
            acc = part if acc is None else acc + part
        y = silu(acc + bias[0:1]).astype(BF16)
        out[g0 : g0 + step] = y.reshape(step, pixels, wide)


def early(pieces, band, bias):
    pixels, lanes = pieces[0].shape
    wide = band.shape[2]
    own = lanes * len(pieces) // wide
    inner = own - band.shape[1] + 1
    return pl.pallas_call(
        functools.partial(early_kernel, len(pieces)),
        out_shape=jax.ShapeDtypeStruct((inner, pixels, wide), BF16),
        in_specs=[vmem()] * (len(pieces) + 2),
        out_specs=vmem(),
        scratch_shapes=[pltpu.VMEM((own, pixels, wide), BF16)],
        compiler_params=pltpu.CompilerParams(vmem_limit_bytes=6 << 20),
        cost_estimate=pl.CostEstimate(
            flops=pixels * 40_000_000, bytes_accessed=1 << 20, transcendentals=0
        ),
        name="early",
    )(*pieces, band, bias)


def disparity_kernel(
    nd,
    nc,
    heads,
    chunks,
    half,
    *refs,
):
    count = chunks * nd * nc
    pieces = refs[:count]
    begun, refs = refs[count], refs[:count] + refs[count + 1 :]
    band, bias, ends, w_qkv, w_out, w_gate, mean_mat = refs[count : count + 7]
    outs = refs[count + 7 : count + 7 + nd]
    xs, ys, sf, nrm, qe, qo, kk, vv, mix, sec, soft = refs[count + 7 + nd :]
    gain, gate_off = ends[0:1], ends[1:2]
    q_scale = ends[2:3]
    pixels, lanes = outs[0].shape[0], pieces[0].shape[1]
    wide = band.shape[2]
    per_piece = lanes // wide
    groups = per_piece * count
    spans = band.shape[1]
    pad = spans // 2
    ch = wide // PACK
    per_head = ch // heads
    pairs = pixels // 2
    pitch = pixels + 8
    xi, ci = lax.axis_index("disp"), 0

    for side in range(pad):
        xs[side] = jnp.zeros((pixels, wide), BF16)
        xs[pad + groups + side] = jnp.zeros((pixels, wide), BF16)
        ys[side] = jnp.zeros((pixels, wide), BF16)
        ys[pad + groups + side] = jnp.zeros((pixels, wide), BF16)
    for a in range(nd):
        for k in range(nc):
            src_x = lax.rem(xi - a + nd, nd)
            src_c = lax.rem(ci - k + nc, nc)
            for n in range(chunks):
                at = pad + ((src_x * nc + src_c) * chunks + n) * per_piece
                piece = pieces[(n * nd + a) * nc + k]
                for g in range(per_piece):
                    xs[at + g] = piece[
                        half * pixels : (half + 1) * pixels, g * wide : (g + 1) * wide
                    ]

    step = math.gcd(groups, 256 // pixels)

    def conv(src, s, g0):
        acc = None
        for j in range(spans):
            lhs = src[pl.ds(g0 + j, step)].reshape(step * pixels, wide)
            part = dot(lhs, band[s, j])
            acc = part if acc is None else acc + part
        return acc + bias[s : s + 1]

    inner = begun.shape[0]
    own = groups // nd
    for g in range(inner):
        ys[xi * own + 2 * pad + g] = begun[g, half * pixels : (half + 1) * pixels]
    rest = groups - inner
    part_of = max(d for d in range(1, rest + 1) if rest % d == 0 and d * pixels <= 256)
    for i in range(0, rest, part_of):
        where = [lax.rem(xi * own + own - pad + i + g, groups) for g in range(part_of)]
        acc = None
        for j in range(spans):
            lhs = jnp.concatenate([xs[g + j] for g in where], axis=0)
            part = dot(lhs, band[0, j])
            acc = part if acc is None else acc + part
        y = silu(acc + bias[0:1]).astype(BF16)
        for n, g in enumerate(where):
            ys[pad + g] = y[n * pixels : (n + 1) * pixels]

    def second(i, carry):
        g0 = i * step
        y = conv(ys, 1, g0).astype(BF16).astype(F32)
        for i in range(step):
            at = pl.ds(pl.multiple_of((g0 + i) * pitch, 8), pixels)
            for b in range(wide // 128):
                sf[b, at, :] = y[i * pixels : (i + 1) * pixels, b * 128 : (b + 1) * 128]
        return carry

    lax.fori_loop(0, groups // step, second, 0, unroll=True)

    def gather(p, carry):
        at = pl.ds(pl.multiple_of(p * groups, groups), groups)
        for q in range(2):
            for b in range(wide // 128):
                piece = sf[b, pl.ds(2 * p + q, groups, stride=pitch), :]
                sec[q, at, b * 128 : (b + 1) * 128] = piece
        return carry

    lax.fori_loop(0, pairs, gather, 0, unroll=True)

    for q in range(2):
        s = sec[q]
        hi = (s * s).astype(BF16)
        mean = dot(hi, mean_mat[...])
        nrm[q] = (s * lax.rsqrt(mean + 1e-05) * gain).astype(BF16)
    low = lax.broadcasted_iota(jnp.int32, (pairs * groups, 2 * ch), 1) < ch
    part = [[dot(nrm[q], w_qkv[i]) for q in range(2)] for i in range(3)]
    part[0] = [p * q_scale for p in part[0]]
    for t in range(PACK // 2):
        here = slice(t * 2 * ch, (t + 1) * 2 * ch)
        even = slice(2 * t * 2 * ch, (2 * t + 1) * 2 * ch)
        odd = slice((2 * t + 1) * 2 * ch, (2 * t + 2) * 2 * ch)
        a, b = part[0][0][:, here], part[0][1][:, here]
        qe[:, even] = jnp.where(low, a, 0.0).astype(BF16)
        qe[:, odd] = jnp.where(low, pltpu.roll(a, ch, 1), 0.0).astype(BF16)
        qo[:, even] = jnp.where(low, 0.0, pltpu.roll(b, ch, 1)).astype(BF16)
        qo[:, odd] = jnp.where(low, 0.0, b).astype(BF16)
        for i, ref in ((1, kk), (2, vv)):
            a, b = part[i][0][:, here], part[i][1][:, here]
            ref[:, even] = jnp.where(low, a, pltpu.roll(b, ch, 1)).astype(BF16)
            ref[:, odd] = jnp.where(low, pltpu.roll(a, ch, 1), b).astype(BF16)

    keys = PACK * groups
    lane = lax.broadcasted_iota(jnp.int32, (keys, 2 * ch), 1)
    head_of = lax.rem(lane, ch) // per_head
    ones_row = lax.broadcasted_iota(jnp.int32, (16, keys * heads), 0)
    ones_col = lax.broadcasted_iota(jnp.int32, (16, keys * heads), 1)
    ones = jnp.where(ones_row == ones_col // keys, 1.0, 0.0).astype(BF16)

    def stack(ref, at):
        return jnp.concatenate(
            [ref[at, u * 2 * ch : (u + 1) * 2 * ch] for u in range(PACK)], axis=0
        )

    def score(p, carry):
        at = pl.ds(pl.multiple_of(p * groups, groups), groups)
        queries = jnp.concatenate([stack(qe, at), stack(qo, at)], axis=0)
        key = stack(kk, at)
        zero = jnp.zeros_like(key)
        for h in range(heads):
            part = dot_nt(jnp.where(head_of == h, key, zero), queries)
            top = jnp.max(part, axis=0, keepdims=True)
            soft[p, h * keys : (h + 1) * keys] = jnp.exp2(part - top).astype(BF16)
        return carry

    blank = jnp.zeros((per_head, keys), BF16)

    def mixing(p, carry):
        at = pl.ds(pl.multiple_of(p * groups, groups), groups)
        value_t = stack(vv, at).astype(F32).T.astype(BF16)
        rows = []
        for q in range(2):
            for h in range(heads):
                base = q * ch + h * per_head
                rows.append(
                    jnp.concatenate(
                        [
                            value_t[base : base + per_head] if m == h else blank
                            for m in range(heads)
                        ],
                        axis=1,
                    )
                )
        rows.append(ones)
        summed = dot(jnp.concatenate(rows, axis=0), soft[p])
        inv = 1.0 / summed[2 * ch : 2 * ch + heads]
        blocks = []
        for q in range(2):
            cols = slice(q * keys, (q + 1) * keys)
            for h in range(heads):
                base = q * ch + h * per_head
                blocks.append(
                    summed[base : base + per_head, cols] * inv[h : h + 1, cols]
                )
        mixed = jnp.concatenate(blocks, axis=0).T
        for u in range(PACK):
            mix[at, u * 2 * ch : (u + 1) * 2 * ch] = mixed[
                u * groups : (u + 1) * groups
            ].astype(BF16)
        return carry

    lax.fori_loop(0, pairs, score, 0, unroll=min(pairs, 8))
    lax.fori_loop(0, pairs, mixing, 0, unroll=min(pairs, 8))

    for q in range(2):
        attended = sec[q] + dot(mix[...], w_out[q])
        logits = dot(attended.astype(BF16), w_gate[...]) + gate_off
        sec[q] = sigmoid(logits)

    def scatter(p, carry):
        at = pl.ds(pl.multiple_of(p * groups, groups), groups)
        for q in range(2):
            for b in range(wide // 128):
                sf[b, pl.ds(2 * p + q, groups, stride=pitch), :] = sec[
                    q, at, b * 128 : (b + 1) * 128
                ]
        return carry

    lax.fori_loop(0, pairs, scatter, 0, unroll=True)
    slab = groups // nd
    for a in range(nd):
        g0 = lax.rem(xi + a, nd) * slab
        for g in range(slab):
            row = pl.ds(pl.multiple_of((g0 + g) * pitch, 8), pixels)
            for b in range(wide // 128):
                at = g * wide + b * 128
                outs[a][:, at : at + 128] = sf[b, row, :].astype(BF16)


def disparity(nd, nc, heads, chunks, half, halves, pieces, begun, weights):
    pixels, lanes = pieces[0].shape
    pixels //= halves
    band = weights[0]
    wide = band.shape[2]
    groups = lanes * nd * nc * chunks // wide
    pad = band.shape[1] // 2
    pairs = pixels // 2
    scratch = [
        pltpu.VMEM((groups + 2 * pad, pixels, wide), BF16),
        pltpu.VMEM((groups + 2 * pad, pixels, wide), BF16),
        pltpu.VMEM((wide // 128, groups * (pixels + 8), 128), F32),
        pltpu.VMEM((2, pairs * groups, wide), BF16),
        pltpu.VMEM((pairs * groups, 2 * wide), BF16),
        pltpu.VMEM((pairs * groups, 2 * wide), BF16),
        pltpu.VMEM((pairs * groups, 2 * wide), BF16),
        pltpu.VMEM((pairs * groups, 2 * wide), BF16),
        pltpu.VMEM((pairs * groups, 2 * wide), BF16),
        pltpu.VMEM((2, pairs * groups, wide), F32),
        pltpu.VMEM((pairs, heads * PACK * groups, 2 * PACK * groups), BF16),
    ]
    return pl.pallas_call(
        functools.partial(disparity_kernel, nd, nc, heads, chunks, half),
        out_shape=[jax.ShapeDtypeStruct((pixels, groups * wide // nd), BF16)] * nd,
        in_specs=[vmem()] * (len(pieces) + 8),
        out_specs=[vmem()] * nd,
        scratch_shapes=scratch,
        compiler_params=pltpu.CompilerParams(vmem_limit_bytes=18 << 20),
        cost_estimate=pl.CostEstimate(
            flops=pixels * 340_000_000, bytes_accessed=4 << 20, transcendentals=0
        ),
        name="disparity",
    )(*pieces, begun, *weights)


def gate_kernel(nd, halves, volume, *refs):
    gates, out = refs[: nd * halves], refs[nd * halves]
    rows, cols, _ = volume.shape
    part = rows // nd
    own = part // halves
    for h in range(halves):
        for a in range(nd):
            top = lax.rem(lax.axis_index("disp") - a + nd, nd) * part + h * own
            for r in range(own):
                g = gates[h * nd + a][r * cols : (r + 1) * cols]
                v = volume[top + r].astype(F32) * g.astype(F32)
                out[top + r] = v.astype(BF16)


def gate(nd, halves, volume, gates):
    return pl.pallas_call(
        functools.partial(gate_kernel, nd, halves),
        out_shape=jax.ShapeDtypeStruct(volume.shape, volume.dtype),
        in_specs=[vmem()] * (1 + nd * halves),
        out_specs=vmem(),
        compiler_params=pltpu.CompilerParams(vmem_limit_bytes=3 << 20),
        name="gate",
    )(volume, *gates)


def shift_pairs(sizes, moves):
    out = []
    count = math.prod(sizes)
    for flat in range(count):
        rest, place = flat, []
        for size in reversed(sizes):
            place.append(rest % size)
            rest //= size
        place = place[::-1]
        target = 0
        for at, move, size in zip(place, moves, sizes):
            target = target * size + (at + move) % size
        out.append((flat, target))
    return out


def per_device(
    volume,
    planar_taps,
    planar_bias,
    shift_taps,
    shift_bias,
    norm_gain,
    qkv,
    exit_proj,
    head_scale,
    gate_proj,
    gate_bias,
):
    layers = planar_bias.shape[0]
    heads = head_scale.shape[0]
    nz, nd, nc = [lax.axis_size(a) for a in ("rows", "disp", "cols")]

    if nc > 2:
        raise ValueError("cols: 1 or 2")
    lanes = volume.shape[2]
    chunks = 2 if lanes % (2 * WIDE) == 0 else 1
    sends = []
    for n in range(chunks):
        send_a, send_b, *whole = cut(layers, chunks, n, volume)
        sends += [send_a, send_b]
    mine = whole[0]
    pairs_a = [(z, z + 1) for z in range(0, nz - 1, 2)]
    pairs_b = [(z, z + 1) for z in range(1, nz - 1, 2)]
    both = [ps + [(j, i) for i, j in ps] for ps in (pairs_a, pairs_b)]
    halos = []
    for i, v in enumerate(sends):
        halos.append(lax.ppermute(v, "rows", both[i % 2]))

    made = prepare(
        planar_taps,
        planar_bias,
        shift_taps,
        shift_bias,
        norm_gain,
        qkv,
        exit_proj,
        head_scale,
        gate_proj,
        gate_bias,
    )
    rows_w, band, w_qkv, w_out, w_gate, mean_mat, plane_b, shift_b, ends = made
    got = []
    for n in range(chunks):
        halo_a, halo_b = halos[2 * n : 2 * n + 2]
        side = edge(n, mine, halo_a, halo_b)
        if nc > 1:
            side = lax.ppermute(side, "cols", [(0, 1), (1, 0)])
        pieces = planar(nd, nc, n, mine, halo_a, halo_b, side, rows_w, plane_b)
        for a, piece in enumerate(pieces):
            if a:
                piece = lax.ppermute(piece, "disp", shift_pairs((nd,), (a,)))
            got.append(piece)
    pixels = got[0].shape[0]
    halves = 2 if pixels % 32 == 0 else 1
    weights = [band, shift_b, ends, w_qkv, w_out, w_gate, mean_mat]
    begun = early(got[::nd], band, shift_b)
    gates = []
    for h in range(halves):
        parts = disparity(nd, 1, heads, chunks, h, halves, got, begun, weights)
        for a, g in enumerate(parts):
            if a:
                g = lax.ppermute(g, "disp", shift_pairs((nd,), (a,)))
            gates.append(g)
    return gate(nd, halves, volume, gates)


def solution(mesh):
    spec = P(("groups", "rows"), "cols", "disp")

    return jax.shard_map(
        per_device, mesh=mesh, in_specs=(spec,) + (P(),) * 10, out_specs=spec, check_vma=False
    )
```

```python
import functools
import math

import jax
import jax.numpy as jnp
from jax import lax
from jax.experimental import pallas as pl
from jax.experimental.pallas import tpu as pltpu
from jax.sharding import PartitionSpec as P


F32 = jnp.float32
BF16 = jnp.bfloat16
SPLIT = 2
PACK = 4
WIDE = 256


def vmem():
    return pl.BlockSpec(memory_space=pltpu.VMEM)


def silu(v):
    half = 0.5 * v
    return half + half * jnp.tanh(half)


def sigmoid(v):
    return 0.5 + 0.5 * jnp.tanh(0.5 * v)


def dot(a, b):
    return jnp.dot(a, b, preferred_element_type=F32)


def dot_nt(a, b):
    return lax.dot_general(a, b, (((1,), (1,)), ((), ())), preferred_element_type=F32)


def prepare_kernel(heads, taps17, qkv, exit_proj, gate_proj, vecs, *rest):
    outs, (t17, wq, we, wg, vec, sems) = rest[:7], rest[7:]
    copies = [
        pltpu.make_async_copy(src, dst, sems.at[i])
        for i, (src, dst) in enumerate(
            [(taps17, t17), (qkv, wq), (exit_proj, we), (gate_proj, wg)]
        )
    ]
    for i, v in enumerate(vecs):
        copies.append(pltpu.make_async_copy(v, vec[i], sems.at[4 + i]))
    for c in copies:
        c.start()
    band, w_qkv, w_out, w_gate, mean_mat, shift_b, ends = outs
    ch = we.shape[0]
    spans = band.shape[1]
    taps = t17.shape[1]
    zero = jnp.zeros((ch, ch), BF16)
    none = jnp.zeros((ch, 2 * ch), BF16)
    for ref in (w_qkv, w_out, w_gate):
        ref[...] = jnp.zeros_like(ref)
    r = lax.broadcasted_iota(jnp.int32, mean_mat.shape, 0) // ch
    c = lax.broadcasted_iota(jnp.int32, mean_mat.shape, 1) // ch
    mean_mat[...] = jnp.where(r == c, 1.0 / ch, 0.0).astype(BF16)
    for c in copies:
        c.wait()

    def pair(x, y):
        return jnp.concatenate([x, y], axis=1)

    def band_block(s, carry):
        table = []
        for t in range(taps + 1):
            table.append(
                pair(t17[s, t] if t < taps else zero, t17[s, t - 1] if t else zero)
            )
        for j in range(spans):
            for u in range(PACK):
                for b in range(PACK // 2):
                    t = PACK * (j - spans // 2) + u - 2 * b + taps // 2
                    block = table[t] if 0 <= t <= taps else none
                    band[s, j, u * ch : (u + 1) * ch, 2 * b * ch : 2 * (b + 1) * ch] = block
        return carry

    lax.fori_loop(0, 2, band_block, 0)
    w = wq[...]
    parts = [w[:, i * ch : (i + 1) * ch] for i in range(3)]
    lo = [pair(p, zero) for p in parts]
    hi = [pair(zero, p) for p in parts]
    out_lo, out_hi = pair(we[...], zero), pair(zero, we[...])
    gate_lo, gate_hi = pair(wg[...], zero), pair(zero, wg[...])
    for u in range(PACK):
        rows = slice(u * ch, (u + 1) * ch)
        tile = slice((u // 2) * 2 * ch, (u // 2 + 1) * 2 * ch)
        for i in range(3):
            w_qkv[i, rows, tile] = hi[i] if u % 2 else lo[i]
        for q in range(2):
            at = u * 2 * ch + q * ch
            w_out[q, at : at + ch, tile] = out_hi if u % 2 else out_lo
        w_gate[rows, tile] = gate_hi if u % 2 else gate_lo

    def tiled(v):
        return jnp.concatenate([v] * PACK, axis=1)

    shift_b[...] = tiled(vec[0][...])
    ends[0:1] = tiled(vec[1][...])
    ends[1:2] = tiled(vec[2][...])
    head = lax.rem(lax.broadcasted_iota(jnp.int32, (1, PACK * ch), 1), ch) // (ch // heads)
    row = jnp.zeros((1, PACK * ch), F32)
    for h in range(heads):
        row = jnp.where(head == h, vec[3][:, h : h + 1], row)
    ends[2:3] = row * (math.log2(math.e) / math.sqrt(ch // heads))


def prepare(shift_taps, shift_bias, gain, qkv, exit_proj, head_scale, gate_proj, gate_bias):
    ch = gain.shape[0]
    taps = shift_taps.shape[1]
    heads = head_scale.shape[0]
    spans = 2 * (-(-(taps // 2) // PACK)) + 1
    size = PACK * ch
    sds = jax.ShapeDtypeStruct
    outs = [
        sds((2, spans, size, size), BF16),
        sds((3, size, size), BF16),
        sds((2, 2 * size, size), BF16),
        sds((size, size), BF16),
        sds((size, size), BF16),
        sds((2, size), F32),
        sds((3, size), F32),
    ]
    vecs = [shift_bias, gain[None], gate_bias[None], head_scale[None]]
    big = [shift_taps, qkv, exit_proj, gate_proj]

    def body(*refs):
        prepare_kernel(
            heads, *refs[:4], refs[4:8], *refs[8:15], *refs[15:19], refs[19:23], refs[23]
        )

    return from_hbm(body, outs, big + vecs)


def from_hbm(body, outs, args):
    return pl.pallas_call(
        body,
        out_shape=outs,
        in_specs=[pl.BlockSpec(memory_space=pltpu.HBM)] * len(args),
        out_specs=[vmem()] * len(outs),
        scratch_shapes=[pltpu.VMEM(v.shape, v.dtype) for v in args]
        + [pltpu.SemaphoreType.DMA((len(args),))],
        compiler_params=pltpu.CompilerParams(vmem_limit_bytes=10 << 20),
        cost_estimate=pl.CostEstimate(flops=0, bytes_accessed=4 << 20, transcendentals=0),
    )(*[pltpu.with_memory_space_constraint(v, pltpu.HBM) for v in args])


def planar_weights_kernel(taps3, bias, rows_w, plane_b, t3, vec, sems):
    copies = [
        pltpu.make_async_copy(taps3, t3, sems.at[0]),
        pltpu.make_async_copy(bias, vec, sems.at[1]),
    ]
    for c in copies:
        c.start()
    layers, ch = vec.shape
    zero = jnp.zeros((ch, ch), BF16)
    none = jnp.zeros((ch, 2 * ch), BF16)
    for c in copies:
        c.wait()

    def pair(x, y):
        return jnp.concatenate([x, y], axis=1)

    def planar_block(layer, carry):
        for j in range(3):
            tap = [t3[layer * 9 + i * 3 + j] for i in range(3)] + [zero]
            for rr in range(6):
                top = (j * 6 + rr) * ch
                for b in range(2):
                    t = rr - 2 * b
                    block = none
                    if 0 <= t <= 3:
                        block = pair(tap[t], tap[t - 1] if t else zero)
                    rows_w[layer, top : top + ch, b * 2 * ch : (b + 1) * 2 * ch] = block
        return carry

    lax.fori_loop(0, layers, planar_block, 0)

    plane_b[...] = jnp.concatenate([vec[...]] * PACK, axis=1)


def planar_weights(taps, bias):
    layers, ch = bias.shape
    outs = [
        jax.ShapeDtypeStruct((layers, 18 * ch, PACK * ch), BF16),
        jax.ShapeDtypeStruct((layers, PACK * ch), F32),
    ]
    args = [taps.reshape(layers * 9, ch, ch), bias]
    return from_hbm(planar_weights_kernel, outs, args)


def cut_kernel(halo, chunk, volume, *rest):
    outs, sems = rest[:-1], rest[-1]
    rows = volume.shape[0]
    lanes = outs[0].shape[2]
    even = lax.rem(lax.axis_index("rows") + 1, 2)
    copies = []
    for i, far in enumerate((even, 1 - even)):
        at = slice(chunk * lanes, (chunk + 1) * lanes)
        part = volume.at[pl.ds(far * (rows - halo), halo), :, at]
        copies.append(pltpu.make_async_copy(part, outs[i], sems.at[i]))
    if len(outs) > 2:
        copies.append(pltpu.make_async_copy(volume, outs[2], sems.at[2]))
    for c in copies:
        c.start()
    for c in copies:
        c.wait()


def cut(halo, chunks, chunk, volume):
    _, cols, lanes = volume.shape
    outs = [jax.ShapeDtypeStruct((halo, cols, lanes // chunks), BF16)] * 2
    if chunk == chunks - 1:
        outs.append(jax.ShapeDtypeStruct(volume.shape, BF16))
    return pl.pallas_call(
        functools.partial(cut_kernel, halo, chunk),
        out_shape=outs,
        in_specs=[pl.BlockSpec(memory_space=pltpu.HBM)],
        out_specs=[vmem()] * len(outs),
        scratch_shapes=[pltpu.SemaphoreType.DMA((len(outs),))],
        compiler_params=pltpu.CompilerParams(vmem_limit_bytes=3 << 20),
        name="cut",
    )(pltpu.with_memory_space_constraint(volume, pltpu.HBM))


def edge_kernel(chunk, mine, halo_a, halo_b, out):
    rows = mine.shape[0]
    halo, lanes = halo_a.shape[0], halo_a.shape[2]
    width = out.shape[1]
    even = lax.rem(lax.axis_index("rows") + 1, 2)
    first = lax.axis_index("cols") == 0
    at_a = even * (halo + rows)
    at_b = (1 - even) * (halo + rows)
    last = mine.shape[1] - width

    def take(v):
        v = v.astype(F32)
        return jnp.where(first, v[last:], v[:width]).astype(BF16)

    for r in range(rows):
        out[halo + r] = take(mine[r, :, chunk * lanes : (chunk + 1) * lanes])
    for r in range(halo):
        out[at_a + r] = take(halo_a[r])
        out[at_b + r] = take(halo_b[r])


def edge(chunk, mine, halo_a, halo_b):
    halo, cols, lanes = halo_a.shape
    total = mine.shape[0] + 2 * halo
    return pl.pallas_call(
        functools.partial(edge_kernel, chunk),
        out_shape=jax.ShapeDtypeStruct((total, min(8, cols), lanes), BF16),
        in_specs=[vmem()] * 3,
        out_specs=vmem(),
        compiler_params=pltpu.CompilerParams(vmem_limit_bytes=3 << 20),
        name="edge",
    )(mine, halo_a, halo_b)


def planar_kernel(nd, nc, chunk, *refs):
    mine, halo_a, halo_b, side, weights, bias = refs[:6]
    outs = refs[6 : 6 + nd]
    flat, x1, *xs, last, back = refs[6 + nd :]
    rows, own = mine.shape[:2]
    halo, lanes = halo_a.shape[0], halo_a.shape[2]
    layers = bias.shape[0]
    width = side.shape[1]
    tiles = lanes // 128
    pitch = own + 8
    ch = 64
    total = rows + 2 * halo
    xi, zi = [lax.axis_index(n) for n in ("disp", "rows")]
    ci = lax.axis_index("cols") if nc > 1 else 0
    more = layers if nc > 1 else 0
    nz = lax.axis_size("rows")
    even = lax.rem(zi + 1, 2)
    at_a = even * (halo + rows)
    at_b = (1 - even) * (halo + rows)

    def put(r, base, value):
        for t in range(tiles):
            at = t * pitch + base
            flat[r, at : at + value.shape[0], :] = value[:, t * 128 : (t + 1) * 128].astype(F32)

    def put_own(r, carry):
        put(halo + r, 0, mine[r, :, chunk * lanes : (chunk + 1) * lanes])
        return carry

    def put_halo(r, carry):
        put(at_a + r, 0, halo_a[r])
        put(at_b + r, 0, halo_b[r])
        return carry

    def put_side(r, carry):
        put(r, own, side[r])
        return carry

    lax.fori_loop(0, rows, put_own, 0)
    lax.fori_loop(0, halo, put_halo, 0)
    if more:
        lax.fori_loop(0, total, put_side, 0)
    low = lax.broadcasted_iota(jnp.int32, (tiles, 128), 1) < ch
    stages = [x1] + xs
    for x in stages:
        x[0] = jnp.zeros(x.shape[1:], BF16)
        x[x.shape[0] - 1] = jnp.zeros(x.shape[1:], BF16)

    def turn(source, target):
        at = pl.ds(source, tiles, stride=pitch)
        for p in range(total // 2):
            a, b = flat[2 * p, at, :], flat[2 * p + 1, at, :]
            e = jnp.where(low, a, pltpu.roll(b, ch, 1))
            o = jnp.where(low, pltpu.roll(a, ch, 1), b)
            x1[target + 1, :, p * 128 : (p + 1) * 128] = jnp.concatenate([e, o], axis=0).astype(BF16)

    def turn_own(c, carry):
        turn(c, more * ci + c)
        return carry

    lax.fori_loop(0, own, turn_own, 0, unroll=16)
    for c in range(more):
        turn(own + c + (width - more) * ci, own * (1 - ci) + c)
    row_of = lax.broadcasted_iota(jnp.int32, (1, 256), 1) // ch
    for layer in range(layers):
        height = total - 2 * (layer + 1)
        beyond = layers - 1 - layer
        src = stages[layer]
        count = own + max(more - 1 - layer, 0)
        block = -(-count // SPLIT)
        shift = ci if more else 0
        for q in range(0, height // 2, 2):
            single = q + 1 == height // 2
            span = 128 * (2 if single else 3)
            wide = 128 if single else 256
            row = row_of[:, :wide] + 2 * q
            keep = jnp.ones((1, wide), F32)
            keep = jnp.where((row < beyond) & (zi == 0), 0.0, keep)
            keep = jnp.where((row >= height - beyond) & (zi == nz - 1), 0.0, keep)

            for c0 in [min(i, count - block) for i in range(0, count, block)]:
                lhs = jnp.concatenate(
                    [
                        src[pl.ds(c0 + shift + j, block), :, q * 128 : q * 128 + span].reshape(
                            block * 2 * tiles, span
                        )
                        for j in range(3)
                    ],
                    axis=1,
                )
                if single:
                    rhs = jnp.concatenate(
                        [weights[layer, j * 384 : j * 384 + span, :wide] for j in range(3)], axis=0
                    )
                else:
                    rhs = weights[layer]
                y = silu(dot(lhs, rhs) + bias[layer : layer + 1, :wide])
                if layer < layers - 1:
                    y = (y * keep).astype(BF16).reshape(block, 2 * tiles, wide)
                    stages[layer + 1][c0 + 1 : c0 + 1 + block, :, q * 128 : q * 128 + wide] = y
                else:
                    y = y.reshape(block, 2 * tiles, wide)
                    last[c0 : c0 + block, :, q * 128 : q * 128 + wide] = y

    def turn_back(c, carry):
        at = pl.ds(c, tiles, stride=pitch)
        for p in range(rows // 2):
            e = last[c, :tiles, p * 128 : (p + 1) * 128]
            o = last[c, tiles:, p * 128 : (p + 1) * 128]
            back[2 * p, at, :] = jnp.where(low, e, pltpu.roll(o, ch, 1))
            back[2 * p + 1, at, :] = jnp.where(low, pltpu.roll(e, ch, 1), o)
        return carry

    lax.fori_loop(0, own, turn_back, 0, unroll=16)
    part = rows // nd
    for a in range(nd):
        top = lax.rem(xi + a, nd) * part
        for r in range(part):
            for t in range(tiles):
                outs[a][r * own : (r + 1) * own, t * 128 : (t + 1) * 128] = back[
                    top + r, t * pitch : t * pitch + own, :
                ].astype(BF16)


def planar(nd, nc, chunk, mine, halo_a, halo_b, side, weights, bias):
    rows, own = mine.shape[:2]
    halo, lanes = halo_a.shape[0], halo_a.shape[2]
    layers = bias.shape[0]
    tiles = lanes // 128
    total = rows + 2 * halo
    more = layers if nc > 1 else 0
    scratch = [pltpu.VMEM((total, tiles * (own + 8), 128), F32)]
    scratch += [
        pltpu.VMEM((own + max(more - k, 0) + 2, 2 * tiles, (total // 2 - k) * 128), BF16)
        for k in range(layers)
    ]
    scratch += [
        pltpu.VMEM((own, 2 * tiles, rows * 64), F32),
        pltpu.VMEM((rows, tiles * (own + 8), 128), F32),
    ]
    return pl.pallas_call(
        functools.partial(planar_kernel, nd, nc, chunk),
        out_shape=[jax.ShapeDtypeStruct((rows * own // nd, lanes), BF16)] * nd,
        in_specs=[vmem()] * 6,
        out_specs=[vmem()] * nd,
        scratch_shapes=scratch,
        compiler_params=pltpu.CompilerParams(vmem_limit_bytes=18 << 20),
        cost_estimate=pl.CostEstimate(
            flops=36 * lanes * 2 * own * total * 256, bytes_accessed=4 << 20, transcendentals=0
        ),
        name="planar",
    )(mine, halo_a, halo_b, side, weights, bias)


def early_kernel(chunks, *refs):
    pieces, band, bias, out, xs = refs[:chunks], *refs[chunks:]
    pixels, lanes = pieces[0].shape
    wide = band.shape[2]
    spans = band.shape[1]
    per_piece = lanes // wide
    for n in range(chunks):
        for g in range(per_piece):
            xs[n * per_piece + g] = pieces[n][:, g * wide : (g + 1) * wide]
    inner = out.shape[0]
    step = max(d for d in range(1, inner + 1) if inner % d == 0 and d * pixels <= 256)
    for g0 in range(0, inner, step):
        acc = None
        for j in range(spans):
            lhs = xs[g0 + j : g0 + j + step].reshape(step * pixels, wide)
            part = dot(lhs, band[0, j])
            acc = part if acc is None else acc + part
        y = silu(acc + bias[0:1]).astype(BF16)
        out[g0 : g0 + step] = y.reshape(step, pixels, wide)


def early(pieces, band, bias):
    pixels, lanes = pieces[0].shape
    wide = band.shape[2]
    own = lanes * len(pieces) // wide
    inner = own - band.shape[1] + 1
    return pl.pallas_call(
        functools.partial(early_kernel, len(pieces)),
        out_shape=jax.ShapeDtypeStruct((inner, pixels, wide), BF16),
        in_specs=[vmem()] * (len(pieces) + 2),
        out_specs=vmem(),
        scratch_shapes=[pltpu.VMEM((own, pixels, wide), BF16)],
        compiler_params=pltpu.CompilerParams(vmem_limit_bytes=6 << 20),
        cost_estimate=pl.CostEstimate(
            flops=pixels * 40_000_000, bytes_accessed=1 << 20, transcendentals=0
        ),
        name="early",
    )(*pieces, band, bias)


def disparity_kernel(
    nd,
    nc,
    heads,
    chunks,
    half,
    *refs,
):
    count = chunks * nd * nc
    pieces = refs[:count]
    begun, refs = refs[count], refs[:count] + refs[count + 1 :]
    band, bias, ends, w_qkv, w_out, w_gate, mean_mat = refs[count : count + 7]
    outs = refs[count + 7 : count + 7 + nd]
    xs, ys, sf, nrm, qe, qo, kk, vv, mix, sec, soft = refs[count + 7 + nd :]
    gain, gate_off = ends[0:1], ends[1:2]
    q_scale = ends[2:3]
    pixels, lanes = outs[0].shape[0], pieces[0].shape[1]
    wide = band.shape[2]
    per_piece = lanes // wide
    groups = per_piece * count
    spans = band.shape[1]
    pad = spans // 2
    ch = wide // PACK
    per_head = ch // heads
    pairs = pixels // 2
    pitch = pixels + 8
    xi, ci = lax.axis_index("disp"), 0

    for side in range(pad):
        xs[side] = jnp.zeros((pixels, wide), BF16)
        xs[pad + groups + side] = jnp.zeros((pixels, wide), BF16)
        ys[side] = jnp.zeros((pixels, wide), BF16)
        ys[pad + groups + side] = jnp.zeros((pixels, wide), BF16)
    for a in range(nd):
        for k in range(nc):
            src_x = lax.rem(xi - a + nd, nd)
            src_c = lax.rem(ci - k + nc, nc)
            for n in range(chunks):
                at = pad + ((src_x * nc + src_c) * chunks + n) * per_piece
                piece = pieces[(n * nd + a) * nc + k]
                for g in range(per_piece):
                    xs[at + g] = piece[
                        half * pixels : (half + 1) * pixels, g * wide : (g + 1) * wide
                    ]

    step = math.gcd(groups, 256 // pixels)

    def conv(src, s, g0):
        acc = None
        for j in range(spans):
            lhs = src[pl.ds(g0 + j, step)].reshape(step * pixels, wide)
            part = dot(lhs, band[s, j])
            acc = part if acc is None else acc + part
        return acc + bias[s : s + 1]

    inner = begun.shape[0]
    own = groups // nd
    for g in range(inner):
        ys[xi * own + 2 * pad + g] = begun[g, half * pixels : (half + 1) * pixels]
    rest = groups - inner
    part_of = max(d for d in range(1, rest + 1) if rest % d == 0 and d * pixels <= 256)
    for i in range(0, rest, part_of):
        where = [lax.rem(xi * own + own - pad + i + g, groups) for g in range(part_of)]
        acc = None
        for j in range(spans):
            lhs = jnp.concatenate([xs[g + j] for g in where], axis=0)
            part = dot(lhs, band[0, j])
            acc = part if acc is None else acc + part
        y = silu(acc + bias[0:1]).astype(BF16)
        for n, g in enumerate(where):
            ys[pad + g] = y[n * pixels : (n + 1) * pixels]

    def second(i, carry):
        g0 = i * step
        y = conv(ys, 1, g0).astype(BF16).astype(F32)
        for i in range(step):
            at = pl.ds(pl.multiple_of((g0 + i) * pitch, 8), pixels)
            for b in range(wide // 128):
                sf[b, at, :] = y[i * pixels : (i + 1) * pixels, b * 128 : (b + 1) * 128]
        return carry

    lax.fori_loop(0, groups // step, second, 0, unroll=True)

    def gather(p, carry):
        at = pl.ds(pl.multiple_of(p * groups, groups), groups)
        for q in range(2):
            for b in range(wide // 128):
                piece = sf[b, pl.ds(2 * p + q, groups, stride=pitch), :]
                sec[q, at, b * 128 : (b + 1) * 128] = piece
        return carry

    lax.fori_loop(0, pairs, gather, 0, unroll=True)

    for q in range(2):
        s = sec[q]
        hi = (s * s).astype(BF16)
        mean = dot(hi, mean_mat[...])
        nrm[q] = (s * lax.rsqrt(mean + 1e-05) * gain).astype(BF16)
    low = lax.broadcasted_iota(jnp.int32, (pairs * groups, 2 * ch), 1) < ch
    part = [[dot(nrm[q], w_qkv[i]) for q in range(2)] for i in range(3)]
    part[0] = [p * q_scale for p in part[0]]
    for t in range(PACK // 2):
        here = slice(t * 2 * ch, (t + 1) * 2 * ch)
        even = slice(2 * t * 2 * ch, (2 * t + 1) * 2 * ch)
        odd = slice((2 * t + 1) * 2 * ch, (2 * t + 2) * 2 * ch)
        a, b = part[0][0][:, here], part[0][1][:, here]
        qe[:, even] = jnp.where(low, a, 0.0).astype(BF16)
        qe[:, odd] = jnp.where(low, pltpu.roll(a, ch, 1), 0.0).astype(BF16)
        qo[:, even] = jnp.where(low, 0.0, pltpu.roll(b, ch, 1)).astype(BF16)
        qo[:, odd] = jnp.where(low, 0.0, b).astype(BF16)
        for i, ref in ((1, kk), (2, vv)):
            a, b = part[i][0][:, here], part[i][1][:, here]
            ref[:, even] = jnp.where(low, a, pltpu.roll(b, ch, 1)).astype(BF16)
            ref[:, odd] = jnp.where(low, pltpu.roll(a, ch, 1), b).astype(BF16)

    keys = PACK * groups
    lane = lax.broadcasted_iota(jnp.int32, (keys, 2 * ch), 1)
    head_of = lax.rem(lane, ch) // per_head
    ones_row = lax.broadcasted_iota(jnp.int32, (16, keys * heads), 0)
    ones_col = lax.broadcasted_iota(jnp.int32, (16, keys * heads), 1)
    ones = jnp.where(ones_row == ones_col // keys, 1.0, 0.0).astype(BF16)

    def stack(ref, at):
        return jnp.concatenate(
            [ref[at, u * 2 * ch : (u + 1) * 2 * ch] for u in range(PACK)], axis=0
        )

    def score(p, carry):
        at = pl.ds(pl.multiple_of(p * groups, groups), groups)
        queries = jnp.concatenate([stack(qe, at), stack(qo, at)], axis=0)
        key = stack(kk, at)
        zero = jnp.zeros_like(key)
        for h in range(heads):
            part = dot_nt(jnp.where(head_of == h, key, zero), queries)
            top = jnp.max(part, axis=0, keepdims=True)
            soft[p, h * keys : (h + 1) * keys] = jnp.exp2(part - top).astype(BF16)
        return carry

    blank = jnp.zeros((per_head, keys), BF16)

    def mixing(p, carry):
        at = pl.ds(pl.multiple_of(p * groups, groups), groups)
        value_t = stack(vv, at).astype(F32).T.astype(BF16)
        rows = []
        for q in range(2):
            for h in range(heads):
                base = q * ch + h * per_head
                rows.append(
                    jnp.concatenate(
                        [
                            value_t[base : base + per_head] if m == h else blank
                            for m in range(heads)
                        ],
                        axis=1,
                    )
                )
        rows.append(ones)
        summed = dot(jnp.concatenate(rows, axis=0), soft[p])
        inv = 1.0 / summed[2 * ch : 2 * ch + heads]
        blocks = []
        for q in range(2):
            cols = slice(q * keys, (q + 1) * keys)
            for h in range(heads):
                base = q * ch + h * per_head
                blocks.append(
                    summed[base : base + per_head, cols] * inv[h : h + 1, cols]
                )
        mixed = jnp.concatenate(blocks, axis=0).T
        for u in range(PACK):
            mix[at, u * 2 * ch : (u + 1) * 2 * ch] = mixed[
                u * groups : (u + 1) * groups
            ].astype(BF16)
        return carry

    lax.fori_loop(0, pairs, score, 0, unroll=min(pairs, 8))
    lax.fori_loop(0, pairs, mixing, 0, unroll=min(pairs, 8))

    for q in range(2):
        attended = sec[q] + dot(mix[...], w_out[q])
        logits = dot(attended.astype(BF16), w_gate[...]) + gate_off
        sec[q] = sigmoid(logits)

    def scatter(p, carry):
        at = pl.ds(pl.multiple_of(p * groups, groups), groups)
        for q in range(2):
            for b in range(wide // 128):
                sf[b, pl.ds(2 * p + q, groups, stride=pitch), :] = sec[
                    q, at, b * 128 : (b + 1) * 128
                ]
        return carry

    lax.fori_loop(0, pairs, scatter, 0, unroll=True)
    slab = groups // nd
    for a in range(nd):
        g0 = lax.rem(xi + a, nd) * slab
        for g in range(slab):
            row = pl.ds(pl.multiple_of((g0 + g) * pitch, 8), pixels)
            for b in range(wide // 128):
                at = g * wide + b * 128
                outs[a][:, at : at + 128] = sf[b, row, :].astype(BF16)


def disparity(nd, nc, heads, chunks, half, halves, pieces, begun, weights):
    pixels, lanes = pieces[0].shape
    pixels //= halves
    band = weights[0]
    wide = band.shape[2]
    groups = lanes * nd * nc * chunks // wide
    pad = band.shape[1] // 2
    pairs = pixels // 2
    scratch = [
        pltpu.VMEM((groups + 2 * pad, pixels, wide), BF16),
        pltpu.VMEM((groups + 2 * pad, pixels, wide), BF16),
        pltpu.VMEM((wide // 128, groups * (pixels + 8), 128), F32),
        pltpu.VMEM((2, pairs * groups, wide), BF16),
        pltpu.VMEM((pairs * groups, 2 * wide), BF16),
        pltpu.VMEM((pairs * groups, 2 * wide), BF16),
        pltpu.VMEM((pairs * groups, 2 * wide), BF16),
        pltpu.VMEM((pairs * groups, 2 * wide), BF16),
        pltpu.VMEM((pairs * groups, 2 * wide), BF16),
        pltpu.VMEM((2, pairs * groups, wide), F32),
        pltpu.VMEM((pairs, heads * PACK * groups, 2 * PACK * groups), BF16),
    ]
    return pl.pallas_call(
        functools.partial(disparity_kernel, nd, nc, heads, chunks, half),
        out_shape=[jax.ShapeDtypeStruct((pixels, groups * wide // nd), BF16)] * nd,
        in_specs=[vmem()] * (len(pieces) + 8),
        out_specs=[vmem()] * nd,
        scratch_shapes=scratch,
        compiler_params=pltpu.CompilerParams(vmem_limit_bytes=18 << 20),
        cost_estimate=pl.CostEstimate(
            flops=pixels * 340_000_000, bytes_accessed=4 << 20, transcendentals=0
        ),
        name="disparity",
    )(*pieces, begun, *weights)


def gate_kernel(nd, halves, volume, *refs):
    gates, out = refs[: nd * halves], refs[nd * halves]
    rows, cols, _ = volume.shape
    part = rows // nd
    own = part // halves
    for h in range(halves):
        for a in range(nd):
            top = lax.rem(lax.axis_index("disp") - a + nd, nd) * part + h * own
            for r in range(own):
                g = gates[h * nd + a][r * cols : (r + 1) * cols]
                v = volume[top + r].astype(F32) * g.astype(F32)
                out[top + r] = v.astype(BF16)


def gate(nd, halves, volume, gates):
    return pl.pallas_call(
        functools.partial(gate_kernel, nd, halves),
        out_shape=jax.ShapeDtypeStruct(volume.shape, volume.dtype),
        in_specs=[vmem()] * (1 + nd * halves),
        out_specs=vmem(),
        compiler_params=pltpu.CompilerParams(vmem_limit_bytes=3 << 20),
        name="gate",
    )(volume, *gates)


def shift_pairs(sizes, moves):
    out = []
    count = math.prod(sizes)
    for flat in range(count):
        rest, place = flat, []
        for size in reversed(sizes):
            place.append(rest % size)
            rest //= size
        place = place[::-1]
        target = 0
        for at, move, size in zip(place, moves, sizes):
            target = target * size + (at + move) % size
        out.append((flat, target))
    return out


def per_device(
    volume,
    planar_taps,
    planar_bias,
    shift_taps,
    shift_bias,
    norm_gain,
    qkv,
    exit_proj,
    head_scale,
    gate_proj,
    gate_bias,
):
    layers = planar_bias.shape[0]
    heads = head_scale.shape[0]
    nz, nd, nc = [lax.axis_size(a) for a in ("rows", "disp", "cols")]

    if nc > 2:
        raise ValueError("cols: 1 or 2")
    lanes = volume.shape[2]
    chunks = 2 if lanes % (2 * WIDE) == 0 else 1
    sends = []
    for n in range(chunks):
        send_a, send_b, *whole = cut(layers, chunks, n, volume)
        sends += [send_a, send_b]
    mine = whole[0]
    pairs_a = [(z, z + 1) for z in range(0, nz - 1, 2)]
    pairs_b = [(z, z + 1) for z in range(1, nz - 1, 2)]
    both = [ps + [(j, i) for i, j in ps] for ps in (pairs_a, pairs_b)]
    halos = []
    for i, v in enumerate(sends):
        halos.append(lax.ppermute(v, "rows", both[i % 2]))

    rows_w, plane_b = planar_weights(planar_taps, planar_bias)
    made = prepare(
        shift_taps, shift_bias, norm_gain, qkv, exit_proj, head_scale, gate_proj, gate_bias
    )
    band, w_qkv, w_out, w_gate, mean_mat, shift_b, ends = made
    got = []
    for n in range(chunks):
        halo_a, halo_b = halos[2 * n : 2 * n + 2]
        side = edge(n, mine, halo_a, halo_b)
        if nc > 1:
            side = lax.ppermute(side, "cols", [(0, 1), (1, 0)])
        pieces = planar(nd, nc, n, mine, halo_a, halo_b, side, rows_w, plane_b)
        for a, piece in enumerate(pieces):
            if a:
                piece = lax.ppermute(piece, "disp", shift_pairs((nd,), (a,)))
            got.append(piece)
    pixels = got[0].shape[0]
    halves = 2 if pixels % 32 == 0 else 1
    weights = [band, shift_b, ends, w_qkv, w_out, w_gate, mean_mat]
    begun = early(got[::nd], band, shift_b)
    gates = []
    for h in range(halves):
        parts = disparity(nd, 1, heads, chunks, h, halves, got, begun, weights)
        for a, g in enumerate(parts):
            if a:
                g = lax.ppermute(g, "disp", shift_pairs((nd,), (a,)))
            gates.append(g)
    return gate(nd, halves, volume, gates)


def solution(mesh):
    spec = P(("groups", "rows"), "cols", "disp")

    return jax.shard_map(
        per_device, mesh=mesh, in_specs=(spec,) + (P(),) * 10, out_specs=spec, check_vma=False
    )
```

```python
import functools
import math

import jax
import jax.numpy as jnp
from jax import lax
from jax.experimental import pallas as pl
from jax.experimental.pallas import tpu as pltpu
from jax.sharding import PartitionSpec as P


F32 = jnp.float32
BF16 = jnp.bfloat16
SPLIT = 2
PACK = 4
WIDE = 256


def vmem():
    return pl.BlockSpec(memory_space=pltpu.VMEM)


def silu(v):
    half = 0.5 * v
    return half + half * jnp.tanh(half)


def sigmoid(v):
    return 0.5 + 0.5 * jnp.tanh(0.5 * v)


def dot(a, b):
    return jnp.dot(a, b, preferred_element_type=F32)


def dot_nt(a, b):
    return lax.dot_general(a, b, (((1,), (1,)), ((), ())), preferred_element_type=F32)


def prepare_kernel(heads, taps17, qkv, exit_proj, gate_proj, vecs, *rest):
    outs, (t17, wq, we, wg, vec, sems) = rest[:7], rest[7:]
    copies = [
        pltpu.make_async_copy(src, dst, sems.at[i])
        for i, (src, dst) in enumerate(
            [(taps17, t17), (qkv, wq), (exit_proj, we), (gate_proj, wg)]
        )
    ]
    for i, v in enumerate(vecs):
        copies.append(pltpu.make_async_copy(v, vec[i], sems.at[4 + i]))
    for c in copies:
        c.start()
    band, w_qkv, w_out, w_gate, mean_mat, shift_b, ends = outs
    ch = we.shape[0]
    spans = band.shape[1]
    taps = t17.shape[1]
    zero = jnp.zeros((ch, ch), BF16)
    none = jnp.zeros((ch, 2 * ch), BF16)
    for ref in (w_qkv, w_out, w_gate):
        ref[...] = jnp.zeros_like(ref)
    r = lax.broadcasted_iota(jnp.int32, mean_mat.shape, 0) // ch
    c = lax.broadcasted_iota(jnp.int32, mean_mat.shape, 1) // ch
    mean_mat[...] = jnp.where(r == c, 1.0 / ch, 0.0).astype(BF16)
    for c in copies:
        c.wait()

    def pair(x, y):
        return jnp.concatenate([x, y], axis=1)

    def band_block(s, carry):
        table = []
        for t in range(taps + 1):
            table.append(
                pair(t17[s, t] if t < taps else zero, t17[s, t - 1] if t else zero)
            )
        for j in range(spans):
            for u in range(PACK):
                for b in range(PACK // 2):
                    t = PACK * (j - spans // 2) + u - 2 * b + taps // 2
                    block = table[t] if 0 <= t <= taps else none
                    band[s, j, u * ch : (u + 1) * ch, 2 * b * ch : 2 * (b + 1) * ch] = block
        return carry

    lax.fori_loop(0, 2, band_block, 0)
    w = wq[...]
    parts = [w[:, i * ch : (i + 1) * ch] for i in range(3)]
    lo = [pair(p, zero) for p in parts]
    hi = [pair(zero, p) for p in parts]
    out_lo, out_hi = pair(we[...], zero), pair(zero, we[...])
    gate_lo, gate_hi = pair(wg[...], zero), pair(zero, wg[...])
    for u in range(PACK):
        rows = slice(u * ch, (u + 1) * ch)
        tile = slice((u // 2) * 2 * ch, (u // 2 + 1) * 2 * ch)
        for i in range(3):
            w_qkv[i, rows, tile] = hi[i] if u % 2 else lo[i]
        for q in range(2):
            at = u * 2 * ch + q * ch
            w_out[q, at : at + ch, tile] = out_hi if u % 2 else out_lo
        w_gate[rows, tile] = gate_hi if u % 2 else gate_lo

    def tiled(v):
        return jnp.concatenate([v] * PACK, axis=1)

    shift_b[...] = tiled(vec[0][...])
    ends[0:1] = tiled(vec[1][...])
    ends[1:2] = tiled(vec[2][...])
    head = lax.rem(lax.broadcasted_iota(jnp.int32, (1, PACK * ch), 1), ch) // (ch // heads)
    row = jnp.zeros((1, PACK * ch), F32)
    for h in range(heads):
        row = jnp.where(head == h, vec[3][:, h : h + 1], row)
    ends[2:3] = row * (math.log2(math.e) / math.sqrt(ch // heads))


def prepare(shift_taps, shift_bias, gain, qkv, exit_proj, head_scale, gate_proj, gate_bias):
    ch = gain.shape[0]
    taps = shift_taps.shape[1]
    heads = head_scale.shape[0]
    spans = 2 * (-(-(taps // 2) // PACK)) + 1
    size = PACK * ch
    sds = jax.ShapeDtypeStruct
    outs = [
        sds((2, spans, size, size), BF16),
        sds((3, size, size), BF16),
        sds((2, 2 * size, size), BF16),
        sds((size, size), BF16),
        sds((size, size), BF16),
        sds((2, size), F32),
        sds((3, size), F32),
    ]
    vecs = [shift_bias, gain[None], gate_bias[None], head_scale[None]]
    big = [shift_taps, qkv, exit_proj, gate_proj]

    def body(*refs):
        prepare_kernel(
            heads, *refs[:4], refs[4:8], *refs[8:15], *refs[15:19], refs[19:23], refs[23]
        )

    return from_hbm(body, outs, big + vecs)


def from_hbm(body, outs, args):
    return pl.pallas_call(
        body,
        out_shape=outs,
        in_specs=[pl.BlockSpec(memory_space=pltpu.HBM)] * len(args),
        out_specs=[vmem()] * len(outs),
        scratch_shapes=[pltpu.VMEM(v.shape, v.dtype) for v in args]
        + [pltpu.SemaphoreType.DMA((len(args),))],
        compiler_params=pltpu.CompilerParams(vmem_limit_bytes=10 << 20),
        cost_estimate=pl.CostEstimate(flops=0, bytes_accessed=4 << 20, transcendentals=0),
    )(*[pltpu.with_memory_space_constraint(v, pltpu.HBM) for v in args])


def planar_weights_kernel(taps3, bias, rows_w, plane_b, t3, vec, sems):
    copies = [
        pltpu.make_async_copy(taps3, t3, sems.at[0]),
        pltpu.make_async_copy(bias, vec, sems.at[1]),
    ]
    for c in copies:
        c.start()
    layers, ch = vec.shape
    zero = jnp.zeros((ch, ch), BF16)
    none = jnp.zeros((ch, 2 * ch), BF16)
    for c in copies:
        c.wait()

    def pair(x, y):
        return jnp.concatenate([x, y], axis=1)

    def planar_block(layer, carry):
        for j in range(3):
            tap = [t3[layer * 9 + i * 3 + j] for i in range(3)] + [zero]
            for rr in range(6):
                top = (j * 6 + rr) * ch
                for b in range(2):
                    t = rr - 2 * b
                    block = none
                    if 0 <= t <= 3:
                        block = pair(tap[t], tap[t - 1] if t else zero)
                    rows_w[layer, top : top + ch, b * 2 * ch : (b + 1) * 2 * ch] = block
        return carry

    lax.fori_loop(0, layers, planar_block, 0)

    plane_b[...] = jnp.concatenate([vec[...]] * PACK, axis=1)


def planar_weights(taps, bias):
    layers, ch = bias.shape
    outs = [
        jax.ShapeDtypeStruct((layers, 18 * ch, PACK * ch), BF16),
        jax.ShapeDtypeStruct((layers, PACK * ch), F32),
    ]
    args = [taps.reshape(layers * 9, ch, ch), bias]
    return from_hbm(planar_weights_kernel, outs, args)


def cut_kernel(halo, chunk, volume, *rest):
    outs, sems = rest[:-1], rest[-1]
    rows = volume.shape[0]
    lanes = outs[0].shape[2]
    even = lax.rem(lax.axis_index("rows") + 1, 2)
    copies = []
    for i, far in enumerate((even, 1 - even)):
        at = slice(chunk * lanes, (chunk + 1) * lanes)
        part = volume.at[pl.ds(far * (rows - halo), halo), :, at]
        copies.append(pltpu.make_async_copy(part, outs[i], sems.at[i]))
    if len(outs) > 2:
        copies.append(pltpu.make_async_copy(volume, outs[2], sems.at[2]))
    for c in copies:
        c.start()
    for c in copies:
        c.wait()


def cut(halo, chunks, chunk, volume):
    _, cols, lanes = volume.shape
    outs = [jax.ShapeDtypeStruct((halo, cols, lanes // chunks), BF16)] * 2
    if chunk == chunks - 1:
        outs.append(jax.ShapeDtypeStruct(volume.shape, BF16))
    return pl.pallas_call(
        functools.partial(cut_kernel, halo, chunk),
        out_shape=outs,
        in_specs=[pl.BlockSpec(memory_space=pltpu.HBM)],
        out_specs=[vmem()] * len(outs),
        scratch_shapes=[pltpu.SemaphoreType.DMA((len(outs),))],
        compiler_params=pltpu.CompilerParams(vmem_limit_bytes=3 << 20),
        name="cut",
    )(pltpu.with_memory_space_constraint(volume, pltpu.HBM))


def edge_kernel(chunk, mine, halo_a, halo_b, out):
    rows = mine.shape[0]
    halo, lanes = halo_a.shape[0], halo_a.shape[2]
    width = out.shape[1]
    even = lax.rem(lax.axis_index("rows") + 1, 2)
    first = lax.axis_index("cols") == 0
    at_a = even * (halo + rows)
    at_b = (1 - even) * (halo + rows)
    last = mine.shape[1] - width

    def take(v):
        v = v.astype(F32)
        return jnp.where(first, v[last:], v[:width]).astype(BF16)

    for r in range(rows):
        out[halo + r] = take(mine[r, :, chunk * lanes : (chunk + 1) * lanes])
    for r in range(halo):
        out[at_a + r] = take(halo_a[r])
        out[at_b + r] = take(halo_b[r])


def edge(chunk, mine, halo_a, halo_b):
    halo, cols, lanes = halo_a.shape
    total = mine.shape[0] + 2 * halo
    return pl.pallas_call(
        functools.partial(edge_kernel, chunk),
        out_shape=jax.ShapeDtypeStruct((total, min(8, cols), lanes), BF16),
        in_specs=[vmem()] * 3,
        out_specs=vmem(),
        compiler_params=pltpu.CompilerParams(vmem_limit_bytes=3 << 20),
        name="edge",
    )(mine, halo_a, halo_b)


def planar_kernel(nd, nc, chunk, *refs):
    mine, halo_a, halo_b, side, weights, bias = refs[:6]
    outs = refs[6 : 6 + nd]
    flat, x1, *xs, last, back = refs[6 + nd :]
    rows, own = mine.shape[:2]
    halo, lanes = halo_a.shape[0], halo_a.shape[2]
    layers = bias.shape[0]
    width = side.shape[1]
    tiles = lanes // 128
    pitch = own + 8
    ch = 64
    total = rows + 2 * halo
    xi, zi = [lax.axis_index(n) for n in ("disp", "rows")]
    ci = lax.axis_index("cols") if nc > 1 else 0
    more = layers if nc > 1 else 0
    nz = lax.axis_size("rows")
    even = lax.rem(zi + 1, 2)
    at_a = even * (halo + rows)
    at_b = (1 - even) * (halo + rows)

    def put(r, base, value):
        for t in range(tiles):
            at = t * pitch + base
            flat[r, at : at + value.shape[0], :] = value[:, t * 128 : (t + 1) * 128].astype(F32)

    def put_own(r, carry):
        put(halo + r, 0, mine[r, :, chunk * lanes : (chunk + 1) * lanes])
        return carry

    def put_halo(r, carry):
        put(at_a + r, 0, halo_a[r])
        put(at_b + r, 0, halo_b[r])
        return carry

    def put_side(r, carry):
        put(r, own, side[r])
        return carry

    lax.fori_loop(0, rows, put_own, 0)
    lax.fori_loop(0, halo, put_halo, 0)
    if more:
        lax.fori_loop(0, total, put_side, 0)
    low = lax.broadcasted_iota(jnp.int32, (tiles, 128), 1) < ch
    stages = [x1] + xs
    for x in stages:
        x[0] = jnp.zeros(x.shape[1:], BF16)
        x[x.shape[0] - 1] = jnp.zeros(x.shape[1:], BF16)

    def turn(source, target):
        at = pl.ds(source, tiles, stride=pitch)
        for p in range(total // 2):
            a, b = flat[2 * p, at, :], flat[2 * p + 1, at, :]
            e = jnp.where(low, a, pltpu.roll(b, ch, 1))
            o = jnp.where(low, pltpu.roll(a, ch, 1), b)
            x1[target + 1, :, p * 128 : (p + 1) * 128] = jnp.concatenate([e, o], axis=0).astype(BF16)

    def turn_own(c, carry):
        turn(c, more * ci + c)
        return carry

    lax.fori_loop(0, own, turn_own, 0, unroll=16)
    for c in range(more):
        turn(own + c + (width - more) * ci, own * (1 - ci) + c)
    row_of = lax.broadcasted_iota(jnp.int32, (1, 256), 1) // ch
    for layer in range(layers):
        height = total - 2 * (layer + 1)
        beyond = layers - 1 - layer
        src = stages[layer]
        count = own + max(more - 1 - layer, 0)
        block = -(-count // SPLIT)
        shift = ci if more else 0
        for q in range(0, height // 2, 2):
            single = q + 1 == height // 2
            span = 128 * (2 if single else 3)
            wide = 128 if single else 256
            row = row_of[:, :wide] + 2 * q
            keep = jnp.ones((1, wide), F32)
            keep = jnp.where((row < beyond) & (zi == 0), 0.0, keep)
            keep = jnp.where((row >= height - beyond) & (zi == nz - 1), 0.0, keep)

            for c0 in [min(i, count - block) for i in range(0, count, block)]:
                lhs = jnp.concatenate(
                    [
                        src[pl.ds(c0 + shift + j, block), :, q * 128 : q * 128 + span].reshape(
                            block * 2 * tiles, span
                        )
                        for j in range(3)
                    ],
                    axis=1,
                )
                if single:
                    rhs = jnp.concatenate(
                        [weights[layer, j * 384 : j * 384 + span, :wide] for j in range(3)], axis=0
                    )
                else:
                    rhs = weights[layer]
                y = silu(dot(lhs, rhs) + bias[layer : layer + 1, :wide])
                if layer < layers - 1:
                    y = (y * keep).astype(BF16).reshape(block, 2 * tiles, wide)
                    stages[layer + 1][c0 + 1 : c0 + 1 + block, :, q * 128 : q * 128 + wide] = y
                else:
                    y = y.reshape(block, 2 * tiles, wide)
                    last[c0 : c0 + block, :, q * 128 : q * 128 + wide] = y

    def turn_back(c, carry):
        at = pl.ds(c, tiles, stride=pitch)
        for p in range(rows // 2):
            e = last[c, :tiles, p * 128 : (p + 1) * 128]
            o = last[c, tiles:, p * 128 : (p + 1) * 128]
            back[2 * p, at, :] = jnp.where(low, e, pltpu.roll(o, ch, 1))
            back[2 * p + 1, at, :] = jnp.where(low, pltpu.roll(e, ch, 1), o)
        return carry

    lax.fori_loop(0, own, turn_back, 0, unroll=16)
    part = rows // nd
    for a in range(nd):
        top = lax.rem(xi + a, nd) * part
        for r in range(part):
            for t in range(tiles):
                outs[a][r * own : (r + 1) * own, t * 128 : (t + 1) * 128] = back[
                    top + r, t * pitch : t * pitch + own, :
                ].astype(BF16)


def planar(nd, nc, chunk, mine, halo_a, halo_b, side, weights, bias):
    rows, own = mine.shape[:2]
    halo, lanes = halo_a.shape[0], halo_a.shape[2]
    layers = bias.shape[0]
    tiles = lanes // 128
    total = rows + 2 * halo
    more = layers if nc > 1 else 0
    scratch = [pltpu.VMEM((total, tiles * (own + 8), 128), F32)]
    scratch += [
        pltpu.VMEM((own + max(more - k, 0) + 2, 2 * tiles, (total // 2 - k) * 128), BF16)
        for k in range(layers)
    ]
    scratch += [
        pltpu.VMEM((own, 2 * tiles, rows * 64), F32),
        pltpu.VMEM((rows, tiles * (own + 8), 128), F32),
    ]
    return pl.pallas_call(
        functools.partial(planar_kernel, nd, nc, chunk),
        out_shape=[jax.ShapeDtypeStruct((rows * own // nd, lanes), BF16)] * nd,
        in_specs=[vmem()] * 6,
        out_specs=[vmem()] * nd,
        scratch_shapes=scratch,
        compiler_params=pltpu.CompilerParams(vmem_limit_bytes=18 << 20),
        cost_estimate=pl.CostEstimate(
            flops=36 * lanes * 2 * own * total * 256, bytes_accessed=4 << 20, transcendentals=0
        ),
        name="planar",
    )(mine, halo_a, halo_b, side, weights, bias)


def early_kernel(chunks, *refs):
    pieces, band, bias, out, xs = refs[:chunks], *refs[chunks:]
    pixels, lanes = pieces[0].shape
    wide = band.shape[2]
    spans = band.shape[1]
    per_piece = lanes // wide
    for n in range(chunks):
        for g in range(per_piece):
            xs[n * per_piece + g] = pieces[n][:, g * wide : (g + 1) * wide]
    inner = out.shape[0]
    step = max(d for d in range(1, inner + 1) if inner % d == 0 and d * pixels <= 256)
    for g0 in range(0, inner, step):
        acc = None
        for j in range(spans):
            lhs = xs[g0 + j : g0 + j + step].reshape(step * pixels, wide)
            part = dot(lhs, band[0, j])
            acc = part if acc is None else acc + part
        y = silu(acc + bias[0:1]).astype(BF16)
        out[g0 : g0 + step] = y.reshape(step, pixels, wide)


def early(pieces, band, bias):
    pixels, lanes = pieces[0].shape
    wide = band.shape[2]
    own = lanes * len(pieces) // wide
    inner = own - band.shape[1] + 1
    return pl.pallas_call(
        functools.partial(early_kernel, len(pieces)),
        out_shape=jax.ShapeDtypeStruct((inner, pixels, wide), BF16),
        in_specs=[vmem()] * (len(pieces) + 2),
        out_specs=vmem(),
        scratch_shapes=[pltpu.VMEM((own, pixels, wide), BF16)],
        compiler_params=pltpu.CompilerParams(vmem_limit_bytes=6 << 20),
        cost_estimate=pl.CostEstimate(
            flops=pixels * 40_000_000, bytes_accessed=1 << 20, transcendentals=0
        ),
        name="early",
    )(*pieces, band, bias)


def disparity_kernel(
    nd,
    nc,
    heads,
    chunks,
    half,
    *refs,
):
    count = chunks * nd * nc
    pieces = refs[:count]
    begun, refs = refs[count], refs[:count] + refs[count + 1 :]
    band, bias, ends, w_qkv, w_out, w_gate, mean_mat = refs[count : count + 7]
    outs = refs[count + 7 : count + 7 + nd]
    xs, ys, sf, nrm, qe, qo, kk, vv, mix, sec, soft = refs[count + 7 + nd :]
    gain, gate_off = ends[0:1], ends[1:2]
    q_scale = ends[2:3]
    pixels, lanes = outs[0].shape[0], pieces[0].shape[1]
    wide = band.shape[2]
    per_piece = lanes // wide
    groups = per_piece * count
    spans = band.shape[1]
    pad = spans // 2
    ch = wide // PACK
    per_head = ch // heads
    pairs = pixels // 2
    pitch = pixels + 8
    xi, ci = lax.axis_index("disp"), 0

    for side in range(pad):
        xs[side] = jnp.zeros((pixels, wide), BF16)
        xs[pad + groups + side] = jnp.zeros((pixels, wide), BF16)
        ys[side] = jnp.zeros((pixels, wide), BF16)
        ys[pad + groups + side] = jnp.zeros((pixels, wide), BF16)
    for a in range(nd):
        for k in range(nc):
            src_x = lax.rem(xi - a + nd, nd)
            src_c = lax.rem(ci - k + nc, nc)
            for n in range(chunks):
                at = pad + ((src_x * nc + src_c) * chunks + n) * per_piece
                piece = pieces[(n * nd + a) * nc + k]
                for g in range(per_piece):
                    xs[at + g] = piece[
                        half * pixels : (half + 1) * pixels, g * wide : (g + 1) * wide
                    ]

    step = math.gcd(groups, 256 // pixels)

    def conv(src, s, g0):
        acc = None
        for j in range(spans):
            lhs = src[pl.ds(g0 + j, step)].reshape(step * pixels, wide)
            part = dot(lhs, band[s, j])
            acc = part if acc is None else acc + part
        return acc + bias[s : s + 1]

    inner = begun.shape[0]
    own = groups // nd
    for g in range(inner):
        ys[xi * own + 2 * pad + g] = begun[g, half * pixels : (half + 1) * pixels]
    rest = groups - inner
    part_of = max(d for d in range(1, rest + 1) if rest % d == 0 and d * pixels <= 256)
    for i in range(0, rest, part_of):
        where = [lax.rem(xi * own + own - pad + i + g, groups) for g in range(part_of)]
        acc = None
        for j in range(spans):
            lhs = jnp.concatenate([xs[g + j] for g in where], axis=0)
            part = dot(lhs, band[0, j])
            acc = part if acc is None else acc + part
        y = silu(acc + bias[0:1]).astype(BF16)
        for n, g in enumerate(where):
            ys[pad + g] = y[n * pixels : (n + 1) * pixels]

    def second(i, carry):
        g0 = i * step
        y = conv(ys, 1, g0).astype(BF16).astype(F32)
        for i in range(step):
            at = pl.ds(pl.multiple_of((g0 + i) * pitch, 8), pixels)
            for b in range(wide // 128):
                sf[b, at, :] = y[i * pixels : (i + 1) * pixels, b * 128 : (b + 1) * 128]
        return carry

    lax.fori_loop(0, groups // step, second, 0, unroll=True)

    def gather(p, carry):
        at = pl.ds(pl.multiple_of(p * groups, groups), groups)
        for q in range(2):
            for b in range(wide // 128):
                piece = sf[b, pl.ds(2 * p + q, groups, stride=pitch), :]
                sec[q, at, b * 128 : (b + 1) * 128] = piece
        return carry

    lax.fori_loop(0, pairs, gather, 0, unroll=True)

    for q in range(2):
        s = sec[q]
        hi = (s * s).astype(BF16)
        mean = dot(hi, mean_mat[...])
        nrm[q] = (s * lax.rsqrt(mean + 1e-05) * gain).astype(BF16)
    low = lax.broadcasted_iota(jnp.int32, (pairs * groups, 2 * ch), 1) < ch
    part = [[dot(nrm[q], w_qkv[i]) for q in range(2)] for i in range(3)]
    part[0] = [p * q_scale for p in part[0]]
    for t in range(PACK // 2):
        here = slice(t * 2 * ch, (t + 1) * 2 * ch)
        even = slice(2 * t * 2 * ch, (2 * t + 1) * 2 * ch)
        odd = slice((2 * t + 1) * 2 * ch, (2 * t + 2) * 2 * ch)
        a, b = part[0][0][:, here], part[0][1][:, here]
        qe[:, even] = jnp.where(low, a, 0.0).astype(BF16)
        qe[:, odd] = jnp.where(low, pltpu.roll(a, ch, 1), 0.0).astype(BF16)
        qo[:, even] = jnp.where(low, 0.0, pltpu.roll(b, ch, 1)).astype(BF16)
        qo[:, odd] = jnp.where(low, 0.0, b).astype(BF16)
        for i, ref in ((1, kk), (2, vv)):
            a, b = part[i][0][:, here], part[i][1][:, here]
            ref[:, even] = jnp.where(low, a, pltpu.roll(b, ch, 1)).astype(BF16)
            ref[:, odd] = jnp.where(low, pltpu.roll(a, ch, 1), b).astype(BF16)

    keys = PACK * groups
    lane = lax.broadcasted_iota(jnp.int32, (keys, 2 * ch), 1)
    head_of = lax.rem(lane, ch) // per_head
    ones_row = lax.broadcasted_iota(jnp.int32, (16, keys * heads), 0)
    ones_col = lax.broadcasted_iota(jnp.int32, (16, keys * heads), 1)
    ones = jnp.where(ones_row == ones_col // keys, 1.0, 0.0).astype(BF16)

    def stack(ref, at):
        return jnp.concatenate(
            [ref[at, u * 2 * ch : (u + 1) * 2 * ch] for u in range(PACK)], axis=0
        )

    def score(p, carry):
        at = pl.ds(pl.multiple_of(p * groups, groups), groups)
        queries = jnp.concatenate([stack(qe, at), stack(qo, at)], axis=0)
        key = stack(kk, at)
        zero = jnp.zeros_like(key)
        for h in range(heads):
            part = dot_nt(jnp.where(head_of == h, key, zero), queries)
            top = jnp.max(part, axis=0, keepdims=True)
            soft[p, h * keys : (h + 1) * keys] = jnp.exp2(part - top).astype(BF16)
        return carry

    blank = jnp.zeros((per_head, keys), BF16)

    def mixing(p, carry):
        at = pl.ds(pl.multiple_of(p * groups, groups), groups)
        value_t = stack(vv, at).astype(F32).T.astype(BF16)
        rows = []
        for q in range(2):
            for h in range(heads):
                base = q * ch + h * per_head
                rows.append(
                    jnp.concatenate(
                        [
                            value_t[base : base + per_head] if m == h else blank
                            for m in range(heads)
                        ],
                        axis=1,
                    )
                )
        rows.append(ones)
        summed = dot(jnp.concatenate(rows, axis=0), soft[p])
        inv = 1.0 / summed[2 * ch : 2 * ch + heads]
        blocks = []
        for q in range(2):
            cols = slice(q * keys, (q + 1) * keys)
            for h in range(heads):
                base = q * ch + h * per_head
                blocks.append(
                    summed[base : base + per_head, cols] * inv[h : h + 1, cols]
                )
        mixed = jnp.concatenate(blocks, axis=0).T
        for u in range(PACK):
            mix[at, u * 2 * ch : (u + 1) * 2 * ch] = mixed[
                u * groups : (u + 1) * groups
            ].astype(BF16)
        return carry

    lax.fori_loop(0, pairs, score, 0, unroll=min(pairs, 8))
    lax.fori_loop(0, pairs, mixing, 0, unroll=min(pairs, 8))

    for q in range(2):
        attended = sec[q] + dot(mix[...], w_out[q])
        logits = dot(attended.astype(BF16), w_gate[...]) + gate_off
        sec[q] = sigmoid(logits)

    def scatter(p, carry):
        at = pl.ds(pl.multiple_of(p * groups, groups), groups)
        for q in range(2):
            for b in range(wide // 128):
                sf[b, pl.ds(2 * p + q, groups, stride=pitch), :] = sec[
                    q, at, b * 128 : (b + 1) * 128
                ]
        return carry

    lax.fori_loop(0, pairs, scatter, 0, unroll=True)
    slab = groups // nd
    for a in range(nd):
        g0 = lax.rem(xi + a, nd) * slab
        for g in range(slab):
            row = pl.ds(pl.multiple_of((g0 + g) * pitch, 8), pixels)
            for b in range(wide // 128):
                at = g * wide + b * 128
                outs[a][:, at : at + 128] = sf[b, row, :].astype(BF16)


def disparity(nd, nc, heads, chunks, half, halves, pieces, begun, weights):
    pixels, lanes = pieces[0].shape
    pixels //= halves
    band = weights[0]
    wide = band.shape[2]
    groups = lanes * nd * nc * chunks // wide
    pad = band.shape[1] // 2
    pairs = pixels // 2
    scratch = [
        pltpu.VMEM((groups + 2 * pad, pixels, wide), BF16),
        pltpu.VMEM((groups + 2 * pad, pixels, wide), BF16),
        pltpu.VMEM((wide // 128, groups * (pixels + 8), 128), F32),
        pltpu.VMEM((2, pairs * groups, wide), BF16),
        pltpu.VMEM((pairs * groups, 2 * wide), BF16),
        pltpu.VMEM((pairs * groups, 2 * wide), BF16),
        pltpu.VMEM((pairs * groups, 2 * wide), BF16),
        pltpu.VMEM((pairs * groups, 2 * wide), BF16),
        pltpu.VMEM((pairs * groups, 2 * wide), BF16),
        pltpu.VMEM((2, pairs * groups, wide), F32),
        pltpu.VMEM((pairs, heads * PACK * groups, 2 * PACK * groups), BF16),
    ]
    return pl.pallas_call(
        functools.partial(disparity_kernel, nd, nc, heads, chunks, half),
        out_shape=[jax.ShapeDtypeStruct((pixels, groups * wide // nd), BF16)] * nd,
        in_specs=[vmem()] * (len(pieces) + 8),
        out_specs=[vmem()] * nd,
        scratch_shapes=scratch,
        compiler_params=pltpu.CompilerParams(vmem_limit_bytes=18 << 20),
        cost_estimate=pl.CostEstimate(
            flops=pixels * 340_000_000, bytes_accessed=4 << 20, transcendentals=0
        ),
        name="disparity",
    )(*pieces, begun, *weights)


def gate_kernel(nd, halves, volume, *refs):
    gates, (out, held, sems) = refs[: nd * halves], refs[nd * halves :]
    rows, cols, _ = volume.shape
    part = rows // nd
    own = part // halves
    copies = []
    for h in range(halves):
        for a in range(nd):
            top = lax.rem(lax.axis_index("disp") - a + nd, nd) * part + h * own
            for r in range(own):
                g = gates[h * nd + a][r * cols : (r + 1) * cols]
                v = volume[top + r].astype(F32) * g.astype(F32)
                at = len(copies)
                held[at] = v.astype(BF16)
                copies.append(pltpu.make_async_copy(held.at[at], out.at[top + r], sems.at[at]))
                copies[-1].start()
    for c in copies:
        c.wait()


def gate(nd, halves, volume, gates):
    return pl.pallas_call(
        functools.partial(gate_kernel, nd, halves),
        out_shape=jax.ShapeDtypeStruct(volume.shape, volume.dtype),
        in_specs=[vmem()] * (1 + nd * halves),
        out_specs=pl.BlockSpec(memory_space=pltpu.HBM),
        scratch_shapes=[
            pltpu.VMEM(volume.shape, volume.dtype),
            pltpu.SemaphoreType.DMA((volume.shape[0],)),
        ],
        compiler_params=pltpu.CompilerParams(vmem_limit_bytes=3 << 20),
        name="gate",
    )(volume, *gates)


def shift_pairs(sizes, moves):
    out = []
    count = math.prod(sizes)
    for flat in range(count):
        rest, place = flat, []
        for size in reversed(sizes):
            place.append(rest % size)
            rest //= size
        place = place[::-1]
        target = 0
        for at, move, size in zip(place, moves, sizes):
            target = target * size + (at + move) % size
        out.append((flat, target))
    return out


def per_device(
    volume,
    planar_taps,
    planar_bias,
    shift_taps,
    shift_bias,
    norm_gain,
    qkv,
    exit_proj,
    head_scale,
    gate_proj,
    gate_bias,
):
    layers = planar_bias.shape[0]
    heads = head_scale.shape[0]
    nz, nd, nc = [lax.axis_size(a) for a in ("rows", "disp", "cols")]

    if nc > 2:
        raise ValueError("cols: 1 or 2")
    lanes = volume.shape[2]
    chunks = 2 if lanes % (2 * WIDE) == 0 else 1
    sends = []
    for n in range(chunks):
        send_a, send_b, *whole = cut(layers, chunks, n, volume)
        sends += [send_a, send_b]
    mine = whole[0]
    pairs_a = [(z, z + 1) for z in range(0, nz - 1, 2)]
    pairs_b = [(z, z + 1) for z in range(1, nz - 1, 2)]
    both = [ps + [(j, i) for i, j in ps] for ps in (pairs_a, pairs_b)]
    halos = []
    for i, v in enumerate(sends):
        halos.append(lax.ppermute(v, "rows", both[i % 2]))

    rows_w, plane_b = planar_weights(planar_taps, planar_bias)
    made = prepare(
        shift_taps, shift_bias, norm_gain, qkv, exit_proj, head_scale, gate_proj, gate_bias
    )
    band, w_qkv, w_out, w_gate, mean_mat, shift_b, ends = made
    got = []
    for n in range(chunks):
        halo_a, halo_b = halos[2 * n : 2 * n + 2]
        side = edge(n, mine, halo_a, halo_b)
        if nc > 1:
            side = lax.ppermute(side, "cols", [(0, 1), (1, 0)])
        pieces = planar(nd, nc, n, mine, halo_a, halo_b, side, rows_w, plane_b)
        for a, piece in enumerate(pieces):
            if a:
                piece = lax.ppermute(piece, "disp", shift_pairs((nd,), (a,)))
            got.append(piece)
    pixels = got[0].shape[0]
    halves = 2 if pixels % 32 == 0 else 1
    weights = [band, shift_b, ends, w_qkv, w_out, w_gate, mean_mat]
    begun = early(got[::nd], band, shift_b)
    gates = []
    for h in range(halves):
        parts = disparity(nd, 1, heads, chunks, h, halves, got, begun, weights)
        for a, g in enumerate(parts):
            if a:
                g = lax.ppermute(g, "disp", shift_pairs((nd,), (a,)))
            gates.append(g)
    return gate(nd, halves, volume, gates)


def solution(mesh):
    spec = P(("groups", "rows"), "cols", "disp")

    return jax.shard_map(
        per_device, mesh=mesh, in_specs=(spec,) + (P(),) * 10, out_specs=spec, check_vma=False
    )
```
